32 devices in a mesh: dp: 16 (over z, y, core), tensor: 2 (over x).
Axes of the slice: x: 2, y: 2, z: 4, core: 2. Of those that a mesh axis runs over, the one named last changes fastest.
Arguments:
- layer_input: bfloat16 [65536, 512], P(('dp', 'tensor')), may hold values from -6 to 6
- output_grad: bfloat16 [65536, 512], P(('dp', 'tensor')), may hold values from -6 to 6
- qkv_weight: bfloat16 [1536, 512], P('tensor'), may hold values from -0.375 to 0.375
- query_bias: bfloat16 [512], P('tensor'), may hold values from -3 to 3
- value_bias: bfloat16 [512], P('tensor'), may hold values from -3 to 3
- proj_weight: bfloat16 [512, 512], P('tensor'), may hold values from -0.875 to 0.875
- proj_bias: bfloat16 [512], replicated, may hold values from -2 to 2
- first_gain: bfloat16 [512], replicated, may hold values from 0.5 to 1.5
- first_shift: bfloat16 [512], replicated, may hold values from -2 to 2
- up_weight: bfloat16 [512, 2048], P(None, 'tensor'), may hold values from -0.25 to 0.25
- up_bias: bfloat16 [2048], P('tensor'), may hold values from -3 to 3
- down_weight: bfloat16 [2048, 512], P('tensor'), may hold values from -0.125 to 0.125
- down_bias: bfloat16 [512], replicated, may hold values from -2 to 2
- second_gain: bfloat16 [512], replicated, may hold values from 0.5 to 1.5
- second_shift: bfloat16 [512], replicated, may hold values from -2 to 2
Outputs:
- layer_output: bfloat16 [65536, 512], P(('dp', 'tensor'))
- input_grad: bfloat16 [65536, 512], P(('dp', 'tensor'))
- qkv_weight_grad: float32 [1536, 512], P('tensor')
- query_bias_grad: float32 [512], P('tensor')
- value_bias_grad: float32 [512], P('tensor')
- proj_weight_grad: float32 [512, 512], P('tensor')
- proj_bias_grad: float32 [512], replicated
- first_gain_grad: float32 [512], replicated
- first_shift_grad: float32 [512], replicated
- up_weight_grad: float32 [512, 2048], P(None, 'tensor')
- up_bias_grad: float32 [2048], P('tensor')
- down_weight_grad: float32 [2048, 512], P('tensor')
- down_bias_grad: float32 [512], replicated
- second_gain_grad: float32 [512], replicated
- second_shift_grad: float32 [512], replicated
The draws below stay inside these ranges and needn't reach their ends.
All inputs are finite; a program needn't handle non-finite values.
Results may differ from the reference program's by a relative error of at most 0.022.
The reference program's roundings to bfloat16 on the way count: a program that leaves them out, or rounds other values in their place, can miss the bound.
Values may be sent and summed in bfloat16 or wider, within the bound.
No kernel may reach another device: no remote copies, remote signals or barrier semaphores. Data moves between devices by JAX's collectives and lax.ppermute only.
A program may use at most 256 MiB of HBM per device.

```python
import math
import jax
import jax.numpy as jnp
from jax import lax

D = 512
HEADS = 8
HEAD_DIM = 64
FF = 2048
SEQ_LEN = 1024
SEQ_DEV = 4
TOKENS = 65536
N_DP = 16


def block_levels(rng, shape, cuts, least, top_value):
    factor_of, own = 1.0, jax.random.fold_in(rng, 6)
    for axis_at, shards_of in cuts:
        steps = jnp.exp(jax.random.uniform(jax.random.fold_in(own, axis_at), (shards_of,), jnp.float32, least / len(cuts), top_value / len(cuts)))
        factor_of = factor_of * jnp.repeat(steps, shape[axis_at] // shards_of).reshape([-1 if axis == axis_at else 1 for axis in range(len(shape))])
    return factor_of


def centred(rng, dims, width, most, cuts=(), dtype=jnp.bfloat16):
    array = width * jax.random.normal(rng, dims, jnp.float32)
    if cuts:
        array = array * block_levels(rng, dims, cuts, -0.22, 0.18)
    return jnp.clip(array, -most, most).astype(dtype)


def setup_inputs(seed: int = 0) -> dict:
    arg_keys = jax.random.split(jax.random.key(seed), 16)
    layer_input = centred(arg_keys[0], (TOKENS, D), 1.0, 6.0, ((0, 32),))
    output_grad = centred(arg_keys[1], (TOKENS, D), 1.0, 6.0, ((0, 32),))
    qkv_weight = centred(arg_keys[2], (3 * HEADS * HEAD_DIM, D), (D // 2) ** -0.5, 0.375, ((0, 2),))
    query_bias = centred(arg_keys[3], (HEADS * HEAD_DIM,), 0.5, 3.0, ((0, 2),))
    value_bias = centred(arg_keys[4], (HEADS * HEAD_DIM,), 0.5, 3.0, ((0, 2),))
    proj_weight = centred(arg_keys[5], (HEADS * HEAD_DIM, D), (HEADS * HEAD_DIM // 10) ** -0.5, 0.875, ((0, 2),))
    proj_bias = centred(arg_keys[6], (D,), 0.3, 2.0)
    first_gain = jnp.clip(1.0 + 0.1 * jax.random.normal(arg_keys[7], (D,), jnp.float32), 0.5, 1.5).astype(jnp.bfloat16)
    first_shift = centred(arg_keys[8], (D,), 0.3, 2.0)
    up_weight = centred(arg_keys[9], (D, FF), D ** -0.5, 0.25, ((1, 2),))
    up_bias = centred(arg_keys[10], (FF,), 0.5, 3.0, ((0, 2),))
    down_weight = centred(arg_keys[11], (FF, D), FF ** -0.5, 0.125, ((0, 2),))
    down_bias = centred(arg_keys[12], (D,), 0.3, 2.0)
    second_gain = jnp.clip(1.0 + 0.1 * jax.random.normal(arg_keys[13], (D,), jnp.float32), 0.5, 1.5).astype(jnp.bfloat16)
    second_shift = centred(arg_keys[14], (D,), 0.3, 2.0)
    return {"layer_input": layer_input, "output_grad": output_grad, "qkv_weight": qkv_weight, "query_bias": query_bias, "value_bias": value_bias, "proj_weight": proj_weight, "proj_bias": proj_bias, "first_gain": first_gain, "first_shift": first_shift, "up_weight": up_weight, "up_bias": up_bias, "down_weight": down_weight, "down_bias": down_bias, "second_gain": second_gain, "second_shift": second_shift}


highest = lax.Precision.HIGHEST
norm_eps = 1e-05

@jax.custom_vjp
def low(v):
    return lax.optimization_barrier(v.astype(jnp.bfloat16)).astype(jnp.float32)

@jax.custom_vjp
def low_back(v):
    return v

def low_keep(v):
    return (low(v), None)

def low_pass(kept, grad):
    return (grad,)

def back_keep(v):
    return (v, None)

def back_low(kept, grad):
    return (low(grad),)
low.defvjp(low_keep, low_pass)
low_back.defvjp(back_keep, back_low)

def layer_norm(hidden, gain_vec, shift_vec):
    center = lax.optimization_barrier(jnp.mean(hidden, axis=-1, keepdims=True))
    second = lax.optimization_barrier(jnp.mean(hidden * hidden, axis=-1, keepdims=True)) - center * center
    return (hidden - center) * lax.rsqrt(second + norm_eps) * gain_vec + shift_vec

def attend(sequence):
    queries = sequence[:, :, 0]
    key_rows = sequence[:, :, 1]
    value_rows = sequence[:, :, 2]
    score_scale = HEAD_DIM ** (-0.5)
    scores = low_back(jnp.einsum('qhd,khd->hqk', queries, key_rows, precision=highest) * score_scale)
    row_top = lax.optimization_barrier(jnp.max(scores, axis=-1, keepdims=True))
    exponent = jnp.exp(scores - row_top)
    probs_all = exponent / lax.optimization_barrier(jnp.sum(exponent, axis=-1, keepdims=True))
    return jnp.einsum('hqk,khd->qhd', low(probs_all), value_rows, precision=highest)

def layer_forward(row_block, qkv_weight, query_bias, value_bias, proj_weight, proj_bias, first_gain, first_shift, up_weight, up_bias, down_weight, down_bias, second_gain, second_shift):
    row_count = row_block.shape[0]
    seq_count = row_count // SEQ_LEN
    projected = jnp.dot(row_block, qkv_weight.T, precision=highest).reshape(row_count, HEADS, 3, HEAD_DIM)
    bias_rows = jnp.stack([query_bias.reshape(HEADS, HEAD_DIM), jnp.zeros((HEADS, HEAD_DIM), jnp.float32), value_bias.reshape(HEADS, HEAD_DIM)], axis=1)
    packed = low(low_back(projected + bias_rows))
    sequences = packed.reshape(seq_count, SEQ_LEN, HEADS, 3, HEAD_DIM)
    context = lax.map(jax.checkpoint(attend), sequences)
    context = low(low_back(context.reshape(row_count, HEADS * HEAD_DIM)))
    branch = low_back(jnp.dot(context, proj_weight, precision=highest) + proj_bias)
    normed_one = layer_norm(row_block + branch, first_gain, first_shift)
    inner_pre = low_back(jnp.dot(low(normed_one), up_weight, precision=highest) + up_bias)
    active = low(jax.nn.gelu(inner_pre, approximate=False))
    second = low_back(jnp.dot(active, down_weight, precision=highest) + down_bias)
    return layer_norm(normed_one + second, second_gain, second_shift)

def reference(layer_input, output_grad, qkv_weight, query_bias, value_bias, proj_weight, proj_bias, first_gain, first_shift, up_weight, up_bias, down_weight, down_bias, second_gain, second_shift):
    params = tuple((element.astype(jnp.float32) for element in (qkv_weight, query_bias, value_bias, proj_weight, proj_bias, first_gain, first_shift, up_weight, up_bias, down_weight, down_bias, second_gain, second_shift)))
    seq_total = SEQ_DEV * N_DP
    group_seqs = math.gcd(seq_total, max(1, 4096 // SEQ_LEN))
    group_count = seq_total // group_seqs
    group_rows = group_seqs * SEQ_LEN
    inputs_all = layer_input.astype(jnp.float32).reshape(group_count, group_rows, D)
    cotangent_all = output_grad.astype(jnp.float32).reshape(group_count, group_rows, D)

    def one_group(totals, group_item):
        rows_here, cot_here = group_item
        result_rows, pullback = jax.vjp(layer_forward, rows_here, *params)
        gradients = pullback(cot_here)
        new_totals = tuple((total_old + grad_new for total_old, grad_new in zip(totals, gradients[1:])))
        return (new_totals, (result_rows.astype(jnp.bfloat16), gradients[0].astype(jnp.bfloat16)))
    start = tuple((jnp.zeros(element.shape, jnp.float32) for element in params))
    totals, (outputs, input_grads) = lax.scan(one_group, start, (inputs_all, cotangent_all))
    return (outputs.reshape(TOKENS, D), input_grads.reshape(TOKENS, D), totals[0], totals[1], totals[2], totals[3], totals[4], totals[5], totals[6], totals[7], totals[8], totals[9], totals[10], totals[11], totals[12])
```

```python
from functools import partial

import jax
import jax.numpy as jnp
from jax import lax
from jax.experimental import pallas as pl
from jax.experimental.pallas import tpu as pltpu
from jax.sharding import PartitionSpec as P

HEAD_DIM = 64
SEQ_LEN = 1024
PART_ROWS = 3 * HEAD_DIM

norm_eps = 1e-05
f32 = jnp.float32
bf16 = jnp.bfloat16


def matmul_rows(left, right):
    return lax.dot_general(
        left, right, (((0,), (0,)), ((), ())), preferred_element_type=jnp.float32
    )


def matmul_back(left, right):
    return lax.dot_general(
        left, right, (((1,), (1,)), ((), ())), preferred_element_type=jnp.float32
    )


def attend_forward(queries, key_rows, value_rows):
    seq_heads = key_rows.shape[0] * key_rows.shape[1]
    head_dim = queries.shape[-1]
    score_scale = head_dim ** (-0.5)
    block_rows = min(512, SEQ_LEN)
    block_count = SEQ_LEN // block_rows
    item_count = seq_heads * block_count
    query_items = queries.reshape(item_count, block_rows, head_dim)
    key_all = key_rows.reshape(seq_heads, SEQ_LEN, head_dim)
    value_all = value_rows.reshape(seq_heads, SEQ_LEN, head_dim)

    def one_block(block_item):
        query_blk, position = block_item
        owner_index = position // block_count
        keys_here = key_all[owner_index]
        values_here = value_all[owner_index]
        scores = matmul_back(query_blk, keys_here) * score_scale
        row_top = jnp.max(scores, axis=-1, keepdims=True)
        exponent = jnp.exp(scores - row_top)
        row_total = jnp.sum(exponent, axis=-1, keepdims=True)
        weights_now = exponent / row_total
        mixed_rows = jnp.dot(
            weights_now.astype(jnp.bfloat16), values_here, preferred_element_type=jnp.float32
        )
        return (mixed_rows, row_top[:, 0] + jnp.log(row_total[:, 0]))

    mixed_rows, log_total = lax.map(
        one_block, (query_items, jnp.arange(item_count, dtype=jnp.int32))
    )
    return (mixed_rows.reshape(queries.shape), log_total.reshape(queries.shape[:-1]))


def attend_backward(queries, key_rows, value_rows, log_total, context_low):
    seq_heads = key_rows.shape[0] * key_rows.shape[1]
    head_dim = queries.shape[-1]
    score_scale = head_dim ** (-0.5)
    block_rows = min(512, SEQ_LEN)
    block_count = SEQ_LEN // block_rows
    item_count = seq_heads * block_count
    query_items = queries.reshape(item_count, block_rows, head_dim)
    total_items = log_total.reshape(item_count, block_rows)
    grad_items = context_low.reshape(item_count, block_rows, head_dim)
    key_all = key_rows.reshape(seq_heads, SEQ_LEN, head_dim)
    value_all = value_rows.reshape(seq_heads, SEQ_LEN, head_dim)

    def one_block(block_item):
        query_blk, total_blk, grad_blk, position = block_item
        owner_index = position // block_count
        keys_here = key_all[owner_index]
        values_here = value_all[owner_index]
        scores = matmul_back(query_blk, keys_here) * score_scale
        weights_now = jnp.exp(scores - total_blk[:, None])
        grad_weights = matmul_back(grad_blk, values_here)
        grad_scores = weights_now * (
            grad_weights - jnp.sum(weights_now * grad_weights, axis=-1, keepdims=True)
        )
        score_low = grad_scores.astype(jnp.bfloat16)
        grad_query = jnp.dot(score_low, keys_here, preferred_element_type=jnp.float32) * score_scale
        grad_key = matmul_rows(score_low, query_blk) * score_scale
        grad_value = matmul_rows(weights_now.astype(jnp.bfloat16), grad_blk)
        return (grad_query, grad_key, grad_value)

    grad_query, grad_key, grad_value = lax.map(
        one_block, (query_items, total_items, grad_items, jnp.arange(item_count, dtype=jnp.int32))
    )
    grad_key = jnp.sum(grad_key.reshape(seq_heads, block_count, SEQ_LEN, head_dim), axis=1)
    grad_value = jnp.sum(grad_value.reshape(seq_heads, block_count, SEQ_LEN, head_dim), axis=1)
    return (
        grad_query.reshape(queries.shape),
        grad_key.reshape(key_rows.shape),
        grad_value.reshape(value_rows.shape),
    )


def norm_forward(hidden, gain_vec, shift_vec):
    center = jnp.mean(hidden, axis=-1)
    second = jnp.mean(hidden * hidden, axis=-1) - center * center
    inv_std = lax.rsqrt(second + norm_eps)
    normal = (hidden - center[:, None]) * inv_std[:, None]
    return (normal * gain_vec + shift_vec, normal, inv_std)


def norm_backward(upstream, normal, inv_std, gain_vec):
    scaled = upstream * gain_vec
    first_mean = jnp.mean(scaled, axis=-1)
    second_mean = jnp.mean(scaled * normal, axis=-1)
    grad_in = inv_std[:, None] * (scaled - first_mean[:, None] - normal * second_mean[:, None])
    return (grad_in, jnp.sum(upstream * normal, axis=0), jnp.sum(upstream, axis=0))


def rows_in(value):
    return lax.all_gather(value, "tensor", axis=0, tiled=True)


def part_out(value):
    return lax.psum_scatter(value, "tensor", scatter_dimension=0, tiled=True)


def gather_grad(value):
    return lax.all_gather(value, "tensor", axis=0, tiled=True)


def part_back(value):
    return lax.psum_scatter(value, "tensor", scatter_dimension=0, tiled=True)


def token_body(
    layer_input,
    output_grad,
    qkv_weight,
    query_bias,
    value_bias,
    proj_weight,
    proj_bias,
    first_gain,
    first_shift,
    up_weight,
    up_bias,
    down_weight,
    down_bias,
    second_gain,
    second_shift,
):
    heads_here = query_bias.shape[0] // HEAD_DIM
    query_bf = query_bias.astype(jnp.float32).reshape(heads_here, HEAD_DIM)
    value_bf = value_bias.astype(jnp.float32).reshape(heads_here, HEAD_DIM)
    bias_rows = jnp.stack([query_bf, jnp.zeros_like(query_bf), value_bf], axis=1)
    gain_one = first_gain.astype(jnp.float32)
    shift_one = first_shift.astype(jnp.float32)
    gain_two = second_gain.astype(jnp.float32)
    shift_two = second_shift.astype(jnp.float32)
    input_full = rows_in(layer_input)
    row_count = input_full.shape[0]
    seq_count = row_count // SEQ_LEN
    projected = matmul_back(input_full, qkv_weight).reshape(row_count, heads_here, 3, HEAD_DIM)
    packed = (projected + bias_rows).astype(jnp.bfloat16)
    parts = packed.reshape(seq_count, SEQ_LEN, heads_here, 3, HEAD_DIM).transpose(3, 0, 2, 1, 4)
    queries, key_rows, value_rows = (parts[0], parts[1], parts[2])
    mixed_rows, log_total = attend_forward(queries, key_rows, value_rows)
    context = (
        mixed_rows.transpose(0, 2, 1, 3)
        .reshape(row_count, heads_here * HEAD_DIM)
        .astype(jnp.bfloat16)
    )
    partial_branch = jnp.dot(context, proj_weight, preferred_element_type=jnp.float32)
    branch = part_out(partial_branch) + proj_bias.astype(jnp.float32)
    normed_one, normal_one, inv_one = norm_forward(
        layer_input.astype(jnp.float32) + branch, gain_one, shift_one
    )
    normed_full = rows_in(normed_one.astype(jnp.bfloat16))
    inner_pre = jnp.dot(
        normed_full, up_weight, preferred_element_type=jnp.float32
    ) + up_bias.astype(jnp.float32)
    active, gelu_back = jax.vjp(partial(jax.nn.gelu, approximate=False), inner_pre)
    active_low = active.astype(jnp.bfloat16)
    second = part_out(
        jnp.dot(active_low, down_weight, preferred_element_type=jnp.float32)
    ) + down_bias.astype(jnp.float32)
    result_rows, normal_two, inv_two = norm_forward(normed_one + second, gain_two, shift_two)
    upstream = output_grad.astype(jnp.float32)
    grad_two, gain_two_grad, shift_two_grad = norm_backward(upstream, normal_two, inv_two, gain_two)
    second_low = grad_two.astype(jnp.bfloat16)
    down_b_grad = jnp.sum(second_low.astype(jnp.float32), axis=0)
    second_full = gather_grad(second_low)
    down_w_grad = matmul_rows(active_low, second_full)
    grad_active = matmul_back(second_full, down_weight)
    inner_low = gelu_back(grad_active)[0].astype(jnp.bfloat16)
    up_b_grad = jnp.sum(inner_low.astype(jnp.float32), axis=0)
    up_w_grad = matmul_rows(normed_full, inner_low)
    grad_mid = grad_two + part_back(matmul_back(inner_low, up_weight))
    grad_one, gain_one_grad, shift_one_grad = norm_backward(grad_mid, normal_one, inv_one, gain_one)
    branch_low = grad_one.astype(jnp.bfloat16)
    proj_b_grad = jnp.sum(branch_low.astype(jnp.float32), axis=0)
    branch_full = gather_grad(branch_low)
    proj_w_grad = matmul_rows(context, branch_full)
    context_low = matmul_back(branch_full, proj_weight).astype(jnp.bfloat16)
    context_low = context_low.reshape(seq_count, SEQ_LEN, heads_here, HEAD_DIM).transpose(
        0, 2, 1, 3
    )
    grad_query, grad_key, grad_value = attend_backward(
        queries, key_rows, value_rows, log_total, context_low
    )
    packed_low = jnp.stack([grad_query, grad_key, grad_value], axis=0).transpose(1, 3, 2, 0, 4)
    packed_low = packed_low.reshape(row_count, heads_here * 3 * HEAD_DIM).astype(jnp.bfloat16)
    packed_sums = jnp.sum(packed_low.astype(jnp.float32), axis=0).reshape(heads_here, 3, HEAD_DIM)
    query_b_grad = packed_sums[:, 0].reshape(heads_here * HEAD_DIM)
    value_b_grad = packed_sums[:, 2].reshape(heads_here * HEAD_DIM)
    qkv_w_grad = matmul_rows(packed_low, input_full)
    input_grad = (
        grad_one + part_back(jnp.dot(packed_low, qkv_weight, preferred_element_type=jnp.float32))
    ).astype(jnp.bfloat16)
    totals = (
        lax.psum(qkv_w_grad.astype(jnp.bfloat16), "dp").astype(jnp.float32),
        lax.psum(query_b_grad.astype(jnp.bfloat16), "dp").astype(jnp.float32),
        lax.psum(value_b_grad.astype(jnp.bfloat16), "dp").astype(jnp.float32),
        lax.psum(proj_w_grad.astype(jnp.bfloat16), "dp").astype(jnp.float32),
        lax.psum(up_w_grad.astype(jnp.bfloat16), "dp").astype(jnp.float32),
        lax.psum(up_b_grad.astype(jnp.bfloat16), "dp").astype(jnp.float32),
        lax.psum(down_w_grad.astype(jnp.bfloat16), "dp").astype(jnp.float32),
    )
    vectors = lax.psum(
        (proj_b_grad, gain_one_grad, shift_one_grad, down_b_grad, gain_two_grad, shift_two_grad),
        ("dp", "tensor"),
    )
    return (
        result_rows.astype(jnp.bfloat16),
        input_grad,
        totals[0],
        totals[1],
        totals[2],
        totals[3],
        vectors[0],
        vectors[1],
        vectors[2],
        totals[4],
        totals[5],
        totals[6],
        vectors[3],
        vectors[4],
        vectors[5],
    )


def mm(left, right):
    return lax.dot_general(left, right, (((1,), (0,)), ((), ())), preferred_element_type=f32)


def mm_nt(left, right):
    return lax.dot_general(left, right, (((1,), (1,)), ((), ())), preferred_element_type=f32)


def mm_tn(left, right):
    return lax.dot_general(left, right, (((0,), (0,)), ((), ())), preferred_element_type=f32)


def piece_plan(n_dp):
    rest = n_dp // 4
    return [core | (mid << 1) | (far << 2) for core in range(2) for mid in range(2) for far in range(rest)]


def attn_fwd_kernel(x_ref, w_ref, b_ref, *refs, heads, q_block):
    packed_ref, probs_ref, ctx_ref, key_ref, score_a, score_b = refs[-6:]
    seq = x_ref.shape[0]
    scale = HEAD_DIM**-0.5
    packed_ref[0, 0] = (mm_nt(w_ref[...], x_ref[...]) + b_ref[...]).astype(bf16)
    for h in range(heads):
        base = h * PART_ROWS
        keys = packed_ref[0, 0, base + HEAD_DIM : base + 2 * HEAD_DIM, :].astype(f32)
        key_ref[h] = (keys.T * scale).astype(bf16)
    tiles = [(h, c) for h in range(heads) for c in range(0, seq, q_block)]
    scores = (score_a, score_b)

    def score(tile, ref):
        h, c = tile
        base = h * PART_ROWS
        ref[...] = mm(key_ref[h], packed_ref[0, 0, base : base + HEAD_DIM, c : c + q_block])

    def finish(tile, ref):
        h, c = tile
        base = h * PART_ROWS
        top = jnp.max(ref[...], axis=0, keepdims=True)
        exponent = jnp.exp(ref[...] - top)
        total = jnp.sum(exponent, axis=0, keepdims=True)
        probs = (exponent * (1.0 / total)).astype(bf16)
        probs_ref[0, 0, h, :, c : c + q_block] = probs
        mixed = mm(packed_ref[0, 0, base + 2 * HEAD_DIM : base + 3 * HEAD_DIM, :], probs)
        ctx_ref[0, 0, h * HEAD_DIM : (h + 1) * HEAD_DIM, c : c + q_block] = mixed.astype(bf16)

    score(tiles[0], scores[0])
    for j, tile in enumerate(tiles):
        if j + 1 < len(tiles):
            score(tiles[j + 1], scores[(j + 1) % 2])
        finish(tile, scores[j % 2])


def attn_fwd(x, weight, bias, shard, n_shards, earlier):
    rows, width = x.shape
    n_seq = rows // SEQ_LEN
    n_heads = weight.shape[0] // PART_ROWS
    heads = 2 if n_heads % 2 == 0 else 1
    q_block = 512
    shapes = [
        jax.ShapeDtypeStruct((n_shards, n_seq, n_heads * PART_ROWS, SEQ_LEN), bf16),
        jax.ShapeDtypeStruct((n_shards, n_seq, n_heads, SEQ_LEN, SEQ_LEN), bf16),
        jax.ShapeDtypeStruct((n_shards, n_seq, n_heads * HEAD_DIM, SEQ_LEN), bf16),
    ]
    out_specs = [
        pl.BlockSpec((1, 1, heads * PART_ROWS, SEQ_LEN), lambda s, h: (shard, s, h, 0)),
        pl.BlockSpec((1, 1, heads, SEQ_LEN, SEQ_LEN), lambda s, h: (shard, s, h, 0, 0)),
        pl.BlockSpec((1, 1, heads * HEAD_DIM, SEQ_LEN), lambda s, h: (shard, s, h, 0)),
    ]
    in_specs = [
        pl.BlockSpec((SEQ_LEN, width), lambda s, h: (s, 0)),
        pl.BlockSpec((heads * PART_ROWS, width), lambda s, h: (h, 0)),
        pl.BlockSpec((heads * PART_ROWS, 1), lambda s, h: (h, 0)),
    ]
    aliases = {}
    if earlier:
        in_specs += [pl.BlockSpec(memory_space=pl.ANY)] * 3
        aliases = {3: 0, 4: 1, 5: 2}
    flops = 2 * rows * width * weight.shape[0] + 4 * n_seq * n_heads * SEQ_LEN * SEQ_LEN * HEAD_DIM
    return pl.pallas_call(
        partial(attn_fwd_kernel, heads=heads, q_block=q_block),
        grid=(n_seq, n_heads // heads),
        in_specs=in_specs,
        out_specs=out_specs,
        out_shape=shapes,
        input_output_aliases=aliases,
        scratch_shapes=[
            pltpu.VMEM((heads, SEQ_LEN, HEAD_DIM), bf16),
            pltpu.VMEM((SEQ_LEN, q_block), f32),
            pltpu.VMEM((SEQ_LEN, q_block), f32),
        ],
        compiler_params=pltpu.CompilerParams(vmem_limit_bytes=40 << 20),
        cost_estimate=pl.CostEstimate(flops=6 * flops, bytes_accessed=20 << 20, transcendentals=0),
        name="attn_fwd",
    )(x, weight, bias, *earlier)


def middle_kernel(
    pos_ref,
    x_ref,
    og_ref,
    ctx_ref,
    proj_ref,
    proj_b_ref,
    gain_one_ref,
    shift_one_ref,
    up_ref,
    up_b_ref,
    down_ref,
    down_b_ref,
    gain_two_ref,
    shift_two_ref,
    out_ref,
    grad_one_ref,
    ctx_low_ref,
    dn_keep_ref,
    dn_send_ref,
    up_keep_ref,
    up_send_ref,
    vec_ref,
    up_bg_ref,
    act_ref,
    slope_ref,
    proj_acc,
    up_acc,
    dn_acc,
    *,
    n_dp,
    chunk,
):
    step = pl.program_id(0)
    n_shards, ctx_rows, width = proj_ref.shape
    hidden = up_ref.shape[2]
    inv_width = 1.0 / width

    def mean(v):
        return jnp.sum(v, axis=1, keepdims=True) * inv_width

    @pl.when(step == 0)
    def _():
        for ref in (proj_acc, up_acc, dn_acc, vec_ref, up_bg_ref):
            ref[...] = jnp.zeros_like(ref)

    branch = proj_b_ref[...]
    for t in range(n_shards):
        branch = branch + mm_tn(ctx_ref[t, 0], proj_ref[t])
    mid_sum = x_ref[...].astype(f32) + branch
    center = mean(mid_sum)
    inv_one = lax.rsqrt(mean(mid_sum * mid_sum) - center * center + norm_eps)
    normal_one = (mid_sum - center) * inv_one
    normed_one = normal_one * gain_one_ref[...] + shift_one_ref[...]
    normed_low = normed_one.astype(bf16)
    second = down_b_ref[...]
    chunks = [(t, c) for t in range(n_shards) for c in range(0, hidden, chunk)]
    for t, c in chunks:
        at = t * hidden + c
        inner = mm(normed_low, up_ref[t, :, c : c + chunk]) + up_b_ref[:, at : at + chunk]
        phi = 0.5 * lax.erf(inner * 0.7071067811865476) + 0.5
        active = (inner * phi).astype(bf16)
        act_ref[:, at : at + chunk] = active
        slope_ref[:, at : at + chunk] = phi + inner * (0.3989422804014327 * jnp.exp(-0.5 * inner * inner))
        second = second + mm(active, down_ref[t, c : c + chunk, :])
    last_sum = normed_one + second
    center_two = mean(last_sum)
    inv_two = lax.rsqrt(mean(last_sum * last_sum) - center_two * center_two + norm_eps)
    normal_two = (last_sum - center_two) * inv_two
    out_ref[...] = (normal_two * gain_two_ref[...] + shift_two_ref[...]).astype(bf16)
    upstream = og_ref[...].astype(f32)
    scaled = upstream * gain_two_ref[...]
    grad_two = inv_two * (scaled - mean(scaled) - normal_two * mean(scaled * normal_two))
    second_low = grad_two.astype(bf16)
    normed_t = normed_low.T
    back = None
    for t, c in chunks:
        at = t * hidden + c
        grad_active = mm_nt(second_low, down_ref[t, c : c + chunk, :])
        inner_low = (grad_active * slope_ref[:, at : at + chunk]).astype(bf16)
        up_bg_ref[:, at : at + chunk] += jnp.sum(inner_low.astype(f32), axis=0, keepdims=True)
        part = mm_nt(inner_low, up_ref[t, :, c : c + chunk])
        back = part if back is None else back + part
        up_acc[t, :, c : c + chunk] += mm(normed_t, inner_low)
        dn_acc[t, c : c + chunk, :] += mm_tn(act_ref[:, at : at + chunk], second_low)
    grad_mid = grad_two + back
    scaled_one = grad_mid * gain_one_ref[...]
    grad_one = inv_one * (scaled_one - mean(scaled_one) - normal_one * mean(scaled_one * normal_one))
    grad_one_ref[...] = grad_one
    branch_low = grad_one.astype(bf16)
    sums = (
        branch_low.astype(f32),
        grad_mid * normal_one,
        grad_mid,
        second_low.astype(f32),
        upstream * normal_two,
        upstream,
    )
    for k, value in enumerate(sums):
        vec_ref[k : k + 1, :] += jnp.sum(value, axis=0, keepdims=True)
    for t in range(n_shards):
        ctx_low_ref[t, 0] = mm_nt(proj_ref[t], branch_low).astype(bf16)
        proj_acc[t] += mm(ctx_ref[t, 0], branch_low)

    @pl.when(step == pl.num_programs(0) - 1)
    def _():
        pos = pos_ref[0]
        dn_rows, up_rows, proj_rows = hidden // n_dp, width // n_dp, ctx_rows // n_dp
        half = n_dp // 2
        for slot, bits in enumerate(piece_plan(n_dp)):
            at = lax.bitwise_xor(pos, bits)
            dn_ref = dn_keep_ref if slot < half else dn_send_ref
            upk_ref = up_keep_ref if slot < half else up_send_ref
            k = slot % half
            for t in range(n_shards):
                rows = pl.ds(pl.multiple_of(at * dn_rows, dn_rows), dn_rows)
                dn_ref[t, k] = dn_acc[t, rows, :].astype(bf16)
                rows = pl.ds(pl.multiple_of(at * proj_rows, proj_rows), proj_rows)
                upk_ref[t, k, :proj_rows] = proj_acc[t, rows, :].astype(bf16)
                rows = pl.ds(pl.multiple_of(at * up_rows, up_rows), up_rows)
                for j in range(hidden // width):
                    to = proj_rows + j * up_rows
                    upk_ref[t, k, to : to + up_rows] = up_acc[t, rows, j * width : (j + 1) * width].astype(bf16)


def middle(pos, x, out_grad, ctx, proj, vectors, up, up_b, down, n_dp):
    rows, width = x.shape
    n_shards, n_seq, ctx_rows, _ = ctx.shape
    hidden = up.shape[2]
    block = 512
    per_seq = SEQ_LEN // block
    half = n_dp // 2
    dn_rows, up_rows = hidden // n_dp, (ctx_rows + width * (hidden // width)) // n_dp

    def whole(*shape):
        return pl.BlockSpec(shape, lambda i, pos: (0,) * len(shape), pipeline_mode=pl.Buffered(1))

    def kept(*shape):
        return pl.BlockSpec(shape, lambda i, pos: (0,) * len(shape))

    row = pl.BlockSpec((block, width), lambda i, pos: (i, 0))
    cols = pl.BlockSpec((n_shards, 1, ctx_rows, block), lambda i, pos: (0, i // per_seq, 0, i % per_seq))
    proj_b, gain_one, shift_one, down_b, gain_two, shift_two = vectors
    vec = whole(1, width)
    dn_shape, up_shape = (n_shards, half, dn_rows, width), (n_shards, half, up_rows, width)
    return pl.pallas_call(
        partial(middle_kernel, n_dp=n_dp, chunk=min(1024, hidden)),
        grid_spec=pltpu.PrefetchScalarGridSpec(
            num_scalar_prefetch=1,
            grid=(rows // block,),
            in_specs=[
                row,
                row,
                cols,
                whole(*proj.shape),
                vec,
                vec,
                vec,
                whole(*up.shape),
                whole(1, n_shards * hidden),
                whole(*down.shape),
                vec,
                vec,
                vec,
            ],
            out_specs=[
                row,
                row,
                cols,
                kept(*dn_shape),
                kept(*dn_shape),
                kept(*up_shape),
                kept(*up_shape),
                kept(8, width),
                kept(1, n_shards * hidden),
            ],
            scratch_shapes=[
                pltpu.VMEM((block, n_shards * hidden), bf16),
                pltpu.VMEM((block, n_shards * hidden), f32),
                pltpu.VMEM(proj.shape, f32),
                pltpu.VMEM(up.shape, f32),
                pltpu.VMEM(down.shape, f32),
            ],
        ),
        out_shape=[
            jax.ShapeDtypeStruct((rows, width), bf16),
            jax.ShapeDtypeStruct((rows, width), f32),
            jax.ShapeDtypeStruct(ctx.shape, bf16),
            jax.ShapeDtypeStruct(dn_shape, bf16),
            jax.ShapeDtypeStruct(dn_shape, bf16),
            jax.ShapeDtypeStruct(up_shape, bf16),
            jax.ShapeDtypeStruct(up_shape, bf16),
            jax.ShapeDtypeStruct((8, width), f32),
            jax.ShapeDtypeStruct((1, n_shards * hidden), f32),
        ],
        compiler_params=pltpu.CompilerParams(vmem_limit_bytes=62 << 20),
        cost_estimate=pl.CostEstimate(flops=30 << 30, bytes_accessed=30 << 20, transcendentals=0),
        name="middle",
    )(
        pos,
        x,
        out_grad,
        ctx,
        proj,
        proj_b,
        gain_one,
        shift_one,
        up,
        up_b,
        down,
        down_b,
        gain_two,
        shift_two,
    )


def attn_bwd_kernel(
    pos_ref,
    x_ref,
    packed_ref,
    probs_ref,
    ctx_low_ref,
    grad_ref,
    keep_ref,
    send_ref,
    bias_ref,
    value_ref,
    key_acc,
    value_acc,
    weight_acc,
    grad_a,
    grad_b,
    *,
    n_dp,
    q_block,
):
    step = pl.program_id(0)
    seq = x_ref.shape[0]
    n_shards = packed_ref.shape[0]
    scale = HEAD_DIM**-0.5
    for t in range(n_shards):
        value_ref[t] = packed_ref[t, 0, 2 * HEAD_DIM : 3 * HEAD_DIM, :].T
    tiles = [(t, c) for t in range(n_shards) for c in range(0, seq, q_block)]
    slots = (grad_a, grad_b)

    def start(tile, ref):
        t, c = tile
        ref[...] = mm(value_ref[t], ctx_low_ref[t, 0, :, c : c + q_block])

    def finish(tile, ref):
        t, c = tile
        cols = slice(c, c + q_block)
        probs_low = probs_ref[t, 0, 0, :, cols]
        probs = probs_low.astype(f32)
        weighted = probs * ref[...]
        total = jnp.sum(weighted, axis=0, keepdims=True)
        score_low = (weighted - probs * total).astype(bf16)
        grad_query = mm(packed_ref[t, 0, HEAD_DIM : 2 * HEAD_DIM, :], score_low) * scale
        grad_ref[t, 0, :HEAD_DIM, cols] = grad_query.astype(bf16)
        grad_key = mm_nt(packed_ref[t, 0, :HEAD_DIM, cols], score_low)
        grad_value = mm_nt(ctx_low_ref[t, 0, :, cols], probs_low)
        if c > 0:
            grad_key = key_acc[...] + grad_key
            grad_value = value_acc[...] + grad_value
        if c + q_block < seq:
            key_acc[...] = grad_key
            value_acc[...] = grad_value
        else:
            grad_ref[t, 0, HEAD_DIM : 2 * HEAD_DIM, :] = (grad_key * scale).astype(bf16)
            grad_ref[t, 0, 2 * HEAD_DIM :, :] = grad_value.astype(bf16)

    start(tiles[0], slots[0])
    for j, tile in enumerate(tiles):
        if j + 1 < len(tiles):
            start(tiles[j + 1], slots[(j + 1) % 2])
        finish(tile, slots[j % 2])

    @pl.when(step == 0)
    def _():
        weight_acc[...] = jnp.zeros_like(weight_acc)
        bias_ref[...] = jnp.zeros_like(bias_ref)

    ones = jnp.ones((8, seq), bf16)
    for t in range(n_shards):
        weight_acc[t] += mm(grad_ref[t, 0], x_ref[...])
        bias_ref[t] += mm_nt(ones, grad_ref[t, 0])

    @pl.when(step == pl.num_programs(0) - 1)
    def _():
        pos = pos_ref[0]
        half = n_dp // 2
        rows, lanes = keep_ref.shape[2:]
        for slot, bits in enumerate(piece_plan(n_dp)):
            at = lax.bitwise_xor(pos, bits)
            row_at = pl.ds(pl.multiple_of(lax.shift_right_logical(at, 2) * rows, 8), rows)
            lane_at = pl.ds(pl.multiple_of(lax.bitwise_and(at, 3) * lanes, 128), lanes)
            ref = keep_ref if slot < half else send_ref
            for t in range(n_shards):
                ref[t, slot % half] = weight_acc[t, row_at, lane_at].astype(bf16)


def attn_bwd(pos, x, packed, probs, ctx_low, head, n_dp):
    rows, width = x.shape
    n_shards, n_seq = packed.shape[:2]
    q_block = 256
    half = n_dp // 2
    pieces = (n_shards, half, PART_ROWS * 4 // n_dp, width // 4)
    return pl.pallas_call(
        partial(attn_bwd_kernel, n_dp=n_dp, q_block=q_block),
        grid_spec=pltpu.PrefetchScalarGridSpec(
            num_scalar_prefetch=1,
            grid=(n_seq,),
            in_specs=[
                pl.BlockSpec((SEQ_LEN, width), lambda s, pos: (s, 0)),
                pl.BlockSpec((n_shards, 1, PART_ROWS, SEQ_LEN), lambda s, pos: (0, s, head, 0)),
                pl.BlockSpec((n_shards, 1, 1, SEQ_LEN, SEQ_LEN), lambda s, pos: (0, s, head, 0, 0)),
                pl.BlockSpec((n_shards, 1, HEAD_DIM, SEQ_LEN), lambda s, pos: (0, s, head, 0)),
            ],
            out_specs=[
                pl.BlockSpec((n_shards, 1, PART_ROWS, SEQ_LEN), lambda s, pos: (0, s, 0, 0)),
                pl.BlockSpec(pieces, lambda s, pos: (0, 0, 0, 0)),
                pl.BlockSpec(pieces, lambda s, pos: (0, 0, 0, 0)),
                pl.BlockSpec((n_shards, 8, PART_ROWS), lambda s, pos: (0, 0, 0)),
            ],
            scratch_shapes=[
                pltpu.VMEM((n_shards, SEQ_LEN, HEAD_DIM), bf16),
                pltpu.VMEM((HEAD_DIM, SEQ_LEN), f32),
                pltpu.VMEM((HEAD_DIM, SEQ_LEN), f32),
                pltpu.VMEM((n_shards, PART_ROWS, width), f32),
                pltpu.VMEM((SEQ_LEN, q_block), f32),
                pltpu.VMEM((SEQ_LEN, q_block), f32),
            ],
        ),
        out_shape=[
            jax.ShapeDtypeStruct((n_shards, n_seq, PART_ROWS, SEQ_LEN), bf16),
            jax.ShapeDtypeStruct(pieces, bf16),
            jax.ShapeDtypeStruct(pieces, bf16),
            jax.ShapeDtypeStruct((n_shards, 8, PART_ROWS), f32),
        ],
        compiler_params=pltpu.CompilerParams(vmem_limit_bytes=40 << 20),
        cost_estimate=pl.CostEstimate(flops=8 << 30, bytes_accessed=10 << 20, transcendentals=0),
        name="attn_bwd",
    )(pos, x, packed, probs, ctx_low)


def input_grad_kernel(grad_one_ref, weight_ref, *refs):
    out_ref = refs[-1]
    total = grad_one_ref[...]
    for head, ref in enumerate(refs[:-1]):
        for t in range(ref.shape[0]):
            total = total + mm_tn(ref[t, 0], weight_ref[t, head * PART_ROWS : (head + 1) * PART_ROWS, :])
    out_ref[...] = total.astype(bf16)


def input_gradient(grad_one, weight, packed_grads):
    rows, width = grad_one.shape
    n_shards = weight.shape[0]
    block = 512
    per_seq = SEQ_LEN // block
    row = pl.BlockSpec((block, width), lambda i: (i, 0))
    cols = pl.BlockSpec((n_shards, 1, PART_ROWS, block), lambda i: (0, i // per_seq, 0, i % per_seq))
    return pl.pallas_call(
        input_grad_kernel,
        grid=(rows // block,),
        in_specs=[row, pl.BlockSpec(weight.shape, lambda i: (0, 0, 0), pipeline_mode=pl.Buffered(1))]
        + [cols] * len(packed_grads),
        out_specs=row,
        out_shape=jax.ShapeDtypeStruct((rows, width), bf16),
        compiler_params=pltpu.CompilerParams(vmem_limit_bytes=40 << 20),
        cost_estimate=pl.CostEstimate(flops=4 << 30, bytes_accessed=12 << 20, transcendentals=0),
        name="input_gradient",
    )(grad_one, weight, *packed_grads)


def mlp_place_kernel(pos_ref, dn_near, dn_far, up_near, up_far, proj_out, up_out, dn_out, *, n_dp):
    pos = pos_ref[0]
    half = n_dp // 2
    width = proj_out.shape[1]
    hidden = dn_out.shape[0]
    dn_rows, up_rows, proj_rows = hidden // n_dp, width // n_dp, proj_out.shape[0] // n_dp
    for slot, bits in enumerate(piece_plan(n_dp)):
        at = lax.bitwise_xor(pos, bits)
        dn_ref = dn_near if slot < half else dn_far
        up_ref = up_near if slot < half else up_far
        k = slot % half
        dn_out[pl.ds(pl.multiple_of(at * dn_rows, dn_rows), dn_rows), :] = dn_ref[k].astype(f32)
        rows = pl.ds(pl.multiple_of(at * proj_rows, proj_rows), proj_rows)
        proj_out[rows, :] = up_ref[k, :proj_rows].astype(f32)
        rows = pl.ds(pl.multiple_of(at * up_rows, up_rows), up_rows)
        for j in range(hidden // width):
            to = proj_rows + j * up_rows
            up_out[rows, j * width : (j + 1) * width] = up_ref[k, to : to + up_rows].astype(f32)


def mlp_place(pos, dn_parts, up_parts, ctx_rows, width, hidden, n_dp):
    return pl.pallas_call(
        partial(mlp_place_kernel, n_dp=n_dp),
        in_specs=[pl.BlockSpec(memory_space=pltpu.SMEM)] + [pl.BlockSpec(memory_space=pltpu.VMEM)] * 4,
        out_specs=[pl.BlockSpec(memory_space=pltpu.VMEM)] * 3,
        out_shape=[
            jax.ShapeDtypeStruct((ctx_rows, width), f32),
            jax.ShapeDtypeStruct((width, hidden), f32),
            jax.ShapeDtypeStruct((hidden, width), f32),
        ],
        compiler_params=pltpu.CompilerParams(vmem_limit_bytes=30 << 20),
        cost_estimate=pl.CostEstimate(flops=0, bytes_accessed=14 << 20, transcendentals=0),
        name="mlp_place",
    )(pos, *dn_parts, *up_parts)


def qkv_place_kernel(pos_ref, *refs, n_dp):
    out_ref = refs[-1]
    pos = pos_ref[0]
    half = n_dp // 2
    rows, lanes = refs[0].shape[1:]
    for slot, bits in enumerate(piece_plan(n_dp)):
        at = lax.bitwise_xor(pos, bits)
        row_at = pl.ds(pl.multiple_of(lax.shift_right_logical(at, 2) * rows, 8), rows)
        lane_at = pl.ds(pl.multiple_of(lax.bitwise_and(at, 3) * lanes, 128), lanes)
        for head in range(len(refs) // 2):
            ref = refs[2 * head + (0 if slot < half else 1)]
            out_ref[head, row_at, lane_at] = ref[slot % half].astype(f32)


def qkv_place(pos, parts, n_dp):
    flat = [half for pair in parts for half in pair]
    _, rows, lanes = flat[0].shape
    heads = len(parts)
    return pl.pallas_call(
        partial(qkv_place_kernel, n_dp=n_dp),
        in_specs=[pl.BlockSpec(memory_space=pltpu.SMEM)] + [pl.BlockSpec(memory_space=pltpu.VMEM)] * len(flat),
        out_specs=pl.BlockSpec(memory_space=pltpu.VMEM),
        out_shape=jax.ShapeDtypeStruct((heads, rows * n_dp // 4, lanes * 4), f32),
        compiler_params=pltpu.CompilerParams(vmem_limit_bytes=20 << 20),
        cost_estimate=pl.CostEstimate(flops=0, bytes_accessed=3 << 20, transcendentals=0),
        name="qkv_place",
    )(pos, *flat)


def swap_dp(value, bits, n_dp):
    return lax.ppermute(value, "dp", [(i, i ^ bits) for i in range(n_dp)])


def shift_tensor(value, by, n_tensor):
    return lax.ppermute(value, "tensor", [((i + by) % n_tensor, i) for i in range(n_tensor)])


def fetch_shards(shard, parity, n_dp, n_tensor):
    half = shard.shape[0] // 2
    mine = lax.dynamic_slice_in_dim(shard, parity * half, half, 0)
    others = []
    for by in range(1, n_tensor):
        near = shift_tensor(mine, by, n_tensor)
        far = swap_dp(near, 1, n_dp)
        low = jnp.where(parity == 0, near, far)
        high = jnp.where(parity == 0, far, near)
        others.append(jnp.concatenate([low, high], axis=0))
    return others


def reduce_pieces(keep, send, n_dp, n_tensor):
    rest = n_dp // 4
    got = swap_dp(send, 1, n_dp)
    own = keep[0].astype(f32) + got[0].astype(f32)
    for by in range(1, n_tensor):
        out = (keep[by].astype(f32) + got[by].astype(f32)).astype(bf16)
        own = own + shift_tensor(out, -by, n_tensor).astype(f32)
    got = swap_dp(own[rest:].astype(bf16), 2, n_dp)
    own = own[:rest] + got.astype(f32)
    if rest > 1:
        low = own[1:].astype(bf16)
        one = own[0]
        for far in range(1, rest):
            one = one + swap_dp(low[far - 1], far << 2, n_dp).astype(f32)
        one = one.astype(bf16)
        near = jnp.stack([one] + [swap_dp(one, far << 2, n_dp) for far in range(1, rest)])
    else:
        near = own.astype(bf16)
    near = jnp.concatenate([near, swap_dp(near, 2, n_dp)], axis=0)
    return near, swap_dp(near, 1, n_dp)


def sum_over_dp(value, n_dp):
    bits = 1
    while bits < n_dp:
        value = value + swap_dp(value, bits, n_dp)
        bits *= 2
    return value


def sequence_body(n_dp, n_tensor, *arrays):
    (
        layer_input,
        output_grad,
        qkv_weight,
        query_bias,
        value_bias,
        proj_weight,
        proj_bias,
        first_gain,
        first_shift,
        up_weight,
        up_bias,
        down_weight,
        down_bias,
        second_gain,
        second_shift,
    ) = arrays
    rows, width = layer_input.shape
    ctx_rows, hidden = proj_weight.shape[0], up_weight.shape[1]
    n_heads = ctx_rows // HEAD_DIM
    place = lax.axis_index("dp").astype(jnp.int32)
    pos = place.reshape(1)
    parity = lax.rem(place, 2)

    def fetch(shard):
        return fetch_shards(shard, parity, n_dp, n_tensor)

    qkv_all = [qkv_weight] + fetch(qkv_weight)
    biases = jnp.stack([query_bias, value_bias, jnp.zeros_like(query_bias)]).astype(f32)
    up_b = up_bias.astype(f32).reshape(1, hidden)
    small = jnp.concatenate([biases.reshape(1, -1), up_b], axis=1)
    small_all = [small] + [shift_tensor(small, by, n_tensor) for by in range(1, n_tensor)]

    def bias_column(packed_small):
        parts = packed_small[0, : 3 * ctx_rows].reshape(3, n_heads, HEAD_DIM)
        return jnp.stack([parts[0], parts[2], parts[1]], axis=1).reshape(n_heads * PART_ROWS, 1)

    stacks = ()
    for t in range(n_tensor):
        stacks = attn_fwd(layer_input, qkv_all[t], bias_column(small_all[t]), t, n_tensor, stacks)
    packed, probs, ctx = stacks
    proj = jnp.stack([proj_weight] + fetch(proj_weight))
    up = jnp.stack([up_weight] + fetch(up_weight))
    down = jnp.stack([down_weight] + fetch(down_weight))
    up_b_all = jnp.concatenate([one[:, 3 * ctx_rows :] for one in small_all], axis=1)
    vectors = [
        v.astype(f32).reshape(1, width)
        for v in (proj_bias, first_gain, first_shift, down_bias, second_gain, second_shift)
    ]
    result, grad_one, ctx_low, dn_keep, dn_send, up_keep, up_send, vec, up_bg = middle(
        pos, layer_input, output_grad, ctx, proj, vectors, up, up_b_all, down, n_dp
    )
    dn_parts = reduce_pieces(dn_keep, dn_send, n_dp, n_tensor)
    up_parts = reduce_pieces(up_keep, up_send, n_dp, n_tensor)
    vec = sum_over_dp(jnp.concatenate([vec.reshape(1, -1), up_bg], axis=1), n_dp)
    packed_grads, qkv_parts, bias_sums = [], [], []
    for head in range(n_heads):
        grads, keep, send, sums = attn_bwd(pos, layer_input, packed, probs, ctx_low, head, n_dp)
        packed_grads.append(grads)
        qkv_parts.append(reduce_pieces(keep, send, n_dp, n_tensor))
        bias_sums.append(sums[:, 0])
    bias_sums = sum_over_dp(jnp.stack(bias_sums, axis=1), n_dp)
    input_grad = input_gradient(grad_one, jnp.stack(qkv_all), packed_grads)
    proj_wg, up_wg, dn_wg = mlp_place(pos, dn_parts, up_parts, ctx_rows, width, hidden, n_dp)
    qkv_wg = qkv_place(pos, qkv_parts, n_dp).reshape(n_heads * PART_ROWS, width)

    own_bias = bias_sums[0]
    size = 8 * width
    shared, up_bg = vec[:, :size], vec[:, size:]
    own_up_bg = up_bg[:, :hidden]
    total = shared
    for by in range(1, n_tensor):
        total = total + shift_tensor(shared, by, n_tensor)
        own_up_bg = own_up_bg + shift_tensor(up_bg[:, by * hidden : (by + 1) * hidden], -by, n_tensor)
        own_bias = own_bias + shift_tensor(bias_sums[by], -by, n_tensor)
    total = total.reshape(8, width)
    return (
        result,
        input_grad,
        qkv_wg,
        own_bias[:, :HEAD_DIM].reshape(ctx_rows),
        own_bias[:, 2 * HEAD_DIM :].reshape(ctx_rows),
        proj_wg,
        total[0],
        total[1],
        total[2],
        up_wg,
        own_up_bg.reshape(hidden),
        dn_wg,
        total[3],
        total[4],
        total[5],
    )


def solution(mesh):
    n_dp, n_tensor = mesh.shape["dp"], mesh.shape["tensor"]

    def body(*arrays):
        rows = arrays[0].shape[0]
        if rows % SEQ_LEN == 0 and n_dp % 4 == 0 and n_dp & (n_dp - 1) == 0:
            return sequence_body(n_dp, n_tensor, *arrays)
        return token_body(*arrays)

    return jax.shard_map(
        body,
        mesh=mesh,
        in_specs=(
            P(("dp", "tensor"), None),
            P(("dp", "tensor"), None),
            P("tensor", None),
            P("tensor"),
            P("tensor"),
            P("tensor", None),
            P(),
            P(),
            P(),
            P(None, "tensor"),
            P("tensor"),
            P("tensor", None),
            P(),
            P(),
            P(),
        ),
        out_specs=(
            P(("dp", "tensor"), None),
            P(("dp", "tensor"), None),
            P("tensor", None),
            P("tensor"),
            P("tensor"),
            P("tensor", None),
            P(),
            P(),
            P(),
            P(None, "tensor"),
            P("tensor"),
            P("tensor", None),
            P(),
            P(),
            P(),
        ),
        check_vma=False,
    )
```

```python
from functools import partial

import jax
import jax.numpy as jnp
from jax import lax
from jax.experimental import pallas as pl
from jax.experimental.pallas import tpu as pltpu
from jax.sharding import PartitionSpec as P

HEAD_DIM = 64
SEQ_LEN = 1024
PART_ROWS = 3 * HEAD_DIM

norm_eps = 1e-05
f32 = jnp.float32
bf16 = jnp.bfloat16


def matmul_rows(left, right):
    return lax.dot_general(
        left, right, (((0,), (0,)), ((), ())), preferred_element_type=jnp.float32
    )


def matmul_back(left, right):
    return lax.dot_general(
        left, right, (((1,), (1,)), ((), ())), preferred_element_type=jnp.float32
    )


def attend_forward(queries, key_rows, value_rows):
    seq_heads = key_rows.shape[0] * key_rows.shape[1]
    head_dim = queries.shape[-1]
    score_scale = head_dim ** (-0.5)
    block_rows = min(512, SEQ_LEN)
    block_count = SEQ_LEN // block_rows
    item_count = seq_heads * block_count
    query_items = queries.reshape(item_count, block_rows, head_dim)
    key_all = key_rows.reshape(seq_heads, SEQ_LEN, head_dim)
    value_all = value_rows.reshape(seq_heads, SEQ_LEN, head_dim)

    def one_block(block_item):
        query_blk, position = block_item
        owner_index = position // block_count
        keys_here = key_all[owner_index]
        values_here = value_all[owner_index]
        scores = matmul_back(query_blk, keys_here) * score_scale
        row_top = jnp.max(scores, axis=-1, keepdims=True)
        exponent = jnp.exp(scores - row_top)
        row_total = jnp.sum(exponent, axis=-1, keepdims=True)
        weights_now = exponent / row_total
        mixed_rows = jnp.dot(
            weights_now.astype(jnp.bfloat16), values_here, preferred_element_type=jnp.float32
        )
        return (mixed_rows, row_top[:, 0] + jnp.log(row_total[:, 0]))

    mixed_rows, log_total = lax.map(
        one_block, (query_items, jnp.arange(item_count, dtype=jnp.int32))
    )
    return (mixed_rows.reshape(queries.shape), log_total.reshape(queries.shape[:-1]))


def attend_backward(queries, key_rows, value_rows, log_total, context_low):
    seq_heads = key_rows.shape[0] * key_rows.shape[1]
    head_dim = queries.shape[-1]
    score_scale = head_dim ** (-0.5)
    block_rows = min(512, SEQ_LEN)
    block_count = SEQ_LEN // block_rows
    item_count = seq_heads * block_count
    query_items = queries.reshape(item_count, block_rows, head_dim)
    total_items = log_total.reshape(item_count, block_rows)
    grad_items = context_low.reshape(item_count, block_rows, head_dim)
    key_all = key_rows.reshape(seq_heads, SEQ_LEN, head_dim)
    value_all = value_rows.reshape(seq_heads, SEQ_LEN, head_dim)

    def one_block(block_item):
        query_blk, total_blk, grad_blk, position = block_item
        owner_index = position // block_count
        keys_here = key_all[owner_index]
        values_here = value_all[owner_index]
        scores = matmul_back(query_blk, keys_here) * score_scale
        weights_now = jnp.exp(scores - total_blk[:, None])
        grad_weights = matmul_back(grad_blk, values_here)
        grad_scores = weights_now * (
            grad_weights - jnp.sum(weights_now * grad_weights, axis=-1, keepdims=True)
        )
        score_low = grad_scores.astype(jnp.bfloat16)
        grad_query = jnp.dot(score_low, keys_here, preferred_element_type=jnp.float32) * score_scale
        grad_key = matmul_rows(score_low, query_blk) * score_scale
        grad_value = matmul_rows(weights_now.astype(jnp.bfloat16), grad_blk)
        return (grad_query, grad_key, grad_value)

    grad_query, grad_key, grad_value = lax.map(
        one_block, (query_items, total_items, grad_items, jnp.arange(item_count, dtype=jnp.int32))
    )
    grad_key = jnp.sum(grad_key.reshape(seq_heads, block_count, SEQ_LEN, head_dim), axis=1)
    grad_value = jnp.sum(grad_value.reshape(seq_heads, block_count, SEQ_LEN, head_dim), axis=1)
    return (
        grad_query.reshape(queries.shape),
        grad_key.reshape(key_rows.shape),
        grad_value.reshape(value_rows.shape),
    )


def norm_forward(hidden, gain_vec, shift_vec):
    center = jnp.mean(hidden, axis=-1)
    second = jnp.mean(hidden * hidden, axis=-1) - center * center
    inv_std = lax.rsqrt(second + norm_eps)
    normal = (hidden - center[:, None]) * inv_std[:, None]
    return (normal * gain_vec + shift_vec, normal, inv_std)


def norm_backward(upstream, normal, inv_std, gain_vec):
    scaled = upstream * gain_vec
    first_mean = jnp.mean(scaled, axis=-1)
    second_mean = jnp.mean(scaled * normal, axis=-1)
    grad_in = inv_std[:, None] * (scaled - first_mean[:, None] - normal * second_mean[:, None])
    return (grad_in, jnp.sum(upstream * normal, axis=0), jnp.sum(upstream, axis=0))


def rows_in(value):
    return lax.all_gather(value, "tensor", axis=0, tiled=True)


def part_out(value):
    return lax.psum_scatter(value, "tensor", scatter_dimension=0, tiled=True)


def gather_grad(value):
    return lax.all_gather(value, "tensor", axis=0, tiled=True)


def part_back(value):
    return lax.psum_scatter(value, "tensor", scatter_dimension=0, tiled=True)


def token_body(
    layer_input,
    output_grad,
    qkv_weight,
    query_bias,
    value_bias,
    proj_weight,
    proj_bias,
    first_gain,
    first_shift,
    up_weight,
    up_bias,
    down_weight,
    down_bias,
    second_gain,
    second_shift,
):
    heads_here = query_bias.shape[0] // HEAD_DIM
    query_bf = query_bias.astype(jnp.float32).reshape(heads_here, HEAD_DIM)
    value_bf = value_bias.astype(jnp.float32).reshape(heads_here, HEAD_DIM)
    bias_rows = jnp.stack([query_bf, jnp.zeros_like(query_bf), value_bf], axis=1)
    gain_one = first_gain.astype(jnp.float32)
    shift_one = first_shift.astype(jnp.float32)
    gain_two = second_gain.astype(jnp.float32)
    shift_two = second_shift.astype(jnp.float32)
    input_full = rows_in(layer_input)
    row_count = input_full.shape[0]
    seq_count = row_count // SEQ_LEN
    projected = matmul_back(input_full, qkv_weight).reshape(row_count, heads_here, 3, HEAD_DIM)
    packed = (projected + bias_rows).astype(jnp.bfloat16)
    parts = packed.reshape(seq_count, SEQ_LEN, heads_here, 3, HEAD_DIM).transpose(3, 0, 2, 1, 4)
    queries, key_rows, value_rows = (parts[0], parts[1], parts[2])
    mixed_rows, log_total = attend_forward(queries, key_rows, value_rows)
    context = (
        mixed_rows.transpose(0, 2, 1, 3)
        .reshape(row_count, heads_here * HEAD_DIM)
        .astype(jnp.bfloat16)
    )
    partial_branch = jnp.dot(context, proj_weight, preferred_element_type=jnp.float32)
    branch = part_out(partial_branch) + proj_bias.astype(jnp.float32)
    normed_one, normal_one, inv_one = norm_forward(
        layer_input.astype(jnp.float32) + branch, gain_one, shift_one
    )
    normed_full = rows_in(normed_one.astype(jnp.bfloat16))
    inner_pre = jnp.dot(
        normed_full, up_weight, preferred_element_type=jnp.float32
    ) + up_bias.astype(jnp.float32)
    active, gelu_back = jax.vjp(partial(jax.nn.gelu, approximate=False), inner_pre)
    active_low = active.astype(jnp.bfloat16)
    second = part_out(
        jnp.dot(active_low, down_weight, preferred_element_type=jnp.float32)
    ) + down_bias.astype(jnp.float32)
    result_rows, normal_two, inv_two = norm_forward(normed_one + second, gain_two, shift_two)
    upstream = output_grad.astype(jnp.float32)
    grad_two, gain_two_grad, shift_two_grad = norm_backward(upstream, normal_two, inv_two, gain_two)
    second_low = grad_two.astype(jnp.bfloat16)
    down_b_grad = jnp.sum(second_low.astype(jnp.float32), axis=0)
    second_full = gather_grad(second_low)
    down_w_grad = matmul_rows(active_low, second_full)
    grad_active = matmul_back(second_full, down_weight)
    inner_low = gelu_back(grad_active)[0].astype(jnp.bfloat16)
    up_b_grad = jnp.sum(inner_low.astype(jnp.float32), axis=0)
    up_w_grad = matmul_rows(normed_full, inner_low)
    grad_mid = grad_two + part_back(matmul_back(inner_low, up_weight))
    grad_one, gain_one_grad, shift_one_grad = norm_backward(grad_mid, normal_one, inv_one, gain_one)
    branch_low = grad_one.astype(jnp.bfloat16)
    proj_b_grad = jnp.sum(branch_low.astype(jnp.float32), axis=0)
    branch_full = gather_grad(branch_low)
    proj_w_grad = matmul_rows(context, branch_full)
    context_low = matmul_back(branch_full, proj_weight).astype(jnp.bfloat16)
    context_low = context_low.reshape(seq_count, SEQ_LEN, heads_here, HEAD_DIM).transpose(
        0, 2, 1, 3
    )
    grad_query, grad_key, grad_value = attend_backward(
        queries, key_rows, value_rows, log_total, context_low
    )
    packed_low = jnp.stack([grad_query, grad_key, grad_value], axis=0).transpose(1, 3, 2, 0, 4)
    packed_low = packed_low.reshape(row_count, heads_here * 3 * HEAD_DIM).astype(jnp.bfloat16)
    packed_sums = jnp.sum(packed_low.astype(jnp.float32), axis=0).reshape(heads_here, 3, HEAD_DIM)
    query_b_grad = packed_sums[:, 0].reshape(heads_here * HEAD_DIM)
    value_b_grad = packed_sums[:, 2].reshape(heads_here * HEAD_DIM)
    qkv_w_grad = matmul_rows(packed_low, input_full)
    input_grad = (
        grad_one + part_back(jnp.dot(packed_low, qkv_weight, preferred_element_type=jnp.float32))
    ).astype(jnp.bfloat16)
    totals = (
        lax.psum(qkv_w_grad.astype(jnp.bfloat16), "dp").astype(jnp.float32),
        lax.psum(query_b_grad.astype(jnp.bfloat16), "dp").astype(jnp.float32),
        lax.psum(value_b_grad.astype(jnp.bfloat16), "dp").astype(jnp.float32),
        lax.psum(proj_w_grad.astype(jnp.bfloat16), "dp").astype(jnp.float32),
        lax.psum(up_w_grad.astype(jnp.bfloat16), "dp").astype(jnp.float32),
        lax.psum(up_b_grad.astype(jnp.bfloat16), "dp").astype(jnp.float32),
        lax.psum(down_w_grad.astype(jnp.bfloat16), "dp").astype(jnp.float32),
    )
    vectors = lax.psum(
        (proj_b_grad, gain_one_grad, shift_one_grad, down_b_grad, gain_two_grad, shift_two_grad),
        ("dp", "tensor"),
    )
    return (
        result_rows.astype(jnp.bfloat16),
        input_grad,
        totals[0],
        totals[1],
        totals[2],
        totals[3],
        vectors[0],
        vectors[1],
        vectors[2],
        totals[4],
        totals[5],
        totals[6],
        vectors[3],
        vectors[4],
        vectors[5],
    )


VMEM_LIMIT = 66_000_000
EXTRA = 16


def mm(left, right):
    return lax.dot_general(left, right, (((1,), (0,)), ((), ())), preferred_element_type=f32)


def mm_nt(left, right):
    return lax.dot_general(left, right, (((1,), (1,)), ((), ())), preferred_element_type=f32)


def mm_tn(left, right):
    return lax.dot_general(left, right, (((0,), (0,)), ((), ())), preferred_element_type=f32)


def kernel_params(limit=VMEM_LIMIT):
    return pltpu.CompilerParams(vmem_limit_bytes=limit)


def cost(flops, size):
    return pl.CostEstimate(flops=int(flops), bytes_accessed=int(size), transcendentals=0)


def in_vmem():
    return pl.BlockSpec(memory_space=pltpu.VMEM)


def aligned(start, size, by):
    return pl.ds(pl.multiple_of(start * size, by), size)


def pack_qkv_kernel(pos_ref, weight_ref, query_b_ref, value_b_ref, packed_ref, own_b_ref):
    half = weight_ref.shape[0]
    wide = query_b_ref.shape[0] // 2
    query_b, value_b = (ref[...].reshape(1, 2 * wide) for ref in (query_b_ref, value_b_ref))
    packed_ref[:half] = weight_ref[...]
    packed_ref[half:] = jnp.zeros_like(packed_ref[half:])
    own_b_ref[...] = jnp.zeros_like(own_b_ref)
    parity = lax.rem(pos_ref[0], 2)
    for k in range(2):
        cols = slice(k * wide, (k + 1) * wide)
        own_b_ref[k * EXTRA : k * EXTRA + 1, :wide] = query_b[:, cols]
        own_b_ref[k * EXTRA : k * EXTRA + 1, wide : 2 * wide] = value_b[:, cols]

        @pl.when(parity == k)
        def _():
            packed_ref[half : half + 1, :wide] = query_b[:, cols]
            packed_ref[half : half + 1, wide : 2 * wide] = value_b[:, cols]


def pack_qkv(pos, weight, query_b, value_b):
    rows, width = weight.shape
    half = rows // 2
    small = pl.BlockSpec(query_b.shape, lambda i, pos: (0,))
    return pl.pallas_call(
        pack_qkv_kernel,
        grid_spec=pltpu.PrefetchScalarGridSpec(
            num_scalar_prefetch=1,
            grid=(1,),
            in_specs=[pl.BlockSpec((half, width), lambda i, pos: (lax.rem(pos[0], 2), 0)), small, small],
            out_specs=[
                pl.BlockSpec((half + EXTRA, width), lambda i, pos: (0, 0)),
                pl.BlockSpec((2 * EXTRA, width), lambda i, pos: (0, 0)),
            ],
        ),
        out_shape=[
            jax.ShapeDtypeStruct((half + EXTRA, width), bf16),
            jax.ShapeDtypeStruct((2 * EXTRA, width), bf16),
        ],
        compiler_params=kernel_params(),
        cost_estimate=cost(0, 1 << 20),
        name="pack_qkv",
    )(pos, weight, query_b, value_b)


def pack_mlp_kernel(pos_ref, proj_ref, down_ref, up_ref, up_b_ref, *refs):
    vec_refs, packed_ref, vecs_ref = refs[:-2], refs[-2], refs[-1]
    width = proj_ref.shape[1]
    at = 0
    for value in (proj_ref[...], down_ref[...]):
        packed_ref[at : at + value.shape[0]] = value
        at += value.shape[0]
    blocks = up_ref.shape[1] // width
    for j in range(blocks):
        packed_ref[at : at + up_ref.shape[0]] = up_ref[:, j * width : (j + 1) * width]
        at += up_ref.shape[0]
    packed_ref[at:] = jnp.zeros_like(packed_ref[at:])
    vecs_ref[...] = jnp.zeros_like(vecs_ref)
    for j in range(blocks):
        row = up_b_ref[j * width : (j + 1) * width].reshape(1, width)
        packed_ref[at + j : at + j + 1] = row
        vecs_ref[8 + j : 9 + j] = row.astype(f32)
    for k, ref in enumerate(vec_refs):
        vecs_ref[k : k + 1] = ref[...].reshape(1, width).astype(f32)


def pack_mlp(pos, proj, down, up, up_b, vectors):
    width, hidden = up.shape
    rows = (proj.shape[0] + 2 * hidden) // 2 + EXTRA

    def half(array):
        return pl.BlockSpec((array.shape[0] // 2, array.shape[1]), lambda i, pos: (lax.rem(pos[0], 2), 0))

    def whole(array):
        return pl.BlockSpec(array.shape, lambda i, pos: (0,))

    return pl.pallas_call(
        pack_mlp_kernel,
        grid_spec=pltpu.PrefetchScalarGridSpec(
            num_scalar_prefetch=1,
            grid=(1,),
            in_specs=[half(proj), half(down), half(up), whole(up_b)] + [whole(v) for v in vectors],
            out_specs=[
                pl.BlockSpec((rows, width), lambda i, pos: (0, 0)),
                pl.BlockSpec((EXTRA, width), lambda i, pos: (0, 0)),
            ],
        ),
        out_shape=[jax.ShapeDtypeStruct((rows, width), bf16), jax.ShapeDtypeStruct((EXTRA, width), f32)],
        compiler_params=kernel_params(),
        cost_estimate=cost(0, 3 << 20),
        name="pack_mlp",
    )(pos, proj, down, up, up_b, *vectors)


def attn_fwd_kernel(pos_ref, x_ref, w_ref, b_ref, *refs, heads, q_block):
    packed_ref, probs_ref, ctx_ref, key_ref, score_a, score_b = refs[-6:]
    seq = x_ref.shape[0]
    scale = HEAD_DIM**-0.5
    wide = heads * HEAD_DIM
    column = b_ref[:8, : 2 * wide].astype(f32).T
    raw = mm_nt(w_ref[...], x_ref[...])
    for h in range(heads):
        base = h * PART_ROWS
        ends = (base + HEAD_DIM, base + 2 * HEAD_DIM, base + PART_ROWS)
        query = raw[base : ends[0]] + column[h * HEAD_DIM : (h + 1) * HEAD_DIM, :1]
        value = raw[ends[1] : ends[2]] + column[wide + h * HEAD_DIM : wide + (h + 1) * HEAD_DIM, :1]
        packed_ref[0, 0, base : ends[0]] = query.astype(bf16)
        packed_ref[0, 0, ends[0] : ends[1]] = raw[ends[0] : ends[1]].astype(bf16)
        packed_ref[0, 0, ends[1] : ends[2]] = value.astype(bf16)
        keys = packed_ref[0, 0, ends[0] : ends[1], :].astype(f32)
        key_ref[h] = (keys.T * scale).astype(bf16)
    tiles = [(h, c) for h in range(heads) for c in range(0, seq, q_block)]
    scores = (score_a, score_b)

    def score(tile, ref):
        h, c = tile
        base = h * PART_ROWS
        ref[...] = mm(key_ref[h], packed_ref[0, 0, base : base + HEAD_DIM, c : c + q_block])

    def finish(tile, ref):
        h, c = tile
        base = h * PART_ROWS
        top = jnp.max(ref[...], axis=0, keepdims=True)
        exponent = jnp.exp(ref[...] - top)
        total = jnp.sum(exponent, axis=0, keepdims=True)
        probs = (exponent * (1.0 / total)).astype(bf16)
        probs_ref[0, 0, h, :, c : c + q_block] = probs
        mixed = mm(packed_ref[0, 0, base + 2 * HEAD_DIM : base + 3 * HEAD_DIM, :], probs)
        ctx_ref[0, 0, h * HEAD_DIM : (h + 1) * HEAD_DIM, c : c + q_block] = mixed.astype(bf16)

    score(tiles[0], scores[0])
    for j, tile in enumerate(tiles):
        if j + 1 < len(tiles):
            score(tiles[j + 1], scores[(j + 1) % 2])
        finish(tile, scores[j % 2])


def attn_fwd(pos, x, weight, bias, shard, halves, shapes, earlier):
    rows, width = x.shape
    n_seq = rows // SEQ_LEN
    heads = shapes[1].shape[2] // 2
    part = heads * PART_ROWS

    def at(k, pos):
        if len(halves) == 2:
            return k
        parity = lax.rem(pos[0], 2)
        return parity if halves[0] == 0 else 1 - parity

    in_specs = [
        pl.BlockSpec((SEQ_LEN, width), lambda s, k, pos: (s, 0)),
        pl.BlockSpec((part, width), lambda s, k, pos: (k, 0)),
        pl.BlockSpec((EXTRA, width), lambda s, k, pos: (k if len(halves) == 2 else part // EXTRA, 0)),
    ] + [pl.BlockSpec(memory_space=pl.ANY)] * len(earlier)
    out_specs = [
        pl.BlockSpec((1, 1, part, SEQ_LEN), lambda s, k, pos: (shard, s, at(k, pos), 0)),
        pl.BlockSpec((1, 1, heads, SEQ_LEN, SEQ_LEN), lambda s, k, pos: (shard, s, at(k, pos), 0, 0)),
        pl.BlockSpec((1, 1, heads * HEAD_DIM, SEQ_LEN), lambda s, k, pos: (shard, s, at(k, pos), 0)),
    ]
    q_block = 512
    share = len(halves) * n_seq * heads
    flops = share * (2 * SEQ_LEN * width * PART_ROWS + 4 * SEQ_LEN * SEQ_LEN * HEAD_DIM * 6)
    return pl.pallas_call(
        partial(attn_fwd_kernel, heads=heads, q_block=q_block),
        grid_spec=pltpu.PrefetchScalarGridSpec(
            num_scalar_prefetch=1,
            grid=(n_seq, len(halves)),
            in_specs=in_specs,
            out_specs=out_specs,
            scratch_shapes=[
                pltpu.VMEM((heads, SEQ_LEN, HEAD_DIM), bf16),
                pltpu.VMEM((SEQ_LEN, q_block), f32),
                pltpu.VMEM((SEQ_LEN, q_block), f32),
            ],
        ),
        out_shape=shapes,
        input_output_aliases={4: 0, 5: 1, 6: 2} if earlier else {},
        compiler_params=kernel_params(),
        cost_estimate=cost(flops, share * 3 << 20),
        name="attn_fwd",
    )(pos, x, weight, bias, *earlier)


def piece_bits(*order):
    bits = [0]
    for bit in reversed(order):
        bits = bits + [b | bit for b in bits]
    return bits


MLP_SLOTS = 8
DOWN_ORDER = ("tensor", 2, 4)
UP_ORDER = (4, "tensor", 2)
DOWN_BITS = piece_bits(1, 2, 4)
UP_BITS = piece_bits(1, 4, 2)


def middle_kernel(
    pos_ref,
    x_ref,
    og_ref,
    ctx_ref,
    vecs_ref,
    proj_own,
    up_own,
    down_own,
    *refs,
    n_others,
    chunk,
):
    fetched, refs = refs[: 2 * n_others], refs[2 * n_others :]
    out_ref, grad_one_ref, ctx_low_ref, dn_keep_ref, dn_send_ref, up_keep_ref, up_send_ref, *refs = refs
    proj_got, up_got, down_got, up_b_ref, act_ref, slope_ref, proj_acc, up_acc, dn_acc, vec_acc, up_b_acc = refs
    step = pl.program_id(0)
    n_shards = n_others + 1
    ctx_rows, width = proj_own.shape
    hidden = up_own.shape[1]
    blocks = hidden // width
    inv_width = 1.0 / width

    def mean(v):
        return jnp.sum(v, axis=1, keepdims=True) * inv_width

    @pl.when(step == 0)
    def _():
        for ref in (proj_acc, up_acc, dn_acc, vec_acc, up_b_acc):
            ref[...] = jnp.zeros_like(ref)
        parity = lax.rem(pos_ref[0], 2)
        for j in range(blocks):
            up_b_ref[:, j * width : (j + 1) * width] = vecs_ref[8 + j : 9 + j, :]
        for t in range(n_others):
            for k in range(2):
                ref = fetched[2 * t + k]
                side = parity if k == 0 else 1 - parity
                rows = ctx_rows // 2
                proj_got[t, aligned(side, rows, rows), :] = ref[:rows]
                at = rows
                rows = hidden // 2
                down_got[t, aligned(side, rows, rows), :] = ref[at : at + rows]
                at += rows
                rows = width // 2
                for j in range(blocks):
                    up_got[t, aligned(side, rows, rows), j * width : (j + 1) * width] = ref[at : at + rows]
                    at += rows
                if k == 0:
                    for j in range(blocks):
                        to = (t + 1) * hidden + j * width
                        up_b_ref[:, to : to + width] = ref[at : at + EXTRA].astype(f32)[j : j + 1]

    def proj(t):
        return proj_own[...] if t == 0 else proj_got[t - 1]

    def up(t, c):
        return up_own[:, c : c + chunk] if t == 0 else up_got[t - 1, :, c : c + chunk]

    def down(t, c):
        return down_own[c : c + chunk, :] if t == 0 else down_got[t - 1, c : c + chunk, :]

    proj_b, gain_one, shift_one, down_b, gain_two, shift_two = (vecs_ref[k : k + 1, :] for k in range(6))
    branch = proj_b
    for t in range(n_shards):
        branch = branch + mm_tn(ctx_ref[t, 0], proj(t))
    mid_sum = x_ref[...].astype(f32) + branch
    center = mean(mid_sum)
    inv_one = lax.rsqrt(mean(mid_sum * mid_sum) - center * center + norm_eps)
    normal_one = (mid_sum - center) * inv_one
    normed_one = normal_one * gain_one + shift_one
    normed_low = normed_one.astype(bf16)
    second = down_b
    chunks = [(t, c) for t in range(n_shards) for c in range(0, hidden, chunk)]
    for t, c in chunks:
        at = t * hidden + c
        inner = mm(normed_low, up(t, c)) + up_b_ref[:, at : at + chunk]
        phi = 0.5 * lax.erf(inner * 0.7071067811865476) + 0.5
        active = (inner * phi).astype(bf16)
        act_ref[:, at : at + chunk] = active
        slope_ref[:, at : at + chunk] = phi + inner * (0.3989422804014327 * jnp.exp(-0.5 * inner * inner))
        second = second + mm(active, down(t, c))
    last_sum = normed_one + second
    center_two = mean(last_sum)
    inv_two = lax.rsqrt(mean(last_sum * last_sum) - center_two * center_two + norm_eps)
    normal_two = (last_sum - center_two) * inv_two
    out_ref[...] = (normal_two * gain_two + shift_two).astype(bf16)
    upstream = og_ref[...].astype(f32)
    scaled = upstream * gain_two
    grad_two = inv_two * (scaled - mean(scaled) - normal_two * mean(scaled * normal_two))
    second_low = grad_two.astype(bf16)
    normed_t = normed_low.T
    back = None
    for t, c in chunks:
        at = t * hidden + c
        grad_active = mm_nt(second_low, down(t, c))
        inner_low = (grad_active * slope_ref[:, at : at + chunk]).astype(bf16)
        up_b_acc[:, at : at + chunk] += jnp.sum(inner_low.astype(f32), axis=0, keepdims=True)
        part = mm_nt(inner_low, up(t, c))
        back = part if back is None else back + part
        up_acc[t, :, c : c + chunk] += mm(normed_t, inner_low)
        dn_acc[t, c : c + chunk, :] += mm_tn(act_ref[:, at : at + chunk], second_low)
    grad_mid = grad_two + back
    scaled_one = grad_mid * gain_one
    grad_one = inv_one * (scaled_one - mean(scaled_one) - normal_one * mean(scaled_one * normal_one))
    grad_one_ref[...] = grad_one
    branch_low = grad_one.astype(bf16)
    sums = (
        branch_low.astype(f32),
        grad_mid * normal_one,
        grad_mid,
        second_low.astype(f32),
        upstream * normal_two,
        upstream,
    )
    for k, value in enumerate(sums):
        vec_acc[k : k + 1, :] += jnp.sum(value, axis=0, keepdims=True)
    for t in range(n_shards):
        ctx_low_ref[t, 0] = mm_nt(proj(t), branch_low).astype(bf16)
        proj_acc[t] += mm(ctx_ref[t, 0], branch_low)

    @pl.when(step == pl.num_programs(0) - 1)
    def _():
        low = lax.rem(pos_ref[0], MLP_SLOTS)
        dn_rows, up_rows, proj_rows = hidden // MLP_SLOTS, width // MLP_SLOTS, ctx_rows // MLP_SLOTS
        half = MLP_SLOTS // 2
        for slot in range(MLP_SLOTS):
            dn_ref = dn_keep_ref if slot < half else dn_send_ref
            upk_ref = up_keep_ref if slot < half else up_send_ref
            k = slot % half
            dn_at = lax.bitwise_xor(low, DOWN_BITS[slot])
            rows = aligned(lax.bitwise_xor(low, UP_BITS[slot]), up_rows, up_rows)
            for t in range(n_shards):
                dn_ref[t, k, :dn_rows] = dn_acc[t, aligned(dn_at, dn_rows, dn_rows), :].astype(bf16)
                dn_ref[t, k, dn_rows:] = proj_acc[t, aligned(dn_at, proj_rows, proj_rows), :].astype(bf16)
                for j in range(blocks):
                    to = j * up_rows
                    upk_ref[t, k, to : to + up_rows] = up_acc[t, rows, j * width : (j + 1) * width].astype(bf16)
                to = blocks * up_rows
                upk_ref[t, k, to : to + 8] = vec_acc[...].astype(bf16)
                tail = [
                    up_b_acc[:, t * hidden + j * width : t * hidden + (j + 1) * width] for j in range(blocks)
                ]
                tail.append(jnp.zeros((8 - blocks, width), f32))
                upk_ref[t, k, to + 8 : to + EXTRA] = jnp.concatenate(tail, axis=0).astype(bf16)


def middle(pos, x, out_grad, ctx, vecs, proj, up, down, fetched):
    rows, width = x.shape
    n_shards, n_seq, ctx_rows, _ = ctx.shape
    hidden = up.shape[1]
    n_others = n_shards - 1
    block = 512
    per_seq = SEQ_LEN // block
    half = MLP_SLOTS // 2
    dn_rows, up_rows = (hidden + ctx_rows) // MLP_SLOTS, hidden // MLP_SLOTS + EXTRA

    def whole(array):
        return pl.BlockSpec(array.shape, lambda i, pos: (0,) * array.ndim, pipeline_mode=pl.Buffered(1))

    def kept(*shape):
        return pl.BlockSpec(shape, lambda i, pos: (0,) * len(shape))

    row = pl.BlockSpec((block, width), lambda i, pos: (i, 0))
    cols = pl.BlockSpec((n_shards, 1, ctx_rows, block), lambda i, pos: (0, i // per_seq, 0, i % per_seq))
    dn_shape, up_shape = (n_shards, half, dn_rows, width), (n_shards, half, up_rows, width)
    consts = [vecs, proj, up, down] + fetched
    return pl.pallas_call(
        partial(middle_kernel, n_others=n_others, chunk=min(1024, hidden)),
        grid_spec=pltpu.PrefetchScalarGridSpec(
            num_scalar_prefetch=1,
            grid=(rows // block,),
            in_specs=[row, row, cols] + [whole(array) for array in consts],
            out_specs=[row, row, cols, kept(*dn_shape), kept(*dn_shape), kept(*up_shape), kept(*up_shape)],
            scratch_shapes=[
                pltpu.VMEM((n_others, ctx_rows, width), bf16),
                pltpu.VMEM((n_others, width, hidden), bf16),
                pltpu.VMEM((n_others, hidden, width), bf16),
                pltpu.VMEM((1, n_shards * hidden), f32),
                pltpu.VMEM((block, n_shards * hidden), bf16),
                pltpu.VMEM((block, n_shards * hidden), f32),
                pltpu.VMEM((n_shards, ctx_rows, width), f32),
                pltpu.VMEM((n_shards, width, hidden), f32),
                pltpu.VMEM((n_shards, hidden, width), f32),
                pltpu.VMEM((8, width), f32),
                pltpu.VMEM((1, n_shards * hidden), f32),
            ],
        ),
        out_shape=[
            jax.ShapeDtypeStruct((rows, width), bf16),
            jax.ShapeDtypeStruct((rows, width), f32),
            jax.ShapeDtypeStruct(ctx.shape, bf16),
            jax.ShapeDtypeStruct(dn_shape, bf16),
            jax.ShapeDtypeStruct(dn_shape, bf16),
            jax.ShapeDtypeStruct(up_shape, bf16),
            jax.ShapeDtypeStruct(up_shape, bf16),
        ],
        compiler_params=kernel_params(),
        cost_estimate=cost(30 << 30, 30 << 20),
        name="middle",
    )(pos, x, out_grad, ctx, *consts)


HEAD_BITS = {2: piece_bits(1), 4: piece_bits(1, 2)}


def attn_bwd_kernel(
    pos_ref,
    x_ref,
    packed_ref,
    probs_ref,
    ctx_low_ref,
    sums_ref,
    *refs,
    head,
    slots,
    extra,
    q_block,
):
    grad_ref, keep_ref, send_ref, bias_ref, *refs = refs[-10:]
    value_ref, key_acc, value_acc, weight_acc, grad_a, grad_b = refs
    step = pl.program_id(0)
    seq = x_ref.shape[0]
    n_shards = packed_ref.shape[0]
    scale = HEAD_DIM**-0.5
    for t in range(n_shards):
        value_ref[t] = packed_ref[t, 0, 2 * HEAD_DIM : 3 * HEAD_DIM, :].T
    tiles = [(t, c) for t in range(n_shards) for c in range(0, seq, q_block)]
    buffers = (grad_a, grad_b)

    def start(tile, ref):
        t, c = tile
        ref[...] = mm(value_ref[t], ctx_low_ref[t, 0, :, c : c + q_block])

    def finish(tile, ref):
        t, c = tile
        cols = slice(c, c + q_block)
        probs_low = probs_ref[t, 0, 0, :, cols]
        probs = probs_low.astype(f32)
        weighted = probs * ref[...]
        total = jnp.sum(weighted, axis=0, keepdims=True)
        score_low = (weighted - probs * total).astype(bf16)
        grad_query = mm(packed_ref[t, 0, HEAD_DIM : 2 * HEAD_DIM, :], score_low) * scale
        grad_ref[t, 0, :HEAD_DIM, cols] = grad_query.astype(bf16)
        grad_key = mm_nt(packed_ref[t, 0, :HEAD_DIM, cols], score_low)
        grad_value = mm_nt(ctx_low_ref[t, 0, :, cols], probs_low)
        if c > 0:
            grad_key = key_acc[...] + grad_key
            grad_value = value_acc[...] + grad_value
        if c + q_block < seq:
            key_acc[...] = grad_key
            value_acc[...] = grad_value
        else:
            grad_ref[t, 0, HEAD_DIM : 2 * HEAD_DIM, :] = (grad_key * scale).astype(bf16)
            grad_ref[t, 0, 2 * HEAD_DIM :, :] = grad_value.astype(bf16)

    start(tiles[0], buffers[0])
    for j, tile in enumerate(tiles):
        if j + 1 < len(tiles):
            start(tiles[j + 1], buffers[(j + 1) % 2])
        finish(tile, buffers[j % 2])

    @pl.when(step == 0)
    def _():
        weight_acc[...] = jnp.zeros_like(weight_acc)
        bias_ref[...] = sums_ref[...]

    ones = jnp.ones((8, seq), bf16)
    for t in range(n_shards):
        weight_acc[t] += mm(grad_ref[t, 0], x_ref[...])
        bias_ref[t, head : head + 1] += mm_nt(ones, grad_ref[t, 0])[:1]

    @pl.when(step == pl.num_programs(0) - 1)
    def _():
        low = lax.rem(pos_ref[0], slots)
        half = slots // 2
        rows = PART_ROWS // slots
        for slot, bits in enumerate(HEAD_BITS[slots]):
            at = lax.bitwise_xor(low, bits)
            ref = keep_ref if slot < half else send_ref
            for t in range(n_shards):
                ref[t, slot % half, :rows] = weight_acc[t, aligned(at, rows, 8), :].astype(bf16)
                if extra:
                    padded = jnp.concatenate(
                        [bias_ref[t], jnp.zeros((EXTRA, ref.shape[3] - PART_ROWS), f32)], axis=1
                    )
                    ref[t, slot % half, rows:] = padded.astype(bf16)


def attn_bwd(pos, x, packed, probs, ctx_low, sums, head, first, group, slots, extra, earlier):
    rows, width = x.shape
    n_shards, n_seq = packed.shape[:2]
    q_block = 256
    each = PART_ROWS // slots + (EXTRA if extra else 0)
    pieces = (n_shards, slots // 2, group * each, width)
    piece = pl.BlockSpec((n_shards, slots // 2, each, width), lambda s, pos: (0, 0, head - first, 0))
    sum_spec = pl.BlockSpec(sums.shape, lambda s, pos: (0, 0, 0))
    return pl.pallas_call(
        partial(attn_bwd_kernel, head=head, slots=slots, extra=extra, q_block=q_block),
        grid_spec=pltpu.PrefetchScalarGridSpec(
            num_scalar_prefetch=1,
            grid=(n_seq,),
            in_specs=[
                pl.BlockSpec((SEQ_LEN, width), lambda s, pos: (s, 0)),
                pl.BlockSpec((n_shards, 1, PART_ROWS, SEQ_LEN), lambda s, pos: (0, s, head, 0)),
                pl.BlockSpec((n_shards, 1, 1, SEQ_LEN, SEQ_LEN), lambda s, pos: (0, s, head, 0, 0)),
                pl.BlockSpec((n_shards, 1, HEAD_DIM, SEQ_LEN), lambda s, pos: (0, s, head, 0)),
                sum_spec,
            ]
            + [pl.BlockSpec(memory_space=pl.ANY)] * len(earlier),
            out_specs=[
                pl.BlockSpec((n_shards, 1, PART_ROWS, SEQ_LEN), lambda s, pos: (0, s, 0, 0)),
                piece,
                piece,
                sum_spec,
            ],
            scratch_shapes=[
                pltpu.VMEM((n_shards, SEQ_LEN, HEAD_DIM), bf16),
                pltpu.VMEM((HEAD_DIM, SEQ_LEN), f32),
                pltpu.VMEM((HEAD_DIM, SEQ_LEN), f32),
                pltpu.VMEM((n_shards, PART_ROWS, width), f32),
                pltpu.VMEM((SEQ_LEN, q_block), f32),
                pltpu.VMEM((SEQ_LEN, q_block), f32),
            ],
        ),
        out_shape=[
            jax.ShapeDtypeStruct((n_shards, n_seq, PART_ROWS, SEQ_LEN), bf16),
            jax.ShapeDtypeStruct(pieces, bf16),
            jax.ShapeDtypeStruct(pieces, bf16),
            jax.ShapeDtypeStruct(sums.shape, f32),
        ],
        input_output_aliases={6: 1, 7: 2} if earlier else {},
        compiler_params=kernel_params(48_000_000),
        cost_estimate=cost(8 << 30, 10 << 20),
        name="attn_bwd",
    )(pos, x, packed, probs, ctx_low, sums, *earlier)


def input_grad_kernel(pos_ref, grad_one_ref, own_ref, *refs, n_others):
    fetched, grads, out_ref, got_ref = refs[: 2 * n_others], refs[2 * n_others : -2], refs[-2], refs[-1]
    half = own_ref.shape[0] // 2

    @pl.when(pl.program_id(0) == 0)
    def _():
        parity = lax.rem(pos_ref[0], 2)
        for t in range(n_others):
            for k in range(2):
                side = parity if k == 0 else 1 - parity
                got_ref[t, aligned(side, half, half), :] = fetched[2 * t + k][:half]

    total = grad_one_ref[...]
    for t in range(n_others + 1):
        weight = own_ref if t == 0 else got_ref.at[t - 1]
        for head, ref in enumerate(grads):
            total = total + mm_tn(ref[t, 0], weight[head * PART_ROWS : (head + 1) * PART_ROWS, :])
    out_ref[...] = total.astype(bf16)


def input_gradient(pos, grad_one, own, fetched, packed_grads):
    rows, width = grad_one.shape
    n_shards = packed_grads[0].shape[0]
    block = 512
    per_seq = SEQ_LEN // block
    row = pl.BlockSpec((block, width), lambda i, pos: (i, 0))
    cols = pl.BlockSpec((n_shards, 1, PART_ROWS, block), lambda i, pos: (0, i // per_seq, 0, i % per_seq))

    def whole(array):
        return pl.BlockSpec(array.shape, lambda i, pos: (0, 0), pipeline_mode=pl.Buffered(1))

    return pl.pallas_call(
        partial(input_grad_kernel, n_others=n_shards - 1),
        grid_spec=pltpu.PrefetchScalarGridSpec(
            num_scalar_prefetch=1,
            grid=(rows // block,),
            in_specs=[row, whole(own)] + [whole(v) for v in fetched] + [cols] * len(packed_grads),
            out_specs=row,
            scratch_shapes=[pltpu.VMEM((n_shards - 1,) + own.shape, bf16)],
        ),
        out_shape=jax.ShapeDtypeStruct((rows, width), bf16),
        compiler_params=kernel_params(48_000_000),
        cost_estimate=cost(4 << 30, 12 << 20),
        name="input_gradient",
    )(pos, grad_one, own, *fetched, *packed_grads)


def mlp_place_kernel(pos_ref, dn_near, dn_far, up_near, up_far, proj_out, up_out, dn_out):
    low = lax.rem(pos_ref[0], MLP_SLOTS)
    half = MLP_SLOTS // 2
    width = proj_out.shape[1]
    hidden = dn_out.shape[0]
    dn_rows, up_rows, proj_rows = hidden // MLP_SLOTS, width // MLP_SLOTS, proj_out.shape[0] // MLP_SLOTS
    for slot in range(MLP_SLOTS):
        dn_ref = dn_near if slot < half else dn_far
        up_ref = up_near if slot < half else up_far
        k = slot % half
        at = lax.bitwise_xor(low, DOWN_BITS[slot])
        dn_out[aligned(at, dn_rows, dn_rows), :] = dn_ref[k, :dn_rows].astype(f32)
        proj_out[aligned(at, proj_rows, proj_rows), :] = dn_ref[k, dn_rows:].astype(f32)
        rows = aligned(lax.bitwise_xor(low, UP_BITS[slot]), up_rows, up_rows)
        for j in range(hidden // width):
            up_out[rows, j * width : (j + 1) * width] = up_ref[k, j * up_rows : (j + 1) * up_rows].astype(f32)


def mlp_place(pos, dn_parts, up_parts, ctx_rows, width, hidden):
    return pl.pallas_call(
        mlp_place_kernel,
        in_specs=[pl.BlockSpec(memory_space=pltpu.SMEM)] + [in_vmem()] * 4,
        out_specs=[in_vmem()] * 3,
        out_shape=[
            jax.ShapeDtypeStruct((ctx_rows, width), f32),
            jax.ShapeDtypeStruct((width, hidden), f32),
            jax.ShapeDtypeStruct((hidden, width), f32),
        ],
        compiler_params=kernel_params(48_000_000),
        cost_estimate=cost(0, 14 << 20),
        name="mlp_place",
    )(pos, *dn_parts, *up_parts)


def qkv_place_kernel(pos_ref, *refs, groups):
    out_ref = refs[-1]
    for g, (first, group, slots, each) in enumerate(groups):
        half = slots // 2
        rows = PART_ROWS // slots
        low = lax.rem(pos_ref[0], slots)
        for slot, bits in enumerate(HEAD_BITS[slots]):
            at = aligned(lax.bitwise_xor(low, bits), rows, 8)
            for k in range(group):
                value = refs[2 * g + slot // half][slot % half, k * each : k * each + rows]
                out_ref[first + k, at, :] = value.astype(f32)


def qkv_place(pos, parts, groups, heads):
    flat = [half for pair in parts for half in pair]
    return pl.pallas_call(
        partial(qkv_place_kernel, groups=groups),
        in_specs=[pl.BlockSpec(memory_space=pltpu.SMEM)] + [in_vmem()] * len(flat),
        out_specs=in_vmem(),
        out_shape=jax.ShapeDtypeStruct((heads, PART_ROWS, flat[0].shape[2]), f32),
        compiler_params=kernel_params(48_000_000),
        cost_estimate=cost(0, 3 << 20),
        name="qkv_place",
    )(pos, *flat)


def swap_dp(value, bits, n_dp):
    return lax.ppermute(value, "dp", [(i, i ^ bits) for i in range(n_dp)])


def shift_tensor(value, by, n_tensor):
    return lax.ppermute(value, "tensor", [((i + by) % n_tensor, i) for i in range(n_tensor)])


def reduce_pieces(keep, send, order, n_dp, n_tensor):
    halved = [axis for axis in order if axis != "tensor"]
    got = swap_dp(send, 1, n_dp)
    got = after(got, (yield send))
    parts = [keep[t].astype(f32) + got[t].astype(f32) for t in range(n_tensor)]
    for axis in order:
        if axis == "tensor":
            outs = [parts[by].astype(bf16) for by in range(1, n_tensor)]
            gots = [shift_tensor(out, -by, n_tensor) for by, out in enumerate(outs, 1)]
            gots = after(gots, (yield outs))
            parts = [sum((got.astype(f32) for got in gots), parts[0])]
        else:
            cut = parts[0].shape[0] // 2
            out = jnp.stack([part[cut:].astype(bf16) for part in parts])
            got = swap_dp(out, axis, n_dp)
            got = after(got, (yield out))
            parts = [part[:cut] + got[t].astype(f32) for t, part in enumerate(parts)]
    own = parts[0]
    bits = 2
    while bits < n_dp:
        if bits not in halved:
            out = own.astype(bf16)
            got = swap_dp(out, bits, n_dp)
            got = after(got, (yield out))
            own = own + got.astype(f32)
        bits *= 2
    near = own.astype(bf16)
    for axis in reversed(halved):
        got = swap_dp(near, axis, n_dp)
        got = after(got, (yield near))
        near = jnp.concatenate([near, got], axis=0)
    got = swap_dp(near, 1, n_dp)
    got = after(got, (yield near))
    return near, got, own


class Sums:
    def __init__(self):
        self.live, self.done, self.fresh = {}, {}, set()

    def add(self, name, generator):
        self.live[name] = generator
        self.fresh.add(name)

    def step(self, ready, *names):
        sent = []
        for name in names:
            if name in self.live:
                try:
                    sent.append(self.live[name].send(None if name in self.fresh else ready))
                    self.fresh.discard(name)
                except StopIteration as stop:
                    self.done[name] = stop.value
                    del self.live[name]
        return sent

    def finish(self):
        while self.live:
            self.step((), *list(self.live))


def after(value, *others):
    return lax.optimization_barrier((value, others))[0]


def sequence_body(n_dp, n_tensor, *arrays):
    (
        layer_input,
        output_grad,
        qkv_weight,
        query_bias,
        value_bias,
        proj_weight,
        proj_bias,
        first_gain,
        first_shift,
        up_weight,
        up_bias,
        down_weight,
        down_bias,
        second_gain,
        second_shift,
    ) = arrays
    rows, width = layer_input.shape
    n_seq = rows // SEQ_LEN
    ctx_rows, hidden = proj_weight.shape[0], up_weight.shape[1]
    n_heads = ctx_rows // HEAD_DIM
    pos = lax.axis_index("dp").astype(jnp.int32).reshape(1)
    shifts = range(1, n_tensor)

    qkv_half, own_bias = pack_qkv(pos, qkv_weight, query_bias, value_bias)
    qkv_near = [shift_tensor(qkv_half, by, n_tensor) for by in shifts]
    vectors = [proj_bias, first_gain, first_shift, down_bias, second_gain, second_shift]
    mlp_half, vecs = pack_mlp(after(pos, qkv_half), proj_weight, down_weight, up_weight, up_bias, vectors)
    shapes = [
        jax.ShapeDtypeStruct((n_tensor, n_seq, n_heads * PART_ROWS, SEQ_LEN), bf16),
        jax.ShapeDtypeStruct((n_tensor, n_seq, n_heads, SEQ_LEN, SEQ_LEN), bf16),
        jax.ShapeDtypeStruct((n_tensor, n_seq, n_heads * HEAD_DIM, SEQ_LEN), bf16),
    ]
    mlp_near = [shift_tensor(mlp_half, by, n_tensor) for by in shifts]
    x = after(layer_input, mlp_half)
    stacks = attn_fwd(pos, x, qkv_weight, own_bias, 0, (0, 1), shapes, ())
    qkv_far = [swap_dp(near, 1, n_dp) for near in qkv_near]
    for t in shifts:
        for k, buffer in enumerate((qkv_near[t - 1], qkv_far[t - 1])):
            stacks = attn_fwd(pos, layer_input, buffer, buffer, t, (k,), shapes, stacks)
    packed, probs, ctx = stacks
    mlp_near = after(mlp_near, ctx)
    mlp_far = [swap_dp(near, 1, n_dp) for near in mlp_near]
    fetched = [half for pair in zip(mlp_near, mlp_far) for half in pair]
    result, grad_one, ctx_low, dn_keep, dn_send, up_keep, up_send = middle(
        pos, layer_input, output_grad, ctx, vecs, proj_weight, up_weight, down_weight, fetched
    )
    sums = Sums()
    sums.add("dn", reduce_pieces(dn_keep, dn_send, DOWN_ORDER, n_dp, n_tensor))
    sums.add("up", reduce_pieces(up_keep, up_send, UP_ORDER, n_dp, n_tensor))
    bias_sums = jnp.zeros((n_tensor, EXTRA, PART_ROWS), f32)
    packed_grads = []
    ready = ()
    early = n_heads - 1
    stacked = ()
    for head in range(n_heads):
        last = head == early
        if last and early:
            sums.add("qa", reduce_pieces(*stacked, ("tensor", 2), n_dp, n_tensor))
        sent = sums.step(ready, *SCHEDULE[min(head, len(SCHEDULE) - 3)])
        x = after(layer_input, sent)
        grads, keep, send, bias_sums = attn_bwd(
            pos,
            x,
            packed,
            probs,
            ctx_low,
            bias_sums,
            head,
            early if last else 0,
            1 if last else early,
            2 if last else 4,
            last,
            () if last else stacked,
        )
        ready = bias_sums
        packed_grads.append(grads)
        if not last:
            stacked = (keep, send)
    sums.add("qb", reduce_pieces(keep, send, ("tensor",), n_dp, n_tensor))
    sent = sums.step(ready, *SCHEDULE[-2])
    qkv_fetched = [half for pair in zip(qkv_near, qkv_far) for half in pair]
    input_grad = input_gradient(pos, after(grad_one, sent), qkv_weight, qkv_fetched, packed_grads)
    sums.step(input_grad, *SCHEDULE[-1])
    sums.finish()
    dn_near, dn_far, _ = sums.done["dn"]
    up_near, up_far, up_own = sums.done["up"]
    proj_wg, up_wg, dn_wg = mlp_place(pos, (dn_near, dn_far), (up_near, up_far), ctx_rows, width, hidden)
    groups = [(0, early, 4, PART_ROWS // 4)] if early else []
    groups.append((early, 1, 2, PART_ROWS // 2 + EXTRA))
    parts = [sums.done[name][:2] for name in ("qa", "qb") if name in sums.done]
    qkv_wg = qkv_place(pos, parts, groups, n_heads)
    small = up_own[0, -EXTRA:]
    bias = sums.done["qb"][2][0, -EXTRA:][:n_heads, :PART_ROWS]
    return (
        result,
        input_grad,
        qkv_wg.reshape(n_heads * PART_ROWS, width),
        bias[:, :HEAD_DIM].reshape(ctx_rows),
        bias[:, 2 * HEAD_DIM :].reshape(ctx_rows),
        proj_wg,
        small[0],
        small[1],
        small[2],
        up_wg,
        small[8 : 8 + hidden // width].reshape(hidden),
        dn_wg,
        small[3],
        small[4],
        small[5],
    )


SCHEDULE = (
    ("dn", "up"),
    ("dn", "up"),
    ("dn", "up"),
    ("dn", "up", "qa"),
    ("dn", "up", "qa", "qb"),
    ("dn", "up", "qa", "qb"),
)


def solution(mesh):
    n_dp, n_tensor = mesh.shape["dp"], mesh.shape["tensor"]

    def body(*arrays):
        rows = arrays[0].shape[0]
        if rows % SEQ_LEN == 0 and n_dp % 8 == 0 and n_dp & (n_dp - 1) == 0:
            return sequence_body(n_dp, n_tensor, *arrays)
        return token_body(*arrays)

    return jax.shard_map(
        body,
        mesh=mesh,
        in_specs=(
            P(("dp", "tensor"), None),
            P(("dp", "tensor"), None),
            P("tensor", None),
            P("tensor"),
            P("tensor"),
            P("tensor", None),
            P(),
            P(),
            P(),
            P(None, "tensor"),
            P("tensor"),
            P("tensor", None),
            P(),
            P(),
            P(),
        ),
        out_specs=(
            P(("dp", "tensor"), None),
            P(("dp", "tensor"), None),
            P("tensor", None),
            P("tensor"),
            P("tensor"),
            P("tensor", None),
            P(),
            P(),
            P(),
            P(None, "tensor"),
            P("tensor"),
            P("tensor", None),
            P(),
            P(),
            P(),
        ),
        check_vma=False,
    )
```

```python
from functools import partial

import jax
import jax.numpy as jnp
from jax import lax
from jax.experimental import pallas as pl
from jax.experimental.pallas import tpu as pltpu
from jax.sharding import PartitionSpec as P

HEAD_DIM = 64
SEQ_LEN = 1024
PART_ROWS = 3 * HEAD_DIM

norm_eps = 1e-05
f32 = jnp.float32
bf16 = jnp.bfloat16


def matmul_rows(left, right):
    return lax.dot_general(
        left, right, (((0,), (0,)), ((), ())), preferred_element_type=jnp.float32
    )


def matmul_back(left, right):
    return lax.dot_general(
        left, right, (((1,), (1,)), ((), ())), preferred_element_type=jnp.float32
    )


def attend_forward(queries, key_rows, value_rows):
    seq_heads = key_rows.shape[0] * key_rows.shape[1]
    head_dim = queries.shape[-1]
    score_scale = head_dim ** (-0.5)
    block_rows = min(512, SEQ_LEN)
    block_count = SEQ_LEN // block_rows
    item_count = seq_heads * block_count
    query_items = queries.reshape(item_count, block_rows, head_dim)
    key_all = key_rows.reshape(seq_heads, SEQ_LEN, head_dim)
    value_all = value_rows.reshape(seq_heads, SEQ_LEN, head_dim)

    def one_block(block_item):
        query_blk, position = block_item
        owner_index = position // block_count
        keys_here = key_all[owner_index]
        values_here = value_all[owner_index]
        scores = matmul_back(query_blk, keys_here) * score_scale
        row_top = jnp.max(scores, axis=-1, keepdims=True)
        exponent = jnp.exp(scores - row_top)
        row_total = jnp.sum(exponent, axis=-1, keepdims=True)
        weights_now = exponent / row_total
        mixed_rows = jnp.dot(
            weights_now.astype(jnp.bfloat16), values_here, preferred_element_type=jnp.float32
        )
        return (mixed_rows, row_top[:, 0] + jnp.log(row_total[:, 0]))

    mixed_rows, log_total = lax.map(
        one_block, (query_items, jnp.arange(item_count, dtype=jnp.int32))
    )
    return (mixed_rows.reshape(queries.shape), log_total.reshape(queries.shape[:-1]))


def attend_backward(queries, key_rows, value_rows, log_total, context_low):
    seq_heads = key_rows.shape[0] * key_rows.shape[1]
    head_dim = queries.shape[-1]
    score_scale = head_dim ** (-0.5)
    block_rows = min(512, SEQ_LEN)
    block_count = SEQ_LEN // block_rows
    item_count = seq_heads * block_count
    query_items = queries.reshape(item_count, block_rows, head_dim)
    total_items = log_total.reshape(item_count, block_rows)
    grad_items = context_low.reshape(item_count, block_rows, head_dim)
    key_all = key_rows.reshape(seq_heads, SEQ_LEN, head_dim)
    value_all = value_rows.reshape(seq_heads, SEQ_LEN, head_dim)

    def one_block(block_item):
        query_blk, total_blk, grad_blk, position = block_item
        owner_index = position // block_count
        keys_here = key_all[owner_index]
        values_here = value_all[owner_index]
        scores = matmul_back(query_blk, keys_here) * score_scale
        weights_now = jnp.exp(scores - total_blk[:, None])
        grad_weights = matmul_back(grad_blk, values_here)
        grad_scores = weights_now * (
            grad_weights - jnp.sum(weights_now * grad_weights, axis=-1, keepdims=True)
        )
        score_low = grad_scores.astype(jnp.bfloat16)
        grad_query = jnp.dot(score_low, keys_here, preferred_element_type=jnp.float32) * score_scale
        grad_key = matmul_rows(score_low, query_blk) * score_scale
        grad_value = matmul_rows(weights_now.astype(jnp.bfloat16), grad_blk)
        return (grad_query, grad_key, grad_value)

    grad_query, grad_key, grad_value = lax.map(
        one_block, (query_items, total_items, grad_items, jnp.arange(item_count, dtype=jnp.int32))
    )
    grad_key = jnp.sum(grad_key.reshape(seq_heads, block_count, SEQ_LEN, head_dim), axis=1)
    grad_value = jnp.sum(grad_value.reshape(seq_heads, block_count, SEQ_LEN, head_dim), axis=1)
    return (
        grad_query.reshape(queries.shape),
        grad_key.reshape(key_rows.shape),
        grad_value.reshape(value_rows.shape),
    )


def norm_forward(hidden, gain_vec, shift_vec):
    center = jnp.mean(hidden, axis=-1)
    second = jnp.mean(hidden * hidden, axis=-1) - center * center
    inv_std = lax.rsqrt(second + norm_eps)
    normal = (hidden - center[:, None]) * inv_std[:, None]
    return (normal * gain_vec + shift_vec, normal, inv_std)


def norm_backward(upstream, normal, inv_std, gain_vec):
    scaled = upstream * gain_vec
    first_mean = jnp.mean(scaled, axis=-1)
    second_mean = jnp.mean(scaled * normal, axis=-1)
    grad_in = inv_std[:, None] * (scaled - first_mean[:, None] - normal * second_mean[:, None])
    return (grad_in, jnp.sum(upstream * normal, axis=0), jnp.sum(upstream, axis=0))


def rows_in(value):
    return lax.all_gather(value, "tensor", axis=0, tiled=True)


def part_out(value):
    return lax.psum_scatter(value, "tensor", scatter_dimension=0, tiled=True)


def gather_grad(value):
    return lax.all_gather(value, "tensor", axis=0, tiled=True)


def part_back(value):
    return lax.psum_scatter(value, "tensor", scatter_dimension=0, tiled=True)


def token_body(
    layer_input,
    output_grad,
    qkv_weight,
    query_bias,
    value_bias,
    proj_weight,
    proj_bias,
    first_gain,
    first_shift,
    up_weight,
    up_bias,
    down_weight,
    down_bias,
    second_gain,
    second_shift,
):
    heads_here = query_bias.shape[0] // HEAD_DIM
    query_bf = query_bias.astype(jnp.float32).reshape(heads_here, HEAD_DIM)
    value_bf = value_bias.astype(jnp.float32).reshape(heads_here, HEAD_DIM)
    bias_rows = jnp.stack([query_bf, jnp.zeros_like(query_bf), value_bf], axis=1)
    gain_one = first_gain.astype(jnp.float32)
    shift_one = first_shift.astype(jnp.float32)
    gain_two = second_gain.astype(jnp.float32)
    shift_two = second_shift.astype(jnp.float32)
    input_full = rows_in(layer_input)
    row_count = input_full.shape[0]
    seq_count = row_count // SEQ_LEN
    projected = matmul_back(input_full, qkv_weight).reshape(row_count, heads_here, 3, HEAD_DIM)
    packed = (projected + bias_rows).astype(jnp.bfloat16)
    parts = packed.reshape(seq_count, SEQ_LEN, heads_here, 3, HEAD_DIM).transpose(3, 0, 2, 1, 4)
    queries, key_rows, value_rows = (parts[0], parts[1], parts[2])
    mixed_rows, log_total = attend_forward(queries, key_rows, value_rows)
    context = (
        mixed_rows.transpose(0, 2, 1, 3)
        .reshape(row_count, heads_here * HEAD_DIM)
        .astype(jnp.bfloat16)
    )
    partial_branch = jnp.dot(context, proj_weight, preferred_element_type=jnp.float32)
    branch = part_out(partial_branch) + proj_bias.astype(jnp.float32)
    normed_one, normal_one, inv_one = norm_forward(
        layer_input.astype(jnp.float32) + branch, gain_one, shift_one
    )
    normed_full = rows_in(normed_one.astype(jnp.bfloat16))
    inner_pre = jnp.dot(
        normed_full, up_weight, preferred_element_type=jnp.float32
    ) + up_bias.astype(jnp.float32)
    active, gelu_back = jax.vjp(partial(jax.nn.gelu, approximate=False), inner_pre)
    active_low = active.astype(jnp.bfloat16)
    second = part_out(
        jnp.dot(active_low, down_weight, preferred_element_type=jnp.float32)
    ) + down_bias.astype(jnp.float32)
    result_rows, normal_two, inv_two = norm_forward(normed_one + second, gain_two, shift_two)
    upstream = output_grad.astype(jnp.float32)
    grad_two, gain_two_grad, shift_two_grad = norm_backward(upstream, normal_two, inv_two, gain_two)
    second_low = grad_two.astype(jnp.bfloat16)
    down_b_grad = jnp.sum(second_low.astype(jnp.float32), axis=0)
    second_full = gather_grad(second_low)
    down_w_grad = matmul_rows(active_low, second_full)
    grad_active = matmul_back(second_full, down_weight)
    inner_low = gelu_back(grad_active)[0].astype(jnp.bfloat16)
    up_b_grad = jnp.sum(inner_low.astype(jnp.float32), axis=0)
    up_w_grad = matmul_rows(normed_full, inner_low)
    grad_mid = grad_two + part_back(matmul_back(inner_low, up_weight))
    grad_one, gain_one_grad, shift_one_grad = norm_backward(grad_mid, normal_one, inv_one, gain_one)
    branch_low = grad_one.astype(jnp.bfloat16)
    proj_b_grad = jnp.sum(branch_low.astype(jnp.float32), axis=0)
    branch_full = gather_grad(branch_low)
    proj_w_grad = matmul_rows(context, branch_full)
    context_low = matmul_back(branch_full, proj_weight).astype(jnp.bfloat16)
    context_low = context_low.reshape(seq_count, SEQ_LEN, heads_here, HEAD_DIM).transpose(
        0, 2, 1, 3
    )
    grad_query, grad_key, grad_value = attend_backward(
        queries, key_rows, value_rows, log_total, context_low
    )
    packed_low = jnp.stack([grad_query, grad_key, grad_value], axis=0).transpose(1, 3, 2, 0, 4)
    packed_low = packed_low.reshape(row_count, heads_here * 3 * HEAD_DIM).astype(jnp.bfloat16)
    packed_sums = jnp.sum(packed_low.astype(jnp.float32), axis=0).reshape(heads_here, 3, HEAD_DIM)
    query_b_grad = packed_sums[:, 0].reshape(heads_here * HEAD_DIM)
    value_b_grad = packed_sums[:, 2].reshape(heads_here * HEAD_DIM)
    qkv_w_grad = matmul_rows(packed_low, input_full)
    input_grad = (
        grad_one + part_back(jnp.dot(packed_low, qkv_weight, preferred_element_type=jnp.float32))
    ).astype(jnp.bfloat16)
    totals = (
        lax.psum(qkv_w_grad.astype(jnp.bfloat16), "dp").astype(jnp.float32),
        lax.psum(query_b_grad.astype(jnp.bfloat16), "dp").astype(jnp.float32),
        lax.psum(value_b_grad.astype(jnp.bfloat16), "dp").astype(jnp.float32),
        lax.psum(proj_w_grad.astype(jnp.bfloat16), "dp").astype(jnp.float32),
        lax.psum(up_w_grad.astype(jnp.bfloat16), "dp").astype(jnp.float32),
        lax.psum(up_b_grad.astype(jnp.bfloat16), "dp").astype(jnp.float32),
        lax.psum(down_w_grad.astype(jnp.bfloat16), "dp").astype(jnp.float32),
    )
    vectors = lax.psum(
        (proj_b_grad, gain_one_grad, shift_one_grad, down_b_grad, gain_two_grad, shift_two_grad),
        ("dp", "tensor"),
    )
    return (
        result_rows.astype(jnp.bfloat16),
        input_grad,
        totals[0],
        totals[1],
        totals[2],
        totals[3],
        vectors[0],
        vectors[1],
        vectors[2],
        totals[4],
        totals[5],
        totals[6],
        vectors[3],
        vectors[4],
        vectors[5],
    )


VMEM_LIMIT = 66_000_000
EXTRA = 16


def mm(left, right):
    return lax.dot_general(left, right, (((1,), (0,)), ((), ())), preferred_element_type=f32)


def mm_nt(left, right):
    return lax.dot_general(left, right, (((1,), (1,)), ((), ())), preferred_element_type=f32)


def mm_tn(left, right):
    return lax.dot_general(left, right, (((0,), (0,)), ((), ())), preferred_element_type=f32)


def kernel_params(limit=VMEM_LIMIT):
    return pltpu.CompilerParams(vmem_limit_bytes=limit)


def cost(flops, size):
    return pl.CostEstimate(flops=int(flops), bytes_accessed=int(size), transcendentals=0)


def in_vmem():
    return pl.BlockSpec(memory_space=pltpu.VMEM)


def aligned(start, size, by):
    return pl.ds(pl.multiple_of(start * size, by), size)


def pack_qkv_kernel(pos_ref, weight_ref, query_b_ref, value_b_ref, packed_ref, own_b_ref):
    half = weight_ref.shape[0]
    wide = query_b_ref.shape[0] // 2
    query_b, value_b = (ref[...].reshape(1, 2 * wide) for ref in (query_b_ref, value_b_ref))
    packed_ref[:half] = weight_ref[...]
    packed_ref[half:] = jnp.zeros_like(packed_ref[half:])
    own_b_ref[...] = jnp.zeros_like(own_b_ref)
    parity = lax.rem(pos_ref[0], 2)
    for k in range(2):
        cols = slice(k * wide, (k + 1) * wide)
        own_b_ref[k * EXTRA : k * EXTRA + 1, :wide] = query_b[:, cols]
        own_b_ref[k * EXTRA : k * EXTRA + 1, wide : 2 * wide] = value_b[:, cols]

        @pl.when(parity == k)
        def _():
            packed_ref[half : half + 1, :wide] = query_b[:, cols]
            packed_ref[half : half + 1, wide : 2 * wide] = value_b[:, cols]


def pack_qkv(pos, weight, query_b, value_b):
    rows, width = weight.shape
    half = rows // 2
    small = pl.BlockSpec(query_b.shape, lambda i, pos: (0,))
    return pl.pallas_call(
        pack_qkv_kernel,
        grid_spec=pltpu.PrefetchScalarGridSpec(
            num_scalar_prefetch=1,
            grid=(1,),
            in_specs=[pl.BlockSpec((half, width), lambda i, pos: (lax.rem(pos[0], 2), 0)), small, small],
            out_specs=[
                pl.BlockSpec((half + EXTRA, width), lambda i, pos: (0, 0)),
                pl.BlockSpec((2 * EXTRA, width), lambda i, pos: (0, 0)),
            ],
        ),
        out_shape=[
            jax.ShapeDtypeStruct((half + EXTRA, width), bf16),
            jax.ShapeDtypeStruct((2 * EXTRA, width), bf16),
        ],
        compiler_params=kernel_params(),
        cost_estimate=cost(0, 1 << 20),
        name="pack_qkv",
    )(pos, weight, query_b, value_b)


def pack_mlp_kernel(pos_ref, proj_ref, down_ref, up_ref, up_b_ref, *refs):
    vec_refs, packed_ref, vecs_ref = refs[:-2], refs[-2], refs[-1]
    width = proj_ref.shape[1]
    at = 0
    for value in (proj_ref[...], down_ref[...]):
        packed_ref[at : at + value.shape[0]] = value
        at += value.shape[0]
    blocks = up_ref.shape[1] // width
    for j in range(blocks):
        packed_ref[at : at + up_ref.shape[0]] = up_ref[:, j * width : (j + 1) * width]
        at += up_ref.shape[0]
    packed_ref[at:] = jnp.zeros_like(packed_ref[at:])
    vecs_ref[...] = jnp.zeros_like(vecs_ref)
    for j in range(blocks):
        row = up_b_ref[j * width : (j + 1) * width].reshape(1, width)
        packed_ref[at + j : at + j + 1] = row
        vecs_ref[8 + j : 9 + j] = row.astype(f32)
    for k, ref in enumerate(vec_refs):
        vecs_ref[k : k + 1] = ref[...].reshape(1, width).astype(f32)


def pack_mlp(pos, proj, down, up, up_b, vectors):
    width, hidden = up.shape
    rows = (proj.shape[0] + 2 * hidden) // 2 + EXTRA

    def half(array):
        return pl.BlockSpec((array.shape[0] // 2, array.shape[1]), lambda i, pos: (lax.rem(pos[0], 2), 0))

    def whole(array):
        return pl.BlockSpec(array.shape, lambda i, pos: (0,))

    return pl.pallas_call(
        pack_mlp_kernel,
        grid_spec=pltpu.PrefetchScalarGridSpec(
            num_scalar_prefetch=1,
            grid=(1,),
            in_specs=[half(proj), half(down), half(up), whole(up_b)] + [whole(v) for v in vectors],
            out_specs=[
                pl.BlockSpec((rows, width), lambda i, pos: (0, 0)),
                pl.BlockSpec((EXTRA, width), lambda i, pos: (0, 0)),
            ],
        ),
        out_shape=[jax.ShapeDtypeStruct((rows, width), bf16), jax.ShapeDtypeStruct((EXTRA, width), f32)],
        compiler_params=kernel_params(),
        cost_estimate=cost(0, 3 << 20),
        name="pack_mlp",
    )(pos, proj, down, up, up_b, *vectors)


def attn_fwd_kernel(pos_ref, x_ref, *refs, heads, q_block, fetched):
    packed_ref, probs_ref, ctx_ref, key_ref, score_a, score_b = refs[-6:]
    seq = x_ref.shape[0]
    scale = HEAD_DIM**-0.5
    wide = heads * HEAD_DIM
    part = heads * PART_ROWS
    if fetched:
        near = pl.program_id(1) == 0
        weight = jnp.where(near, refs[0][:part], refs[1][:part])
        bias = jnp.where(near, refs[0][part:].astype(f32), refs[1][part:].astype(f32))
    else:
        weight, bias = refs[0][...], refs[1][...].astype(f32)
    column = bias[:8, : 2 * wide].T
    raw = mm_nt(weight, x_ref[...])
    for h in range(heads):
        base = h * PART_ROWS
        ends = (base + HEAD_DIM, base + 2 * HEAD_DIM, base + PART_ROWS)
        query = raw[base : ends[0]] + column[h * HEAD_DIM : (h + 1) * HEAD_DIM, :1]
        value = raw[ends[1] : ends[2]] + column[wide + h * HEAD_DIM : wide + (h + 1) * HEAD_DIM, :1]
        packed_ref[0, 0, base : ends[0]] = query.astype(bf16)
        packed_ref[0, 0, ends[0] : ends[1]] = raw[ends[0] : ends[1]].astype(bf16)
        packed_ref[0, 0, ends[1] : ends[2]] = value.astype(bf16)
        keys = packed_ref[0, 0, ends[0] : ends[1], :].astype(f32)
        key_ref[h] = (keys.T * scale).astype(bf16)
    tiles = [(h, c) for h in range(heads) for c in range(0, seq, q_block)]
    scores = (score_a, score_b)

    def score(tile, ref):
        h, c = tile
        base = h * PART_ROWS
        ref[...] = mm(key_ref[h], packed_ref[0, 0, base : base + HEAD_DIM, c : c + q_block])

    def finish(tile, ref):
        h, c = tile
        base = h * PART_ROWS
        top = jnp.max(ref[...], axis=0, keepdims=True)
        exponent = jnp.exp(ref[...] - top)
        total = jnp.sum(exponent, axis=0, keepdims=True)
        probs = (exponent * (1.0 / total)).astype(bf16)
        probs_ref[0, 0, h, :, c : c + q_block] = probs
        mixed = mm(packed_ref[0, 0, base + 2 * HEAD_DIM : base + 3 * HEAD_DIM, :], probs)
        ctx_ref[0, 0, h * HEAD_DIM : (h + 1) * HEAD_DIM, c : c + q_block] = mixed.astype(bf16)

    score(tiles[0], scores[0])
    for j, tile in enumerate(tiles):
        if j + 1 < len(tiles):
            score(tiles[j + 1], scores[(j + 1) % 2])
        finish(tile, scores[j % 2])


def attn_fwd(pos, x, sources, shard, fetched, shapes, earlier):
    rows, width = x.shape
    n_seq = rows // SEQ_LEN
    heads = shapes[1].shape[2] // 2
    part = heads * PART_ROWS

    def at(k, pos):
        return lax.bitwise_xor(k, lax.rem(pos[0], 2)) if fetched else k

    if fetched:
        sizes = [pl.BlockSpec(v.shape, lambda s, k, pos: (0, 0), pipeline_mode=pl.Buffered(1)) for v in sources]
    else:
        sizes = [pl.BlockSpec((size, width), lambda s, k, pos: (k, 0)) for size in (part, EXTRA)]
    out_specs = [
        pl.BlockSpec((1, 1, part, SEQ_LEN), lambda s, k, pos: (shard, s, at(k, pos), 0)),
        pl.BlockSpec((1, 1, heads, SEQ_LEN, SEQ_LEN), lambda s, k, pos: (shard, s, at(k, pos), 0, 0)),
        pl.BlockSpec((1, 1, heads * HEAD_DIM, SEQ_LEN), lambda s, k, pos: (shard, s, at(k, pos), 0)),
    ]
    q_block = 512
    share = 2 * n_seq * heads
    flops = share * (2 * SEQ_LEN * width * PART_ROWS + 4 * SEQ_LEN * SEQ_LEN * HEAD_DIM * 6)
    return pl.pallas_call(
        partial(attn_fwd_kernel, heads=heads, q_block=q_block, fetched=fetched),
        grid_spec=pltpu.PrefetchScalarGridSpec(
            num_scalar_prefetch=1,
            grid=(n_seq, 2),
            in_specs=[pl.BlockSpec((SEQ_LEN, width), lambda s, k, pos: (s, 0))]
            + sizes
            + [pl.BlockSpec(memory_space=pl.ANY)] * len(earlier),
            out_specs=out_specs,
            scratch_shapes=[
                pltpu.VMEM((heads, SEQ_LEN, HEAD_DIM), bf16),
                pltpu.VMEM((SEQ_LEN, q_block), f32),
                pltpu.VMEM((SEQ_LEN, q_block), f32),
            ],
        ),
        out_shape=shapes,
        input_output_aliases={4: 0, 5: 1, 6: 2} if earlier else {},
        compiler_params=kernel_params(),
        cost_estimate=cost(flops // 8 if fetched else flops, share * 3 << 20),
        name="attn_fwd",
    )(pos, x, *sources, *earlier)


def piece_bits(*order):
    bits = [0]
    for bit in reversed(order):
        bits = bits + [b | bit for b in bits]
    return bits


MLP_SLOTS = 8
DOWN_ORDER = ("tensor", 2, 4)
UP_ORDER = (4, "tensor", 2)
DOWN_BITS = piece_bits(1, 2, 4)
UP_BITS = piece_bits(1, 4, 2)


def middle_kernel(
    pos_ref,
    x_ref,
    og_ref,
    ctx_ref,
    vecs_ref,
    proj_own,
    up_own,
    down_own,
    *refs,
    n_others,
    chunk,
):
    fetched, refs = refs[: 2 * n_others], refs[2 * n_others :]
    out_ref, grad_one_ref, ctx_low_ref, dn_keep_ref, dn_send_ref, up_keep_ref, up_send_ref, *refs = refs
    proj_got, up_got, down_got, up_b_ref, act_ref, slope_ref, proj_acc, up_acc, dn_acc, vec_acc, up_b_acc = refs
    step = pl.program_id(0)
    n_shards = n_others + 1
    ctx_rows, width = proj_own.shape
    hidden = up_own.shape[1]
    blocks = hidden // width
    inv_width = 1.0 / width

    def mean(v):
        return jnp.sum(v, axis=1, keepdims=True) * inv_width

    @pl.when(step == 0)
    def _():
        for ref in (proj_acc, up_acc, dn_acc):
            size = min(64, ref.shape[1])

            def clear(i, carry, ref=ref, size=size):
                for t in range(n_shards):
                    ref[t, aligned(i, size, size), :] = jnp.zeros((size, ref.shape[2]), f32)
                return carry

            lax.fori_loop(0, ref.shape[1] // size, clear, 0)
        for ref in (vec_acc, up_b_acc):
            ref[...] = jnp.zeros_like(ref)
        parity = lax.rem(pos_ref[0], 2)
        for j in range(blocks):
            up_b_ref[:, j * width : (j + 1) * width] = vecs_ref[8 + j : 9 + j, :]
        for t in range(n_others):
            for k in range(2):
                ref = fetched[2 * t + k]
                side = parity if k == 0 else 1 - parity
                rows = ctx_rows // 2
                proj_got[t, aligned(side, rows, rows), :] = ref[:rows]
                at = rows
                rows = hidden // 2
                down_got[t, aligned(side, rows, rows), :] = ref[at : at + rows]
                at += rows
                rows = width // 2
                for j in range(blocks):
                    up_got[t, aligned(side, rows, rows), j * width : (j + 1) * width] = ref[at : at + rows]
                    at += rows
                if k == 0:
                    for j in range(blocks):
                        to = (t + 1) * hidden + j * width
                        up_b_ref[:, to : to + width] = ref[at : at + EXTRA].astype(f32)[j : j + 1]

    def proj(t):
        return proj_own[...] if t == 0 else proj_got[t - 1]

    def up(t, c):
        return up_own[:, c : c + chunk] if t == 0 else up_got[t - 1, :, c : c + chunk]

    def down(t, c):
        return down_own[c : c + chunk, :] if t == 0 else down_got[t - 1, c : c + chunk, :]

    proj_b, gain_one, shift_one, down_b, gain_two, shift_two = (vecs_ref[k : k + 1, :] for k in range(6))
    branch = proj_b
    for t in range(n_shards):
        branch = branch + mm_tn(ctx_ref[t, 0], proj(t))
    mid_sum = x_ref[...].astype(f32) + branch
    center = mean(mid_sum)
    inv_one = lax.rsqrt(mean(mid_sum * mid_sum) - center * center + norm_eps)
    normal_one = (mid_sum - center) * inv_one
    normed_one = normal_one * gain_one + shift_one
    normed_low = normed_one.astype(bf16)
    second = down_b
    chunks = [(t, c) for t in range(n_shards) for c in range(0, hidden, chunk)]
    for t, c in chunks:
        at = t * hidden + c
        inner = mm(normed_low, up(t, c)) + up_b_ref[:, at : at + chunk]
        phi = 0.5 * lax.erf(inner * 0.7071067811865476) + 0.5
        active = (inner * phi).astype(bf16)
        act_ref[:, at : at + chunk] = active
        slope_ref[:, at : at + chunk] = phi + inner * (0.3989422804014327 * jnp.exp(-0.5 * inner * inner))
        second = second + mm(active, down(t, c))
    last_sum = normed_one + second
    center_two = mean(last_sum)
    inv_two = lax.rsqrt(mean(last_sum * last_sum) - center_two * center_two + norm_eps)
    normal_two = (last_sum - center_two) * inv_two
    out_ref[...] = (normal_two * gain_two + shift_two).astype(bf16)
    upstream = og_ref[...].astype(f32)
    scaled = upstream * gain_two
    grad_two = inv_two * (scaled - mean(scaled) - normal_two * mean(scaled * normal_two))
    second_low = grad_two.astype(bf16)
    normed_t = normed_low.T
    back = None
    for t, c in chunks:
        at = t * hidden + c
        grad_active = mm_nt(second_low, down(t, c))
        inner_low = (grad_active * slope_ref[:, at : at + chunk]).astype(bf16)
        up_b_acc[:, at : at + chunk] += jnp.sum(inner_low.astype(f32), axis=0, keepdims=True)
        part = mm_nt(inner_low, up(t, c))
        back = part if back is None else back + part
        up_acc[t, :, c : c + chunk] += mm(normed_t, inner_low)
        dn_acc[t, c : c + chunk, :] += mm_tn(act_ref[:, at : at + chunk], second_low)
    grad_mid = grad_two + back
    scaled_one = grad_mid * gain_one
    grad_one = inv_one * (scaled_one - mean(scaled_one) - normal_one * mean(scaled_one * normal_one))
    grad_one_ref[...] = grad_one
    branch_low = grad_one.astype(bf16)
    sums = (
        branch_low.astype(f32),
        grad_mid * normal_one,
        grad_mid,
        second_low.astype(f32),
        upstream * normal_two,
        upstream,
    )
    for k, value in enumerate(sums):
        vec_acc[k : k + 1, :] += jnp.sum(value, axis=0, keepdims=True)
    for t in range(n_shards):
        ctx_low_ref[t, 0] = mm_nt(proj(t), branch_low).astype(bf16)
        proj_acc[t] += mm(ctx_ref[t, 0], branch_low)

    @pl.when(step == pl.num_programs(0) - 1)
    def _():
        low = lax.rem(pos_ref[0], MLP_SLOTS)
        dn_rows, up_rows, proj_rows = hidden // MLP_SLOTS, width // MLP_SLOTS, ctx_rows // MLP_SLOTS
        half = MLP_SLOTS // 2
        for slot in range(MLP_SLOTS):
            dn_ref = dn_keep_ref if slot < half else dn_send_ref
            upk_ref = up_keep_ref if slot < half else up_send_ref
            k = slot % half
            dn_at = lax.bitwise_xor(low, DOWN_BITS[slot])
            rows = aligned(lax.bitwise_xor(low, UP_BITS[slot]), up_rows, up_rows)
            for t in range(n_shards):
                dn_ref[t, k, :dn_rows] = dn_acc[t, aligned(dn_at, dn_rows, dn_rows), :].astype(bf16)
                dn_ref[t, k, dn_rows:] = proj_acc[t, aligned(dn_at, proj_rows, proj_rows), :].astype(bf16)
                for j in range(blocks):
                    to = j * up_rows
                    upk_ref[t, k, to : to + up_rows] = up_acc[t, rows, j * width : (j + 1) * width].astype(bf16)
                to = blocks * up_rows
                upk_ref[t, k, to : to + 8] = vec_acc[...].astype(bf16)
                tail = [
                    up_b_acc[:, t * hidden + j * width : t * hidden + (j + 1) * width] for j in range(blocks)
                ]
                tail.append(jnp.zeros((8 - blocks, width), f32))
                upk_ref[t, k, to + 8 : to + EXTRA] = jnp.concatenate(tail, axis=0).astype(bf16)


def middle(pos, x, out_grad, ctx, vecs, proj, up, down, fetched):
    rows, width = x.shape
    n_shards, n_seq, ctx_rows, _ = ctx.shape
    hidden = up.shape[1]
    n_others = n_shards - 1
    block = 512
    per_seq = SEQ_LEN // block
    half = MLP_SLOTS // 2
    dn_rows, up_rows = (hidden + ctx_rows) // MLP_SLOTS, hidden // MLP_SLOTS + EXTRA

    def whole(array):
        return pl.BlockSpec(array.shape, lambda i, pos: (0,) * array.ndim, pipeline_mode=pl.Buffered(1))

    def kept(*shape):
        return pl.BlockSpec(shape, lambda i, pos: (0,) * len(shape))

    row = pl.BlockSpec((block, width), lambda i, pos: (i, 0))
    cols = pl.BlockSpec((n_shards, 1, ctx_rows, block), lambda i, pos: (0, i // per_seq, 0, i % per_seq))
    dn_shape, up_shape = (n_shards, half, dn_rows, width), (n_shards, half, up_rows, width)
    consts = [vecs, proj, up, down] + fetched
    return pl.pallas_call(
        partial(middle_kernel, n_others=n_others, chunk=min(1024, hidden)),
        grid_spec=pltpu.PrefetchScalarGridSpec(
            num_scalar_prefetch=1,
            grid=(rows // block,),
            in_specs=[row, row, cols] + [whole(array) for array in consts],
            out_specs=[row, row, cols, kept(*dn_shape), kept(*dn_shape), kept(*up_shape), kept(*up_shape)],
            scratch_shapes=[
                pltpu.VMEM((n_others, ctx_rows, width), bf16),
                pltpu.VMEM((n_others, width, hidden), bf16),
                pltpu.VMEM((n_others, hidden, width), bf16),
                pltpu.VMEM((1, n_shards * hidden), f32),
                pltpu.VMEM((block, n_shards * hidden), bf16),
                pltpu.VMEM((block, n_shards * hidden), f32),
                pltpu.VMEM((n_shards, ctx_rows, width), f32),
                pltpu.VMEM((n_shards, width, hidden), f32),
                pltpu.VMEM((n_shards, hidden, width), f32),
                pltpu.VMEM((8, width), f32),
                pltpu.VMEM((1, n_shards * hidden), f32),
            ],
        ),
        out_shape=[
            jax.ShapeDtypeStruct((rows, width), bf16),
            jax.ShapeDtypeStruct((rows, width), f32),
            jax.ShapeDtypeStruct(ctx.shape, bf16),
            jax.ShapeDtypeStruct(dn_shape, bf16),
            jax.ShapeDtypeStruct(dn_shape, bf16),
            jax.ShapeDtypeStruct(up_shape, bf16),
            jax.ShapeDtypeStruct(up_shape, bf16),
        ],
        compiler_params=kernel_params(),
        cost_estimate=cost(30 << 30, 30 << 20),
        name="middle",
    )(pos, x, out_grad, ctx, *consts)


def piece_number(pos, slot, cut):
    number = 0
    for k, bit in enumerate(cut):
        own = lax.bitwise_and(lax.shift_right_logical(pos, bit.bit_length() - 1), 1)
        flip = (slot >> (len(cut) - 1 - k)) & 1
        number = number + (lax.bitwise_xor(own, flip) << k)
    return number


def attn_bwd_kernel(
    pos_ref,
    x_ref,
    packed_ref,
    probs_ref,
    ctx_low_ref,
    sums_ref,
    *refs,
    head,
    cut,
    extra,
    q_block,
    unroll,
):
    grad_ref, keep_ref, send_ref, bias_ref, *refs = refs[-10:]
    value_ref, key_acc, value_acc, weight_acc, grad_a, grad_b = refs
    step = pl.program_id(0)
    seq = x_ref.shape[0]
    n_shards = packed_ref.shape[0]
    scale = HEAD_DIM**-0.5
    for t in range(n_shards):
        value_ref[t] = packed_ref[t, 0, 2 * HEAD_DIM : 3 * HEAD_DIM, :].T
    tiles = list(range(0, seq, q_block))
    buffers = (grad_a, grad_b)

    def start(t, c, ref):
        ref[...] = mm(value_ref[t], ctx_low_ref[t, 0, :, c : c + q_block])

    def finish(t, c, ref):
        cols = slice(c, c + q_block)
        probs_low = probs_ref[t, 0, 0, :, cols]
        probs = probs_low.astype(f32)
        weighted = probs * ref[...]
        total = jnp.sum(weighted, axis=0, keepdims=True)
        score_low = (weighted - probs * total).astype(bf16)
        grad_query = mm(packed_ref[t, 0, HEAD_DIM : 2 * HEAD_DIM, :], score_low) * scale
        grad_ref[t, 0, :HEAD_DIM, cols] = grad_query.astype(bf16)
        grad_key = mm_nt(packed_ref[t, 0, :HEAD_DIM, cols], score_low)
        grad_value = mm_nt(ctx_low_ref[t, 0, :, cols], probs_low)
        if c > 0:
            grad_key = key_acc[...] + grad_key
            grad_value = value_acc[...] + grad_value
        if c + q_block < seq:
            key_acc[...] = grad_key
            value_acc[...] = grad_value
        else:
            grad_ref[t, 0, HEAD_DIM : 2 * HEAD_DIM, :] = (grad_key * scale).astype(bf16)
            grad_ref[t, 0, 2 * HEAD_DIM :, :] = grad_value.astype(bf16)

    start(0, 0, buffers[0])

    def one_shard(t, carry):
        for j, c in enumerate(tiles):
            if j + 1 < len(tiles):
                start(t, tiles[j + 1], buffers[(j + 1) % 2])
            elif not unroll:
                start(jnp.minimum(t + 1, n_shards - 1), 0, buffers[(j + 1) % 2])
            elif t + 1 < n_shards:
                start(t + 1, 0, buffers[(j + 1) % 2])
            finish(t, c, buffers[j % 2])
        return carry

    if unroll:
        for t in range(n_shards):
            one_shard(t, 0)
    else:
        lax.fori_loop(0, n_shards, one_shard, 0)

    @pl.when(step == 0)
    def _():
        weight_acc[...] = jnp.zeros_like(weight_acc)
        bias_ref[...] = sums_ref[...]

    ones = jnp.ones((8, seq), bf16)
    for t in range(n_shards):
        weight_acc[t] += mm(grad_ref[t, 0], x_ref[...])
        bias_ref[t, head : head + 1] += mm_nt(ones, grad_ref[t, 0])[:1]

    @pl.when(step == pl.num_programs(0) - 1)
    def _():
        slots = 1 << len(cut)
        half = slots // 2
        rows = PART_ROWS // slots
        for slot in range(slots):
            at = piece_number(pos_ref[0], slot, cut)
            ref = keep_ref if slot < half else send_ref
            for t in range(n_shards):
                ref[t, slot % half, :rows] = weight_acc[t, aligned(at, rows, 8), :].astype(bf16)
                if extra:
                    padded = jnp.concatenate(
                        [bias_ref[t], jnp.zeros((EXTRA, ref.shape[3] - PART_ROWS), f32)], axis=1
                    )
                    ref[t, slot % half, rows:] = padded.astype(bf16)


def attn_bwd(pos, x, packed, probs, ctx_low, sums, head, first, group, cut, extra, unroll, earlier):
    rows, width = x.shape
    n_shards, n_seq = packed.shape[:2]
    q_block = 256
    slots = 1 << len(cut)
    each = PART_ROWS // slots + (EXTRA if extra else 0)
    pieces = (n_shards, slots // 2, group * each, width)
    piece = pl.BlockSpec((n_shards, slots // 2, each, width), lambda s, pos: (0, 0, head - first, 0))
    sum_spec = pl.BlockSpec(sums.shape, lambda s, pos: (0, 0, 0))
    return pl.pallas_call(
        partial(attn_bwd_kernel, head=head, cut=cut, extra=extra, q_block=q_block, unroll=unroll),
        grid_spec=pltpu.PrefetchScalarGridSpec(
            num_scalar_prefetch=1,
            grid=(n_seq,),
            in_specs=[
                pl.BlockSpec((SEQ_LEN, width), lambda s, pos: (s, 0)),
                pl.BlockSpec((n_shards, 1, PART_ROWS, SEQ_LEN), lambda s, pos: (0, s, head, 0)),
                pl.BlockSpec((n_shards, 1, 1, SEQ_LEN, SEQ_LEN), lambda s, pos: (0, s, head, 0, 0)),
                pl.BlockSpec((n_shards, 1, HEAD_DIM, SEQ_LEN), lambda s, pos: (0, s, head, 0)),
                sum_spec,
            ]
            + [pl.BlockSpec(memory_space=pl.ANY)] * len(earlier),
            out_specs=[
                pl.BlockSpec((n_shards, 1, PART_ROWS, SEQ_LEN), lambda s, pos: (0, s, 0, 0)),
                piece,
                piece,
                sum_spec,
            ],
            scratch_shapes=[
                pltpu.VMEM((n_shards, SEQ_LEN, HEAD_DIM), bf16),
                pltpu.VMEM((HEAD_DIM, SEQ_LEN), f32),
                pltpu.VMEM((HEAD_DIM, SEQ_LEN), f32),
                pltpu.VMEM((n_shards, PART_ROWS, width), f32),
                pltpu.VMEM((SEQ_LEN, q_block), f32),
                pltpu.VMEM((SEQ_LEN, q_block), f32),
            ],
        ),
        out_shape=[
            jax.ShapeDtypeStruct((n_shards, n_seq, PART_ROWS, SEQ_LEN), bf16),
            jax.ShapeDtypeStruct(pieces, bf16),
            jax.ShapeDtypeStruct(pieces, bf16),
            jax.ShapeDtypeStruct(sums.shape, f32),
        ],
        input_output_aliases={6: 1, 7: 2} if earlier else {},
        compiler_params=kernel_params(48_000_000),
        cost_estimate=cost(8 << 30, 10 << 20),
        name="attn_bwd",
    )(pos, x, packed, probs, ctx_low, sums, *earlier)


def input_grad_kernel(pos_ref, grad_one_ref, own_ref, *refs, n_others):
    fetched, grads, out_ref, got_ref = refs[: 2 * n_others], refs[2 * n_others : -2], refs[-2], refs[-1]
    half = own_ref.shape[0] // 2

    @pl.when(pl.program_id(0) == 0)
    def _():
        parity = lax.rem(pos_ref[0], 2)
        for t in range(n_others):
            for k in range(2):
                side = parity if k == 0 else 1 - parity
                got_ref[t, aligned(side, half, half), :] = fetched[2 * t + k][:half]

    total = grad_one_ref[...]
    for t in range(n_others + 1):
        weight = own_ref if t == 0 else got_ref.at[t - 1]
        for head, ref in enumerate(grads):
            total = total + mm_tn(ref[t, 0], weight[head * PART_ROWS : (head + 1) * PART_ROWS, :])
    out_ref[...] = total.astype(bf16)


def input_gradient(pos, grad_one, own, fetched, packed_grads):
    rows, width = grad_one.shape
    n_shards = packed_grads[0].shape[0]
    block = 512
    per_seq = SEQ_LEN // block
    row = pl.BlockSpec((block, width), lambda i, pos: (i, 0))
    cols = pl.BlockSpec((n_shards, 1, PART_ROWS, block), lambda i, pos: (0, i // per_seq, 0, i % per_seq))

    def whole(array):
        return pl.BlockSpec(array.shape, lambda i, pos: (0, 0), pipeline_mode=pl.Buffered(1))

    return pl.pallas_call(
        partial(input_grad_kernel, n_others=n_shards - 1),
        grid_spec=pltpu.PrefetchScalarGridSpec(
            num_scalar_prefetch=1,
            grid=(rows // block,),
            in_specs=[row, whole(own)] + [whole(v) for v in fetched] + [cols] * len(packed_grads),
            out_specs=row,
            scratch_shapes=[pltpu.VMEM((n_shards - 1,) + own.shape, bf16)],
        ),
        out_shape=jax.ShapeDtypeStruct((rows, width), bf16),
        compiler_params=kernel_params(48_000_000),
        cost_estimate=cost(4 << 30, 12 << 20),
        name="input_gradient",
    )(pos, grad_one, own, *fetched, *packed_grads)


def mlp_place_kernel(pos_ref, dn_near, dn_far, up_near, up_far, proj_out, up_out, dn_out):
    low = lax.rem(pos_ref[0], MLP_SLOTS)
    half = MLP_SLOTS // 2
    width = proj_out.shape[1]
    hidden = dn_out.shape[0]
    dn_rows, up_rows, proj_rows = hidden // MLP_SLOTS, width // MLP_SLOTS, proj_out.shape[0] // MLP_SLOTS
    for slot in range(MLP_SLOTS):
        dn_ref = dn_near if slot < half else dn_far
        up_ref = up_near if slot < half else up_far
        k = slot % half
        at = lax.bitwise_xor(low, DOWN_BITS[slot])
        dn_out[aligned(at, dn_rows, dn_rows), :] = dn_ref[k, :dn_rows].astype(f32)
        proj_out[aligned(at, proj_rows, proj_rows), :] = dn_ref[k, dn_rows:].astype(f32)
        rows = aligned(lax.bitwise_xor(low, UP_BITS[slot]), up_rows, up_rows)
        for j in range(hidden // width):
            up_out[rows, j * width : (j + 1) * width] = up_ref[k, j * up_rows : (j + 1) * up_rows].astype(f32)


def mlp_place(pos, dn_parts, up_parts, ctx_rows, width, hidden):
    return pl.pallas_call(
        mlp_place_kernel,
        in_specs=[pl.BlockSpec(memory_space=pltpu.SMEM)] + [in_vmem()] * 4,
        out_specs=[in_vmem()] * 3,
        out_shape=[
            jax.ShapeDtypeStruct((ctx_rows, width), f32),
            jax.ShapeDtypeStruct((width, hidden), f32),
            jax.ShapeDtypeStruct((hidden, width), f32),
        ],
        compiler_params=kernel_params(48_000_000),
        cost_estimate=cost(0, 14 << 20),
        name="mlp_place",
    )(pos, *dn_parts, *up_parts)


def qkv_place_kernel(pos_ref, *refs, groups):
    bias_ref, out_ref, query_ref, value_ref = refs[-4:]
    for g, (first, group, cut, each) in enumerate(groups):
        slots = 1 << len(cut)
        half = slots // 2
        rows = PART_ROWS // slots
        for slot in range(slots):
            at = aligned(piece_number(pos_ref[0], slot, cut), rows, 8)
            for k in range(group):
                value = refs[2 * g + slot // half][slot % half, k * each : k * each + rows]
                out_ref[first + k, at, :] = value.astype(f32)
    heads = out_ref.shape[0]
    for k, ref in ((0, query_ref), (2, value_ref)):
        parts = [bias_ref[h : h + 1, k * HEAD_DIM : (k + 1) * HEAD_DIM] for h in range(heads)]
        ref[...] = jnp.concatenate(parts, axis=1).reshape(heads * HEAD_DIM)


def qkv_place(pos, parts, bias, groups, heads):
    flat = [half for pair in parts for half in pair]
    vector = jax.ShapeDtypeStruct((heads * HEAD_DIM,), f32)
    return pl.pallas_call(
        partial(qkv_place_kernel, groups=groups),
        in_specs=[pl.BlockSpec(memory_space=pltpu.SMEM)] + [in_vmem()] * (len(flat) + 1),
        out_specs=[in_vmem()] * 3,
        out_shape=[jax.ShapeDtypeStruct((heads, PART_ROWS, flat[0].shape[2]), f32), vector, vector],
        compiler_params=kernel_params(48_000_000),
        cost_estimate=cost(0, 3 << 20),
        name="qkv_place",
    )(pos, *flat, bias)


def swap_dp(value, bits, n_dp):
    return lax.ppermute(value, "dp", [(i, i ^ bits) for i in range(n_dp)])


def shift_tensor(value, by, n_tensor):
    return lax.ppermute(value, "tensor", [((i + by) % n_tensor, i) for i in range(n_tensor)])


def reduce_pieces(keep, send, order, n_dp, n_tensor):
    halved = [axis for axis in order if axis != "tensor"]
    got = swap_dp(send, 1, n_dp)
    got = after(got, (yield send))
    parts = [keep[t].astype(f32) + got[t].astype(f32) for t in range(n_tensor)]
    for axis in order:
        if axis == "tensor":
            outs = [parts[by].astype(bf16) for by in range(1, n_tensor)]
            gots = [shift_tensor(out, -by, n_tensor) for by, out in enumerate(outs, 1)]
            gots = after(gots, (yield outs))
            parts = [sum((got.astype(f32) for got in gots), parts[0])]
        else:
            cut = parts[0].shape[0] // 2
            out = jnp.stack([part[cut:].astype(bf16) for part in parts])
            got = swap_dp(out, axis, n_dp)
            got = after(got, (yield out))
            parts = [part[:cut] + got[t].astype(f32) for t, part in enumerate(parts)]
    own = parts[0]
    bits = 2
    while bits < n_dp:
        if bits not in halved:
            out = own.astype(bf16)
            got = swap_dp(out, bits, n_dp)
            got = after(got, (yield out))
            own = own + got.astype(f32)
        bits *= 2
    near = own.astype(bf16)
    for axis in reversed(halved):
        got = swap_dp(near, axis, n_dp)
        got = after(got, (yield near))
        near = jnp.concatenate([near, got], axis=0)
    got = swap_dp(near, 1, n_dp)
    got = after(got, (yield near))
    return near, got, own


class Sums:
    def __init__(self):
        self.live, self.done, self.fresh = {}, {}, set()

    def add(self, name, generator):
        self.live[name] = generator
        self.fresh.add(name)

    def step(self, ready, *names):
        sent = []
        for name in names:
            if name in self.live:
                try:
                    sent.append(self.live[name].send(None if name in self.fresh else ready))
                    self.fresh.discard(name)
                except StopIteration as stop:
                    self.done[name] = stop.value
                    del self.live[name]
        return sent

    def finish(self):
        while self.live:
            self.step((), *list(self.live))


def after(value, *others):
    return lax.optimization_barrier((value, others))[0]


def sequence_body(n_dp, n_tensor, *arrays):
    (
        layer_input,
        output_grad,
        qkv_weight,
        query_bias,
        value_bias,
        proj_weight,
        proj_bias,
        first_gain,
        first_shift,
        up_weight,
        up_bias,
        down_weight,
        down_bias,
        second_gain,
        second_shift,
    ) = arrays
    rows, width = layer_input.shape
    n_seq = rows // SEQ_LEN
    ctx_rows, hidden = proj_weight.shape[0], up_weight.shape[1]
    n_heads = ctx_rows // HEAD_DIM
    pos = lax.axis_index("dp").astype(jnp.int32).reshape(1)
    shifts = range(1, n_tensor)

    qkv_half, own_bias = pack_qkv(pos, qkv_weight, query_bias, value_bias)
    qkv_near = [shift_tensor(qkv_half, by, n_tensor) for by in shifts]
    vectors = [proj_bias, first_gain, first_shift, down_bias, second_gain, second_shift]
    mlp_half, vecs = pack_mlp(after(pos, qkv_half), proj_weight, down_weight, up_weight, up_bias, vectors)
    shapes = [
        jax.ShapeDtypeStruct((n_tensor, n_seq, n_heads * PART_ROWS, SEQ_LEN), bf16),
        jax.ShapeDtypeStruct((n_tensor, n_seq, n_heads, SEQ_LEN, SEQ_LEN), bf16),
        jax.ShapeDtypeStruct((n_tensor, n_seq, n_heads * HEAD_DIM, SEQ_LEN), bf16),
    ]
    mlp_near = [shift_tensor(mlp_half, by, n_tensor) for by in shifts]
    x = after(layer_input, mlp_half)
    stacks = attn_fwd(pos, x, (qkv_weight, own_bias), 0, False, shapes, ())
    qkv_near = after(qkv_near, stacks[2])
    qkv_far = [swap_dp(near, 1, n_dp) for near in qkv_near]
    for t in shifts:
        stacks = attn_fwd(pos, layer_input, (qkv_near[t - 1], qkv_far[t - 1]), t, True, shapes, stacks)
    packed, probs, ctx = stacks
    mlp_near = after(mlp_near, ctx)
    mlp_far = [swap_dp(near, 1, n_dp) for near in mlp_near]
    fetched = [half for pair in zip(mlp_near, mlp_far) for half in pair]
    result, grad_one, ctx_low, dn_keep, dn_send, up_keep, up_send = middle(
        pos, layer_input, output_grad, ctx, vecs, proj_weight, up_weight, down_weight, fetched
    )
    sums = Sums()
    sums.add("dn", reduce_pieces(dn_keep, dn_send, DOWN_ORDER, n_dp, n_tensor))
    sums.add("up", reduce_pieces(up_keep, up_send, UP_ORDER, n_dp, n_tensor))
    bias_sums = jnp.zeros((n_tensor, EXTRA, PART_ROWS), f32)
    packed_grads = []
    ready = ()
    early = n_heads - 1
    stacked = ()
    early_cut, early_order = (1, 2), ("tensor", 2)
    for head in range(n_heads):
        last = head == early
        if last and early:
            sums.add("qa", reduce_pieces(*stacked, early_order, n_dp, n_tensor))
        sent = sums.step(ready, *SCHEDULE[min(head, len(SCHEDULE) - 3)])
        x = after(layer_input, sent)
        grads, keep, send, bias_sums = attn_bwd(
            pos,
            x,
            packed,
            probs,
            ctx_low,
            bias_sums,
            head,
            early if last else 0,
            1 if last else early,
            (1,) if last else early_cut,
            last,
            head in UNROLLED,
            () if last else stacked,
        )
        ready = bias_sums
        packed_grads.append(grads)
        if not last:
            stacked = (keep, send)
    sums.add("qb", reduce_pieces(keep, send, ("tensor",), n_dp, n_tensor))
    sent = sums.step(ready, *SCHEDULE[-2])
    qkv_fetched = [half for pair in zip(qkv_near, qkv_far) for half in pair]
    input_grad = input_gradient(pos, after(grad_one, sent), qkv_weight, qkv_fetched, packed_grads)
    ready = input_grad
    for name in SCHEDULE[-1]:
        sent = sums.step(ready, name)
        ready = sent or ready
    sums.finish()
    dn_near, dn_far, _ = sums.done["dn"]
    up_near, up_far, up_own = sums.done["up"]
    proj_wg, up_wg, dn_wg = mlp_place(pos, (dn_near, dn_far), (up_near, up_far), ctx_rows, width, hidden)
    groups = [(0, early, early_cut, PART_ROWS // 4)] if early else []
    groups.append((early, 1, (1,), PART_ROWS // 2 + EXTRA))
    parts = [sums.done[name][:2] for name in ("qa", "qb") if name in sums.done]
    bias = sums.done["qb"][2][0, -EXTRA:]
    qkv_wg, query_bg, value_bg = qkv_place(pos, parts, bias, groups, n_heads)
    small = up_own[0, -EXTRA:]
    return (
        result,
        input_grad,
        qkv_wg.reshape(n_heads * PART_ROWS, width),
        query_bg,
        value_bg,
        proj_wg,
        small[0],
        small[1],
        small[2],
        up_wg,
        small[8 : 8 + hidden // width].reshape(hidden),
        dn_wg,
        small[3],
        small[4],
        small[5],
    )


SCHEDULE = (
    ("dn", "up"),
    ("dn", "up"),
    ("dn", "up"),
    ("qa", "dn", "up", "qa"),
    ("qb", "qa", "dn", "up", "qb"),
    ("qb", "qa", "dn", "up", "qb", "qa", "up", "dn", "qb", "qa", "up", "dn", "qb", "qa"),
)
UNROLLED = ()


def solution(mesh):
    n_dp, n_tensor = mesh.shape["dp"], mesh.shape["tensor"]

    def body(*arrays):
        rows = arrays[0].shape[0]
        if rows % SEQ_LEN == 0 and n_dp % 8 == 0 and n_dp & (n_dp - 1) == 0:
            return sequence_body(n_dp, n_tensor, *arrays)
        return token_body(*arrays)

    return jax.shard_map(
        body,
        mesh=mesh,
        in_specs=(
            P(("dp", "tensor"), None),
            P(("dp", "tensor"), None),
            P("tensor", None),
            P("tensor"),
            P("tensor"),
            P("tensor", None),
            P(),
            P(),
            P(),
            P(None, "tensor"),
            P("tensor"),
            P("tensor", None),
            P(),
            P(),
            P(),
        ),
        out_specs=(
            P(("dp", "tensor"), None),
            P(("dp", "tensor"), None),
            P("tensor", None),
            P("tensor"),
            P("tensor"),
            P("tensor", None),
            P(),
            P(),
            P(),
            P(None, "tensor"),
            P("tensor"),
            P("tensor", None),
            P(),
            P(),
            P(),
        ),
        check_vma=False,
    )
```

```python
from functools import partial

import jax
import jax.numpy as jnp
from jax import lax
from jax.experimental import pallas as pl
from jax.experimental.pallas import tpu as pltpu
from jax.sharding import PartitionSpec as P

HEAD_DIM = 64
SEQ_LEN = 1024
PART_ROWS = 3 * HEAD_DIM

norm_eps = 1e-05
f32 = jnp.float32
bf16 = jnp.bfloat16


def matmul_rows(left, right):
    return lax.dot_general(
        left, right, (((0,), (0,)), ((), ())), preferred_element_type=jnp.float32
    )


def matmul_back(left, right):
    return lax.dot_general(
        left, right, (((1,), (1,)), ((), ())), preferred_element_type=jnp.float32
    )


def attend_forward(queries, key_rows, value_rows):
    seq_heads = key_rows.shape[0] * key_rows.shape[1]
    head_dim = queries.shape[-1]
    score_scale = head_dim ** (-0.5)
    block_rows = min(512, SEQ_LEN)
    block_count = SEQ_LEN // block_rows
    item_count = seq_heads * block_count
    query_items = queries.reshape(item_count, block_rows, head_dim)
    key_all = key_rows.reshape(seq_heads, SEQ_LEN, head_dim)
    value_all = value_rows.reshape(seq_heads, SEQ_LEN, head_dim)

    def one_block(block_item):
        query_blk, position = block_item
        owner_index = position // block_count
        keys_here = key_all[owner_index]
        values_here = value_all[owner_index]
        scores = matmul_back(query_blk, keys_here) * score_scale
        row_top = jnp.max(scores, axis=-1, keepdims=True)
        exponent = jnp.exp(scores - row_top)
        row_total = jnp.sum(exponent, axis=-1, keepdims=True)
        weights_now = exponent / row_total
        mixed_rows = jnp.dot(
            weights_now.astype(jnp.bfloat16), values_here, preferred_element_type=jnp.float32
        )
        return (mixed_rows, row_top[:, 0] + jnp.log(row_total[:, 0]))

    mixed_rows, log_total = lax.map(
        one_block, (query_items, jnp.arange(item_count, dtype=jnp.int32))
    )
    return (mixed_rows.reshape(queries.shape), log_total.reshape(queries.shape[:-1]))


def attend_backward(queries, key_rows, value_rows, log_total, context_low):
    seq_heads = key_rows.shape[0] * key_rows.shape[1]
    head_dim = queries.shape[-1]
    score_scale = head_dim ** (-0.5)
    block_rows = min(512, SEQ_LEN)
    block_count = SEQ_LEN // block_rows
    item_count = seq_heads * block_count
    query_items = queries.reshape(item_count, block_rows, head_dim)
    total_items = log_total.reshape(item_count, block_rows)
    grad_items = context_low.reshape(item_count, block_rows, head_dim)
    key_all = key_rows.reshape(seq_heads, SEQ_LEN, head_dim)
    value_all = value_rows.reshape(seq_heads, SEQ_LEN, head_dim)

    def one_block(block_item):
        query_blk, total_blk, grad_blk, position = block_item
        owner_index = position // block_count
        keys_here = key_all[owner_index]
        values_here = value_all[owner_index]
        scores = matmul_back(query_blk, keys_here) * score_scale
        weights_now = jnp.exp(scores - total_blk[:, None])
        grad_weights = matmul_back(grad_blk, values_here)
        grad_scores = weights_now * (
            grad_weights - jnp.sum(weights_now * grad_weights, axis=-1, keepdims=True)
        )
        score_low = grad_scores.astype(jnp.bfloat16)
        grad_query = jnp.dot(score_low, keys_here, preferred_element_type=jnp.float32) * score_scale
        grad_key = matmul_rows(score_low, query_blk) * score_scale
        grad_value = matmul_rows(weights_now.astype(jnp.bfloat16), grad_blk)
        return (grad_query, grad_key, grad_value)

    grad_query, grad_key, grad_value = lax.map(
        one_block, (query_items, total_items, grad_items, jnp.arange(item_count, dtype=jnp.int32))
    )
    grad_key = jnp.sum(grad_key.reshape(seq_heads, block_count, SEQ_LEN, head_dim), axis=1)
    grad_value = jnp.sum(grad_value.reshape(seq_heads, block_count, SEQ_LEN, head_dim), axis=1)
    return (
        grad_query.reshape(queries.shape),
        grad_key.reshape(key_rows.shape),
        grad_value.reshape(value_rows.shape),
    )


def norm_forward(hidden, gain_vec, shift_vec):
    center = jnp.mean(hidden, axis=-1)
    second = jnp.mean(hidden * hidden, axis=-1) - center * center
    inv_std = lax.rsqrt(second + norm_eps)
    normal = (hidden - center[:, None]) * inv_std[:, None]
    return (normal * gain_vec + shift_vec, normal, inv_std)


def norm_backward(upstream, normal, inv_std, gain_vec):
    scaled = upstream * gain_vec
    first_mean = jnp.mean(scaled, axis=-1)
    second_mean = jnp.mean(scaled * normal, axis=-1)
    grad_in = inv_std[:, None] * (scaled - first_mean[:, None] - normal * second_mean[:, None])
    return (grad_in, jnp.sum(upstream * normal, axis=0), jnp.sum(upstream, axis=0))


def rows_in(value):
    return lax.all_gather(value, "tensor", axis=0, tiled=True)


def part_out(value):
    return lax.psum_scatter(value, "tensor", scatter_dimension=0, tiled=True)


def gather_grad(value):
    return lax.all_gather(value, "tensor", axis=0, tiled=True)


def part_back(value):
    return lax.psum_scatter(value, "tensor", scatter_dimension=0, tiled=True)


def token_body(
    layer_input,
    output_grad,
    qkv_weight,
    query_bias,
    value_bias,
    proj_weight,
    proj_bias,
    first_gain,
    first_shift,
    up_weight,
    up_bias,
    down_weight,
    down_bias,
    second_gain,
    second_shift,
):
    heads_here = query_bias.shape[0] // HEAD_DIM
    query_bf = query_bias.astype(jnp.float32).reshape(heads_here, HEAD_DIM)
    value_bf = value_bias.astype(jnp.float32).reshape(heads_here, HEAD_DIM)
    bias_rows = jnp.stack([query_bf, jnp.zeros_like(query_bf), value_bf], axis=1)
    gain_one = first_gain.astype(jnp.float32)
    shift_one = first_shift.astype(jnp.float32)
    gain_two = second_gain.astype(jnp.float32)
    shift_two = second_shift.astype(jnp.float32)
    input_full = rows_in(layer_input)
    row_count = input_full.shape[0]
    seq_count = row_count // SEQ_LEN
    projected = matmul_back(input_full, qkv_weight).reshape(row_count, heads_here, 3, HEAD_DIM)
    packed = (projected + bias_rows).astype(jnp.bfloat16)
    parts = packed.reshape(seq_count, SEQ_LEN, heads_here, 3, HEAD_DIM).transpose(3, 0, 2, 1, 4)
    queries, key_rows, value_rows = (parts[0], parts[1], parts[2])
    mixed_rows, log_total = attend_forward(queries, key_rows, value_rows)
    context = (
        mixed_rows.transpose(0, 2, 1, 3)
        .reshape(row_count, heads_here * HEAD_DIM)
        .astype(jnp.bfloat16)
    )
    partial_branch = jnp.dot(context, proj_weight, preferred_element_type=jnp.float32)
    branch = part_out(partial_branch) + proj_bias.astype(jnp.float32)
    normed_one, normal_one, inv_one = norm_forward(
        layer_input.astype(jnp.float32) + branch, gain_one, shift_one
    )
    normed_full = rows_in(normed_one.astype(jnp.bfloat16))
    inner_pre = jnp.dot(
        normed_full, up_weight, preferred_element_type=jnp.float32
    ) + up_bias.astype(jnp.float32)
    active, gelu_back = jax.vjp(partial(jax.nn.gelu, approximate=False), inner_pre)
    active_low = active.astype(jnp.bfloat16)
    second = part_out(
        jnp.dot(active_low, down_weight, preferred_element_type=jnp.float32)
    ) + down_bias.astype(jnp.float32)
    result_rows, normal_two, inv_two = norm_forward(normed_one + second, gain_two, shift_two)
    upstream = output_grad.astype(jnp.float32)
    grad_two, gain_two_grad, shift_two_grad = norm_backward(upstream, normal_two, inv_two, gain_two)
    second_low = grad_two.astype(jnp.bfloat16)
    down_b_grad = jnp.sum(second_low.astype(jnp.float32), axis=0)
    second_full = gather_grad(second_low)
    down_w_grad = matmul_rows(active_low, second_full)
    grad_active = matmul_back(second_full, down_weight)
    inner_low = gelu_back(grad_active)[0].astype(jnp.bfloat16)
    up_b_grad = jnp.sum(inner_low.astype(jnp.float32), axis=0)
    up_w_grad = matmul_rows(normed_full, inner_low)
    grad_mid = grad_two + part_back(matmul_back(inner_low, up_weight))
    grad_one, gain_one_grad, shift_one_grad = norm_backward(grad_mid, normal_one, inv_one, gain_one)
    branch_low = grad_one.astype(jnp.bfloat16)
    proj_b_grad = jnp.sum(branch_low.astype(jnp.float32), axis=0)
    branch_full = gather_grad(branch_low)
    proj_w_grad = matmul_rows(context, branch_full)
    context_low = matmul_back(branch_full, proj_weight).astype(jnp.bfloat16)
    context_low = context_low.reshape(seq_count, SEQ_LEN, heads_here, HEAD_DIM).transpose(
        0, 2, 1, 3
    )
    grad_query, grad_key, grad_value = attend_backward(
        queries, key_rows, value_rows, log_total, context_low
    )
    packed_low = jnp.stack([grad_query, grad_key, grad_value], axis=0).transpose(1, 3, 2, 0, 4)
    packed_low = packed_low.reshape(row_count, heads_here * 3 * HEAD_DIM).astype(jnp.bfloat16)
    packed_sums = jnp.sum(packed_low.astype(jnp.float32), axis=0).reshape(heads_here, 3, HEAD_DIM)
    query_b_grad = packed_sums[:, 0].reshape(heads_here * HEAD_DIM)
    value_b_grad = packed_sums[:, 2].reshape(heads_here * HEAD_DIM)
    qkv_w_grad = matmul_rows(packed_low, input_full)
    input_grad = (
        grad_one + part_back(jnp.dot(packed_low, qkv_weight, preferred_element_type=jnp.float32))
    ).astype(jnp.bfloat16)
    totals = (
        lax.psum(qkv_w_grad.astype(jnp.bfloat16), "dp").astype(jnp.float32),
        lax.psum(query_b_grad.astype(jnp.bfloat16), "dp").astype(jnp.float32),
        lax.psum(value_b_grad.astype(jnp.bfloat16), "dp").astype(jnp.float32),
        lax.psum(proj_w_grad.astype(jnp.bfloat16), "dp").astype(jnp.float32),
        lax.psum(up_w_grad.astype(jnp.bfloat16), "dp").astype(jnp.float32),
        lax.psum(up_b_grad.astype(jnp.bfloat16), "dp").astype(jnp.float32),
        lax.psum(down_w_grad.astype(jnp.bfloat16), "dp").astype(jnp.float32),
    )
    vectors = lax.psum(
        (proj_b_grad, gain_one_grad, shift_one_grad, down_b_grad, gain_two_grad, shift_two_grad),
        ("dp", "tensor"),
    )
    return (
        result_rows.astype(jnp.bfloat16),
        input_grad,
        totals[0],
        totals[1],
        totals[2],
        totals[3],
        vectors[0],
        vectors[1],
        vectors[2],
        totals[4],
        totals[5],
        totals[6],
        vectors[3],
        vectors[4],
        vectors[5],
    )


VMEM_LIMIT = 66_000_000
EXTRA = 16


def mm(left, right):
    return lax.dot_general(left, right, (((1,), (0,)), ((), ())), preferred_element_type=f32)


def mm_nt(left, right):
    return lax.dot_general(left, right, (((1,), (1,)), ((), ())), preferred_element_type=f32)


def mm_tn(left, right):
    return lax.dot_general(left, right, (((0,), (0,)), ((), ())), preferred_element_type=f32)


def kernel_params(limit=VMEM_LIMIT):
    return pltpu.CompilerParams(vmem_limit_bytes=limit)


def cost(flops, size):
    return pl.CostEstimate(flops=int(flops), bytes_accessed=int(size), transcendentals=0)


def in_vmem():
    return pl.BlockSpec(memory_space=pltpu.VMEM)


def aligned(start, size, by):
    return pl.ds(pl.multiple_of(start * size, by), size)


def pack_qkv_kernel(pos_ref, weight_ref, query_b_ref, value_b_ref, packed_ref, own_b_ref):
    half = weight_ref.shape[0]
    wide = query_b_ref.shape[0] // 2
    query_b, value_b = (ref[...].reshape(1, 2 * wide) for ref in (query_b_ref, value_b_ref))
    packed_ref[:half] = weight_ref[...]
    packed_ref[half:] = jnp.zeros_like(packed_ref[half:])
    own_b_ref[...] = jnp.zeros_like(own_b_ref)
    parity = lax.rem(pos_ref[0], 2)
    for k in range(2):
        cols = slice(k * wide, (k + 1) * wide)
        own_b_ref[k * EXTRA : k * EXTRA + 1, :wide] = query_b[:, cols]
        own_b_ref[k * EXTRA : k * EXTRA + 1, wide : 2 * wide] = value_b[:, cols]

        @pl.when(parity == k)
        def _():
            packed_ref[half : half + 1, :wide] = query_b[:, cols]
            packed_ref[half : half + 1, wide : 2 * wide] = value_b[:, cols]


def pack_qkv(pos, weight, query_b, value_b):
    rows, width = weight.shape
    half = rows // 2
    small = pl.BlockSpec(query_b.shape, lambda i, pos: (0,))
    return pl.pallas_call(
        pack_qkv_kernel,
        grid_spec=pltpu.PrefetchScalarGridSpec(
            num_scalar_prefetch=1,
            grid=(1,),
            in_specs=[pl.BlockSpec((half, width), lambda i, pos: (lax.rem(pos[0], 2), 0)), small, small],
            out_specs=[
                pl.BlockSpec((half + EXTRA, width), lambda i, pos: (0, 0)),
                pl.BlockSpec((2 * EXTRA, width), lambda i, pos: (0, 0)),
            ],
        ),
        out_shape=[
            jax.ShapeDtypeStruct((half + EXTRA, width), bf16),
            jax.ShapeDtypeStruct((2 * EXTRA, width), bf16),
        ],
        compiler_params=kernel_params(),
        cost_estimate=cost(0, 1 << 20),
        name="pack_qkv",
    )(pos, weight, query_b, value_b)


def pack_mlp_kernel(pos_ref, proj_ref, down_ref, up_ref, up_b_ref, *refs):
    vec_refs, packed_ref, vecs_ref = refs[:-2], refs[-2], refs[-1]
    width = proj_ref.shape[1]
    at = 0
    for value in (proj_ref[...], down_ref[...]):
        packed_ref[at : at + value.shape[0]] = value
        at += value.shape[0]
    blocks = up_ref.shape[1] // width
    for j in range(blocks):
        packed_ref[at : at + up_ref.shape[0]] = up_ref[:, j * width : (j + 1) * width]
        at += up_ref.shape[0]
    packed_ref[at:] = jnp.zeros_like(packed_ref[at:])
    vecs_ref[...] = jnp.zeros_like(vecs_ref)
    for j in range(blocks):
        row = up_b_ref[j * width : (j + 1) * width].reshape(1, width)
        packed_ref[at + j : at + j + 1] = row
        vecs_ref[8 + j : 9 + j] = row.astype(f32)
    for k, ref in enumerate(vec_refs):
        vecs_ref[k : k + 1] = ref[...].reshape(1, width).astype(f32)


def pack_mlp(pos, proj, down, up, up_b, vectors):
    width, hidden = up.shape
    rows = (proj.shape[0] + 2 * hidden) // 2 + EXTRA

    def half(array):
        return pl.BlockSpec((array.shape[0] // 2, array.shape[1]), lambda i, pos: (lax.rem(pos[0], 2), 0))

    def whole(array):
        return pl.BlockSpec(array.shape, lambda i, pos: (0,))

    return pl.pallas_call(
        pack_mlp_kernel,
        grid_spec=pltpu.PrefetchScalarGridSpec(
            num_scalar_prefetch=1,
            grid=(1,),
            in_specs=[half(proj), half(down), half(up), whole(up_b)] + [whole(v) for v in vectors],
            out_specs=[
                pl.BlockSpec((rows, width), lambda i, pos: (0, 0)),
                pl.BlockSpec((EXTRA, width), lambda i, pos: (0, 0)),
            ],
        ),
        out_shape=[jax.ShapeDtypeStruct((rows, width), bf16), jax.ShapeDtypeStruct((EXTRA, width), f32)],
        compiler_params=kernel_params(),
        cost_estimate=cost(0, 3 << 20),
        name="pack_mlp",
    )(pos, proj, down, up, up_b, *vectors)


def attn_fwd_kernel(pos_ref, x_ref, *refs, heads, q_block, fetched):
    packed_ref, probs_ref, ctx_ref, mixed_ref, key_ref, score_a, score_b = refs[-7:]
    seq = x_ref.shape[0]
    scale = HEAD_DIM**-0.5
    wide = heads * HEAD_DIM
    part = heads * PART_ROWS
    if fetched:
        near = pl.program_id(1) == 0
        weight = jnp.where(near, refs[0][:part], refs[1][:part])
        bias = jnp.where(near, refs[0][part:].astype(f32), refs[1][part:].astype(f32))
    else:
        weight, bias = refs[0][...], refs[1][...].astype(f32)
    column = bias[:8, : 2 * wide].T
    raw = mm_nt(weight, x_ref[...])
    for h in range(heads):
        base = h * PART_ROWS
        ends = (base + HEAD_DIM, base + 2 * HEAD_DIM, base + PART_ROWS)
        query = raw[base : ends[0]] + column[h * HEAD_DIM : (h + 1) * HEAD_DIM, :1]
        value = raw[ends[1] : ends[2]] + column[wide + h * HEAD_DIM : wide + (h + 1) * HEAD_DIM, :1]
        packed_ref[0, 0, base : ends[0]] = query.astype(bf16)
        packed_ref[0, 0, ends[0] : ends[1]] = raw[ends[0] : ends[1]].astype(bf16)
        packed_ref[0, 0, ends[1] : ends[2]] = value.astype(bf16)
        keys = packed_ref[0, 0, ends[0] : ends[1], :].astype(f32)
        key_ref[h] = (keys.T * scale).astype(bf16)
    tiles = [(h, c) for h in range(heads) for c in range(0, seq, q_block)]
    scores = (score_a, score_b)

    def score(tile, ref):
        h, c = tile
        base = h * PART_ROWS
        ref[...] = mm(key_ref[h], packed_ref[0, 0, base : base + HEAD_DIM, c : c + q_block])

    def finish(tile, ref):
        h, c = tile
        base = h * PART_ROWS
        top = jnp.max(ref[...], axis=0, keepdims=True)
        exponent = jnp.exp(ref[...] - top)
        total = jnp.sum(exponent, axis=0, keepdims=True)
        probs = (exponent * (1.0 / total)).astype(bf16)
        probs_ref[0, 0, h, :, c : c + q_block] = probs
        mixed = mm(packed_ref[0, 0, base + 2 * HEAD_DIM : base + 3 * HEAD_DIM, :], probs)
        ctx_ref[0, 0, h * HEAD_DIM : (h + 1) * HEAD_DIM, c : c + q_block] = mixed.astype(bf16)
        mixed_ref[0, 0, h * HEAD_DIM : (h + 1) * HEAD_DIM, c : c + q_block] = mixed

    score(tiles[0], scores[0])
    for j, tile in enumerate(tiles):
        if j + 1 < len(tiles):
            score(tiles[j + 1], scores[(j + 1) % 2])
        finish(tile, scores[j % 2])


def attn_fwd(pos, x, sources, shard, fetched, shapes, earlier):
    rows, width = x.shape
    n_seq = rows // SEQ_LEN
    heads = shapes[1].shape[2] // 2
    part = heads * PART_ROWS

    def at(k, pos):
        return lax.bitwise_xor(k, lax.rem(pos[0], 2)) if fetched else k

    if fetched:
        sizes = [pl.BlockSpec(v.shape, lambda s, k, pos: (0, 0), pipeline_mode=pl.Buffered(1)) for v in sources]
    else:
        sizes = [pl.BlockSpec((size, width), lambda s, k, pos: (k, 0)) for size in (part, EXTRA)]
    out_specs = [
        pl.BlockSpec((1, 1, part, SEQ_LEN), lambda s, k, pos: (shard, s, at(k, pos), 0)),
        pl.BlockSpec((1, 1, heads, SEQ_LEN, SEQ_LEN), lambda s, k, pos: (shard, s, at(k, pos), 0, 0)),
    ] + [pl.BlockSpec((1, 1, heads * HEAD_DIM, SEQ_LEN), lambda s, k, pos: (shard, s, at(k, pos), 0))] * 2
    q_block = 512
    share = 2 * n_seq * heads
    flops = share * (2 * SEQ_LEN * width * PART_ROWS + 4 * SEQ_LEN * SEQ_LEN * HEAD_DIM * 6)
    return pl.pallas_call(
        partial(attn_fwd_kernel, heads=heads, q_block=q_block, fetched=fetched),
        grid_spec=pltpu.PrefetchScalarGridSpec(
            num_scalar_prefetch=1,
            grid=(n_seq, 2),
            in_specs=[pl.BlockSpec((SEQ_LEN, width), lambda s, k, pos: (s, 0))]
            + sizes
            + [pl.BlockSpec(memory_space=pl.ANY)] * len(earlier),
            out_specs=out_specs,
            scratch_shapes=[
                pltpu.VMEM((heads, SEQ_LEN, HEAD_DIM), bf16),
                pltpu.VMEM((SEQ_LEN, q_block), f32),
                pltpu.VMEM((SEQ_LEN, q_block), f32),
            ],
        ),
        out_shape=shapes,
        input_output_aliases={4 + k: k for k in range(len(earlier))},
        compiler_params=kernel_params(),
        cost_estimate=cost(flops // 8 if fetched else flops, share * 3 << 20),
        name="attn_fwd",
    )(pos, x, *sources, *earlier)


def piece_bits(*order):
    bits = [0]
    for bit in reversed(order):
        bits = bits + [b | bit for b in bits]
    return bits


MLP_SLOTS = 8
DOWN_ORDER = ("tensor", 2, 4)
UP_ORDER = (4, "tensor", 2)
DOWN_BITS = piece_bits(1, 2, 4)
UP_BITS = piece_bits(1, 4, 2)


def middle_kernel(
    pos_ref,
    x_ref,
    og_ref,
    ctx_ref,
    vecs_ref,
    proj_own,
    up_own,
    down_own,
    *refs,
    n_others,
    chunk,
):
    fetched, refs = refs[: 2 * n_others], refs[2 * n_others :]
    out_ref, grad_one_ref, ctx_low_ref, dn_keep_ref, dn_send_ref, up_keep_ref, up_send_ref, *refs = refs
    proj_got, up_got, down_got, up_b_ref, act_ref, slope_ref, proj_acc, up_acc, dn_acc, vec_acc, up_b_acc = refs
    step = pl.program_id(0)
    n_shards = n_others + 1
    ctx_rows, width = proj_own.shape
    hidden = up_own.shape[1]
    blocks = hidden // width
    inv_width = 1.0 / width

    def mean(v):
        return jnp.sum(v, axis=1, keepdims=True) * inv_width

    @pl.when(step == 0)
    def _():
        for ref in (proj_acc, up_acc, dn_acc):
            size = min(64, ref.shape[1])

            def clear(i, carry, ref=ref, size=size):
                for t in range(n_shards):
                    ref[t, aligned(i, size, size), :] = jnp.zeros((size, ref.shape[2]), f32)
                return carry

            lax.fori_loop(0, ref.shape[1] // size, clear, 0)
        for ref in (vec_acc, up_b_acc):
            ref[...] = jnp.zeros_like(ref)
        parity = lax.rem(pos_ref[0], 2)
        for j in range(blocks):
            up_b_ref[:, j * width : (j + 1) * width] = vecs_ref[8 + j : 9 + j, :]
        for t in range(n_others):
            for k in range(2):
                ref = fetched[2 * t + k]
                side = parity if k == 0 else 1 - parity
                rows = ctx_rows // 2
                proj_got[t, aligned(side, rows, rows), :] = ref[:rows]
                at = rows
                rows = hidden // 2
                down_got[t, aligned(side, rows, rows), :] = ref[at : at + rows]
                at += rows
                rows = width // 2
                for j in range(blocks):
                    up_got[t, aligned(side, rows, rows), j * width : (j + 1) * width] = ref[at : at + rows]
                    at += rows
                if k == 0:
                    for j in range(blocks):
                        to = (t + 1) * hidden + j * width
                        up_b_ref[:, to : to + width] = ref[at : at + EXTRA].astype(f32)[j : j + 1]

    def proj(t):
        return proj_own[...] if t == 0 else proj_got[t - 1]

    def up(t, c):
        return up_own[:, c : c + chunk] if t == 0 else up_got[t - 1, :, c : c + chunk]

    def down(t, c):
        return down_own[c : c + chunk, :] if t == 0 else down_got[t - 1, c : c + chunk, :]

    proj_b, gain_one, shift_one, down_b, gain_two, shift_two = (vecs_ref[k : k + 1, :] for k in range(6))
    branch = proj_b
    for t in range(n_shards):
        branch = branch + mm_tn(ctx_ref[t, 0], proj(t))
    mid_sum = x_ref[...].astype(f32) + branch
    center = mean(mid_sum)
    inv_one = lax.rsqrt(mean(mid_sum * mid_sum) - center * center + norm_eps)
    normal_one = (mid_sum - center) * inv_one
    normed_one = normal_one * gain_one + shift_one
    normed_low = normed_one.astype(bf16)
    second = down_b
    chunks = [(t, c) for t in range(n_shards) for c in range(0, hidden, chunk)]
    for t, c in chunks:
        at = t * hidden + c
        inner = mm(normed_low, up(t, c)) + up_b_ref[:, at : at + chunk]
        phi = 0.5 * lax.erf(inner * 0.7071067811865476) + 0.5
        active = (inner * phi).astype(bf16)
        act_ref[:, at : at + chunk] = active
        slope_ref[:, at : at + chunk] = phi + inner * (0.3989422804014327 * jnp.exp(-0.5 * inner * inner))
        second = second + mm(active, down(t, c))
    last_sum = normed_one + second
    center_two = mean(last_sum)
    inv_two = lax.rsqrt(mean(last_sum * last_sum) - center_two * center_two + norm_eps)
    normal_two = (last_sum - center_two) * inv_two
    out_ref[...] = (normal_two * gain_two + shift_two).astype(bf16)
    upstream = og_ref[...].astype(f32)
    scaled = upstream * gain_two
    grad_two = inv_two * (scaled - mean(scaled) - normal_two * mean(scaled * normal_two))
    second_low = grad_two.astype(bf16)
    normed_t = normed_low.T
    back = None
    for t, c in chunks:
        at = t * hidden + c
        grad_active = mm_nt(second_low, down(t, c))
        inner_low = (grad_active * slope_ref[:, at : at + chunk]).astype(bf16)
        up_b_acc[:, at : at + chunk] += jnp.sum(inner_low.astype(f32), axis=0, keepdims=True)
        part = mm_nt(inner_low, up(t, c))
        back = part if back is None else back + part
        up_acc[t, :, c : c + chunk] += mm(normed_t, inner_low)
        dn_acc[t, c : c + chunk, :] += mm_tn(act_ref[:, at : at + chunk], second_low)
    grad_mid = grad_two + back
    scaled_one = grad_mid * gain_one
    grad_one = inv_one * (scaled_one - mean(scaled_one) - normal_one * mean(scaled_one * normal_one))
    grad_one_ref[...] = grad_one
    branch_low = grad_one.astype(bf16)
    sums = (
        branch_low.astype(f32),
        grad_mid * normal_one,
        grad_mid,
        second_low.astype(f32),
        upstream * normal_two,
        upstream,
    )
    for k, value in enumerate(sums):
        vec_acc[k : k + 1, :] += jnp.sum(value, axis=0, keepdims=True)
    for t in range(n_shards):
        ctx_low_ref[t, 0] = mm_nt(proj(t), branch_low).astype(bf16)
        proj_acc[t] += mm(ctx_ref[t, 0], branch_low)

    @pl.when(step == pl.num_programs(0) - 1)
    def _():
        low = lax.rem(pos_ref[0], MLP_SLOTS)
        dn_rows, up_rows, proj_rows = hidden // MLP_SLOTS, width // MLP_SLOTS, ctx_rows // MLP_SLOTS
        half = MLP_SLOTS // 2
        for slot in range(MLP_SLOTS):
            dn_ref = dn_keep_ref if slot < half else dn_send_ref
            upk_ref = up_keep_ref if slot < half else up_send_ref
            k = slot % half
            dn_at = lax.bitwise_xor(low, DOWN_BITS[slot])
            rows = aligned(lax.bitwise_xor(low, UP_BITS[slot]), up_rows, up_rows)
            for t in range(n_shards):
                dn_ref[t, k, :dn_rows] = dn_acc[t, aligned(dn_at, dn_rows, dn_rows), :].astype(bf16)
                dn_ref[t, k, dn_rows:] = proj_acc[t, aligned(dn_at, proj_rows, proj_rows), :].astype(bf16)
                for j in range(blocks):
                    to = j * up_rows
                    upk_ref[t, k, to : to + up_rows] = up_acc[t, rows, j * width : (j + 1) * width].astype(bf16)
                to = blocks * up_rows
                upk_ref[t, k, to : to + 8] = vec_acc[...].astype(bf16)
                tail = [
                    up_b_acc[:, t * hidden + j * width : t * hidden + (j + 1) * width] for j in range(blocks)
                ]
                tail.append(jnp.zeros((8 - blocks, width), f32))
                upk_ref[t, k, to + 8 : to + EXTRA] = jnp.concatenate(tail, axis=0).astype(bf16)


def middle(pos, x, out_grad, ctx, vecs, proj, up, down, fetched):
    rows, width = x.shape
    n_shards, n_seq, ctx_rows, _ = ctx.shape
    hidden = up.shape[1]
    n_others = n_shards - 1
    block = 512
    per_seq = SEQ_LEN // block
    half = MLP_SLOTS // 2
    dn_rows, up_rows = (hidden + ctx_rows) // MLP_SLOTS, hidden // MLP_SLOTS + EXTRA

    def whole(array):
        return pl.BlockSpec(array.shape, lambda i, pos: (0,) * array.ndim, pipeline_mode=pl.Buffered(1))

    def kept(*shape):
        return pl.BlockSpec(shape, lambda i, pos: (0,) * len(shape))

    row = pl.BlockSpec((block, width), lambda i, pos: (i, 0))
    cols = pl.BlockSpec((n_shards, 1, ctx_rows, block), lambda i, pos: (0, i // per_seq, 0, i % per_seq))
    dn_shape, up_shape = (n_shards, half, dn_rows, width), (n_shards, half, up_rows, width)
    consts = [vecs, proj, up, down] + fetched
    return pl.pallas_call(
        partial(middle_kernel, n_others=n_others, chunk=min(1024, hidden)),
        grid_spec=pltpu.PrefetchScalarGridSpec(
            num_scalar_prefetch=1,
            grid=(rows // block,),
            in_specs=[row, row, cols] + [whole(array) for array in consts],
            out_specs=[row, row, cols, kept(*dn_shape), kept(*dn_shape), kept(*up_shape), kept(*up_shape)],
            scratch_shapes=[
                pltpu.VMEM((n_others, ctx_rows, width), bf16),
                pltpu.VMEM((n_others, width, hidden), bf16),
                pltpu.VMEM((n_others, hidden, width), bf16),
                pltpu.VMEM((1, n_shards * hidden), f32),
                pltpu.VMEM((block, n_shards * hidden), bf16),
                pltpu.VMEM((block, n_shards * hidden), f32),
                pltpu.VMEM((n_shards, ctx_rows, width), f32),
                pltpu.VMEM((n_shards, width, hidden), f32),
                pltpu.VMEM((n_shards, hidden, width), f32),
                pltpu.VMEM((8, width), f32),
                pltpu.VMEM((1, n_shards * hidden), f32),
            ],
        ),
        out_shape=[
            jax.ShapeDtypeStruct((rows, width), bf16),
            jax.ShapeDtypeStruct((rows, width), f32),
            jax.ShapeDtypeStruct(ctx.shape, bf16),
            jax.ShapeDtypeStruct(dn_shape, bf16),
            jax.ShapeDtypeStruct(dn_shape, bf16),
            jax.ShapeDtypeStruct(up_shape, bf16),
            jax.ShapeDtypeStruct(up_shape, bf16),
        ],
        compiler_params=kernel_params(),
        cost_estimate=cost(30 << 30, 30 << 20),
        name="middle",
    )(pos, x, out_grad, ctx, *consts)


def piece_number(pos, slot, cut):
    number = 0
    for k, bit in enumerate(cut):
        own = lax.bitwise_and(lax.shift_right_logical(pos, bit.bit_length() - 1), 1)
        flip = (slot >> (len(cut) - 1 - k)) & 1
        number = number + (lax.bitwise_xor(own, flip) << k)
    return number


def attn_bwd_kernel(
    pos_ref,
    x_ref,
    packed_ref,
    probs_ref,
    ctx_low_ref,
    mixed_ref,
    sums_ref,
    *refs,
    head,
    cut,
    extra,
    unroll,
):
    grad_ref, keep_ref, send_ref, bias_ref, value_ref, weight_acc = refs[-6:]
    step = pl.program_id(0)
    seq = x_ref.shape[0]
    n_shards = packed_ref.shape[0]
    scale = HEAD_DIM**-0.5
    for t in range(n_shards):
        value_ref[t] = packed_ref[t, 0, 2 * HEAD_DIM : 3 * HEAD_DIM, :].T
    def one_shard(t, carry):
        ctx_low = ctx_low_ref[t, 0]
        total = jnp.sum(ctx_low.astype(f32) * mixed_ref[t, 0], axis=0, keepdims=True)
        probs = probs_ref[t, 0, 0]
        score_low = (probs.astype(f32) * (mm(value_ref[t], ctx_low) - total)).astype(bf16)
        grad_query = mm(packed_ref[t, 0, HEAD_DIM : 2 * HEAD_DIM, :], score_low) * scale
        grad_key = mm_nt(score_low, packed_ref[t, 0, :HEAD_DIM, :]) * scale
        grad_value = mm_nt(probs, ctx_low)
        grad_ref[t, 0, :HEAD_DIM, :] = grad_query.astype(bf16)
        grad_ref[t, 0, HEAD_DIM : 2 * HEAD_DIM, :] = grad_key.T.astype(bf16)
        grad_ref[t, 0, 2 * HEAD_DIM :, :] = grad_value.T.astype(bf16)
        return carry

    if unroll:
        for t in range(n_shards):
            one_shard(t, 0)
    else:
        lax.fori_loop(0, n_shards, one_shard, 0)

    @pl.when(step == 0)
    def _():
        weight_acc[...] = jnp.zeros_like(weight_acc)
        bias_ref[...] = sums_ref[...]

    ones = jnp.ones((8, seq), bf16)
    for t in range(n_shards):
        weight_acc[t] += mm(grad_ref[t, 0], x_ref[...])
        bias_ref[t, head : head + 1] += mm_nt(ones, grad_ref[t, 0])[:1]

    @pl.when(step == pl.num_programs(0) - 1)
    def _():
        slots = 1 << len(cut)
        half = slots // 2
        rows = PART_ROWS // slots
        for slot in range(slots):
            at = piece_number(pos_ref[0], slot, cut)
            ref = keep_ref if slot < half else send_ref
            for t in range(n_shards):
                ref[t, slot % half, :rows] = weight_acc[t, aligned(at, rows, 8), :].astype(bf16)
                if extra:
                    padded = jnp.concatenate(
                        [bias_ref[t], jnp.zeros((EXTRA, ref.shape[3] - PART_ROWS), f32)], axis=1
                    )
                    ref[t, slot % half, rows:] = padded.astype(bf16)


def attn_bwd(pos, x, packed, probs, ctx_low, mixed, sums, head, first, group, cut, extra, unroll, earlier):
    rows, width = x.shape
    n_shards, n_seq = packed.shape[:2]
    slots = 1 << len(cut)
    each = PART_ROWS // slots + (EXTRA if extra else 0)
    pieces = (n_shards, slots // 2, group * each, width)
    piece = pl.BlockSpec((n_shards, slots // 2, each, width), lambda s, pos: (0, 0, head - first, 0))
    sum_spec = pl.BlockSpec(sums.shape, lambda s, pos: (0, 0, 0))
    return pl.pallas_call(
        partial(attn_bwd_kernel, head=head, cut=cut, extra=extra, unroll=unroll),
        grid_spec=pltpu.PrefetchScalarGridSpec(
            num_scalar_prefetch=1,
            grid=(n_seq,),
            in_specs=[
                pl.BlockSpec((SEQ_LEN, width), lambda s, pos: (s, 0)),
                pl.BlockSpec((n_shards, 1, PART_ROWS, SEQ_LEN), lambda s, pos: (0, s, head, 0)),
                pl.BlockSpec((n_shards, 1, 1, SEQ_LEN, SEQ_LEN), lambda s, pos: (0, s, head, 0, 0)),
                pl.BlockSpec((n_shards, 1, HEAD_DIM, SEQ_LEN), lambda s, pos: (0, s, head, 0)),
                pl.BlockSpec((n_shards, 1, HEAD_DIM, SEQ_LEN), lambda s, pos: (0, s, head, 0)),
                sum_spec,
            ]
            + [pl.BlockSpec(memory_space=pl.ANY)] * len(earlier),
            out_specs=[
                pl.BlockSpec((n_shards, 1, PART_ROWS, SEQ_LEN), lambda s, pos: (0, s, 0, 0)),
                piece,
                piece,
                sum_spec,
            ],
            scratch_shapes=[
                pltpu.VMEM((n_shards, SEQ_LEN, HEAD_DIM), bf16),
                pltpu.VMEM((n_shards, PART_ROWS, width), f32),
            ],
        ),
        out_shape=[
            jax.ShapeDtypeStruct((n_shards, n_seq, PART_ROWS, SEQ_LEN), bf16),
            jax.ShapeDtypeStruct(pieces, bf16),
            jax.ShapeDtypeStruct(pieces, bf16),
            jax.ShapeDtypeStruct(sums.shape, f32),
        ],
        input_output_aliases={7: 1, 8: 2} if earlier else {},
        compiler_params=kernel_params(48_000_000),
        cost_estimate=cost(8 << 30, 10 << 20),
        name="attn_bwd",
    )(pos, x, packed, probs, ctx_low, mixed, sums, *earlier)


def input_grad_kernel(pos_ref, grad_one_ref, own_ref, *refs, n_others):
    fetched, grads, out_ref, got_ref = refs[: 2 * n_others], refs[2 * n_others : -2], refs[-2], refs[-1]
    half = own_ref.shape[0] // 2

    @pl.when(pl.program_id(0) == 0)
    def _():
        parity = lax.rem(pos_ref[0], 2)
        for t in range(n_others):
            for k in range(2):
                side = parity if k == 0 else 1 - parity
                got_ref[t, aligned(side, half, half), :] = fetched[2 * t + k][:half]

    total = grad_one_ref[...]
    for t in range(n_others + 1):
        weight = own_ref if t == 0 else got_ref.at[t - 1]
        for head, ref in enumerate(grads):
            total = total + mm_tn(ref[t, 0], weight[head * PART_ROWS : (head + 1) * PART_ROWS, :])
    out_ref[...] = total.astype(bf16)


def input_gradient(pos, grad_one, own, fetched, packed_grads):
    rows, width = grad_one.shape
    n_shards = packed_grads[0].shape[0]
    block = 512
    per_seq = SEQ_LEN // block
    row = pl.BlockSpec((block, width), lambda i, pos: (i, 0))
    cols = pl.BlockSpec((n_shards, 1, PART_ROWS, block), lambda i, pos: (0, i // per_seq, 0, i % per_seq))

    def whole(array):
        return pl.BlockSpec(array.shape, lambda i, pos: (0, 0), pipeline_mode=pl.Buffered(1))

    return pl.pallas_call(
        partial(input_grad_kernel, n_others=n_shards - 1),
        grid_spec=pltpu.PrefetchScalarGridSpec(
            num_scalar_prefetch=1,
            grid=(rows // block,),
            in_specs=[row, whole(own)] + [whole(v) for v in fetched] + [cols] * len(packed_grads),
            out_specs=row,
            scratch_shapes=[pltpu.VMEM((n_shards - 1,) + own.shape, bf16)],
        ),
        out_shape=jax.ShapeDtypeStruct((rows, width), bf16),
        compiler_params=kernel_params(48_000_000),
        cost_estimate=cost(4 << 30, 12 << 20),
        name="input_gradient",
    )(pos, grad_one, own, *fetched, *packed_grads)


def mlp_place_kernel(pos_ref, dn_near, dn_far, up_near, up_far, proj_out, up_out, dn_out):
    low = lax.rem(pos_ref[0], MLP_SLOTS)
    half = MLP_SLOTS // 2
    width = proj_out.shape[1]
    hidden = dn_out.shape[0]
    dn_rows, up_rows, proj_rows = hidden // MLP_SLOTS, width // MLP_SLOTS, proj_out.shape[0] // MLP_SLOTS
    for slot in range(MLP_SLOTS):
        dn_ref = dn_near if slot < half else dn_far
        up_ref = up_near if slot < half else up_far
        k = slot % half
        at = lax.bitwise_xor(low, DOWN_BITS[slot])
        dn_out[aligned(at, dn_rows, dn_rows), :] = dn_ref[k, :dn_rows].astype(f32)
        proj_out[aligned(at, proj_rows, proj_rows), :] = dn_ref[k, dn_rows:].astype(f32)
        rows = aligned(lax.bitwise_xor(low, UP_BITS[slot]), up_rows, up_rows)
        for j in range(hidden // width):
            up_out[rows, j * width : (j + 1) * width] = up_ref[k, j * up_rows : (j + 1) * up_rows].astype(f32)


def mlp_place(pos, dn_parts, up_parts, ctx_rows, width, hidden):
    return pl.pallas_call(
        mlp_place_kernel,
        in_specs=[pl.BlockSpec(memory_space=pltpu.SMEM)] + [in_vmem()] * 4,
        out_specs=[in_vmem()] * 3,
        out_shape=[
            jax.ShapeDtypeStruct((ctx_rows, width), f32),
            jax.ShapeDtypeStruct((width, hidden), f32),
            jax.ShapeDtypeStruct((hidden, width), f32),
        ],
        compiler_params=kernel_params(48_000_000),
        cost_estimate=cost(0, 14 << 20),
        name="mlp_place",
    )(pos, *dn_parts, *up_parts)


def qkv_place_kernel(pos_ref, *refs, groups):
    bias_ref, out_ref, query_ref, value_ref = refs[-4:]
    for g, (first, group, cut, each) in enumerate(groups):
        slots = 1 << len(cut)
        half = slots // 2
        rows = PART_ROWS // slots
        for slot in range(slots):
            at = aligned(piece_number(pos_ref[0], slot, cut), rows, 8)
            for k in range(group):
                value = refs[2 * g + slot // half][slot % half, k * each : k * each + rows]
                out_ref[first + k, at, :] = value.astype(f32)
    heads = out_ref.shape[0]
    for k, ref in ((0, query_ref), (2, value_ref)):
        parts = [bias_ref[h : h + 1, k * HEAD_DIM : (k + 1) * HEAD_DIM] for h in range(heads)]
        ref[...] = jnp.concatenate(parts, axis=1).reshape(heads * HEAD_DIM)


def qkv_place(pos, parts, bias, groups, heads):
    flat = [half for pair in parts for half in pair]
    vector = jax.ShapeDtypeStruct((heads * HEAD_DIM,), f32)
    return pl.pallas_call(
        partial(qkv_place_kernel, groups=groups),
        in_specs=[pl.BlockSpec(memory_space=pltpu.SMEM)] + [in_vmem()] * (len(flat) + 1),
        out_specs=[in_vmem()] * 3,
        out_shape=[jax.ShapeDtypeStruct((heads, PART_ROWS, flat[0].shape[2]), f32), vector, vector],
        compiler_params=kernel_params(48_000_000),
        cost_estimate=cost(0, 3 << 20),
        name="qkv_place",
    )(pos, *flat, bias)


def swap_dp(value, bits, n_dp):
    return lax.ppermute(value, "dp", [(i, i ^ bits) for i in range(n_dp)])


def shift_tensor(value, by, n_tensor):
    return lax.ppermute(value, "tensor", [((i + by) % n_tensor, i) for i in range(n_tensor)])


def reduce_pieces(keep, send, order, n_dp, n_tensor):
    halved = [axis for axis in order if axis != "tensor"]
    got = swap_dp(send, 1, n_dp)
    got = after(got, (yield send))
    parts = [keep[t].astype(f32) + got[t].astype(f32) for t in range(n_tensor)]
    for axis in order:
        if axis == "tensor":
            outs = [parts[by].astype(bf16) for by in range(1, n_tensor)]
            gots = [shift_tensor(out, -by, n_tensor) for by, out in enumerate(outs, 1)]
            gots = after(gots, (yield outs))
            parts = [sum((got.astype(f32) for got in gots), parts[0])]
        else:
            cut = parts[0].shape[0] // 2
            out = jnp.stack([part[cut:].astype(bf16) for part in parts])
            got = swap_dp(out, axis, n_dp)
            got = after(got, (yield out))
            parts = [part[:cut] + got[t].astype(f32) for t, part in enumerate(parts)]
    own = parts[0]
    bits = 2
    while bits < n_dp:
        if bits not in halved:
            out = own.astype(bf16)
            got = swap_dp(out, bits, n_dp)
            got = after(got, (yield out))
            own = own + got.astype(f32)
        bits *= 2
    near = own.astype(bf16)
    for axis in reversed(halved):
        got = swap_dp(near, axis, n_dp)
        got = after(got, (yield near))
        near = jnp.concatenate([near, got], axis=0)
    got = swap_dp(near, 1, n_dp)
    got = after(got, (yield near))
    return near, got, own


class Sums:
    def __init__(self):
        self.live, self.done, self.fresh = {}, {}, set()

    def add(self, name, generator):
        self.live[name] = generator
        self.fresh.add(name)

    def step(self, ready, *names):
        sent = []
        for name in names:
            if name in self.live:
                try:
                    sent.append(self.live[name].send(None if name in self.fresh else ready))
                    self.fresh.discard(name)
                except StopIteration as stop:
                    self.done[name] = stop.value
                    del self.live[name]
        return sent

    def finish(self):
        while self.live:
            self.step((), *list(self.live))


def after(value, *others):
    return lax.optimization_barrier((value, others))[0]


def sequence_body(n_dp, n_tensor, *arrays):
    (
        layer_input,
        output_grad,
        qkv_weight,
        query_bias,
        value_bias,
        proj_weight,
        proj_bias,
        first_gain,
        first_shift,
        up_weight,
        up_bias,
        down_weight,
        down_bias,
        second_gain,
        second_shift,
    ) = arrays
    rows, width = layer_input.shape
    n_seq = rows // SEQ_LEN
    ctx_rows, hidden = proj_weight.shape[0], up_weight.shape[1]
    n_heads = ctx_rows // HEAD_DIM
    pos = lax.axis_index("dp").astype(jnp.int32).reshape(1)
    shifts = range(1, n_tensor)

    qkv_half, own_bias = pack_qkv(pos, qkv_weight, query_bias, value_bias)
    qkv_near = [shift_tensor(qkv_half, by, n_tensor) for by in shifts]
    vectors = [proj_bias, first_gain, first_shift, down_bias, second_gain, second_shift]
    mlp_half, vecs = pack_mlp(after(pos, qkv_half), proj_weight, down_weight, up_weight, up_bias, vectors)
    shapes = [
        jax.ShapeDtypeStruct((n_tensor, n_seq, n_heads * PART_ROWS, SEQ_LEN), bf16),
        jax.ShapeDtypeStruct((n_tensor, n_seq, n_heads, SEQ_LEN, SEQ_LEN), bf16),
        jax.ShapeDtypeStruct((n_tensor, n_seq, n_heads * HEAD_DIM, SEQ_LEN), bf16),
        jax.ShapeDtypeStruct((n_tensor, n_seq, n_heads * HEAD_DIM, SEQ_LEN), f32),
    ]
    mlp_near = [shift_tensor(mlp_half, by, n_tensor) for by in shifts]
    x = after(layer_input, mlp_half)
    stacks = attn_fwd(pos, x, (qkv_weight, own_bias), 0, False, shapes, ())
    qkv_near = after(qkv_near, stacks[2])
    qkv_far = [swap_dp(near, 1, n_dp) for near in qkv_near]
    for t in shifts:
        stacks = attn_fwd(pos, layer_input, (qkv_near[t - 1], qkv_far[t - 1]), t, True, shapes, stacks)
    packed, probs, ctx, mixed = stacks
    mlp_near = after(mlp_near, ctx)
    mlp_far = [swap_dp(near, 1, n_dp) for near in mlp_near]
    fetched = [half for pair in zip(mlp_near, mlp_far) for half in pair]
    result, grad_one, ctx_low, dn_keep, dn_send, up_keep, up_send = middle(
        pos, layer_input, output_grad, ctx, vecs, proj_weight, up_weight, down_weight, fetched
    )
    sums = Sums()
    sums.add("dn", reduce_pieces(dn_keep, dn_send, DOWN_ORDER, n_dp, n_tensor))
    sums.add("up", reduce_pieces(up_keep, up_send, UP_ORDER, n_dp, n_tensor))
    bias_sums = jnp.zeros((n_tensor, EXTRA, PART_ROWS), f32)
    packed_grads = []
    ready = ()
    early = n_heads - 1
    stacked = ()
    early_cut, early_order = (1, 2), ("tensor", 2)
    for head in range(n_heads):
        last = head == early
        if last and early:
            sums.add("qa", reduce_pieces(*stacked, early_order, n_dp, n_tensor))
        sent = sums.step(ready, *SCHEDULE[min(head, len(SCHEDULE) - 3)])
        x = after(layer_input, sent)
        grads, keep, send, bias_sums = attn_bwd(
            pos,
            x,
            packed,
            probs,
            ctx_low,
            mixed,
            bias_sums,
            head,
            early if last else 0,
            1 if last else early,
            (1,) if last else early_cut,
            last,
            head in UNROLLED,
            () if last else stacked,
        )
        ready = bias_sums
        packed_grads.append(grads)
        if not last:
            stacked = (keep, send)
    sums.add("qb", reduce_pieces(keep, send, ("tensor",), n_dp, n_tensor))
    sent = sums.step(ready, *SCHEDULE[-2])
    qkv_fetched = [half for pair in zip(qkv_near, qkv_far) for half in pair]
    input_grad = input_gradient(pos, after(grad_one, sent), qkv_weight, qkv_fetched, packed_grads)
    ready = input_grad
    for name in SCHEDULE[-1]:
        sent = sums.step(ready, name)
        ready = sent or ready
    sums.finish()
    dn_near, dn_far, _ = sums.done["dn"]
    up_near, up_far, up_own = sums.done["up"]
    proj_wg, up_wg, dn_wg = mlp_place(pos, (dn_near, dn_far), (up_near, up_far), ctx_rows, width, hidden)
    groups = [(0, early, early_cut, PART_ROWS // 4)] if early else []
    groups.append((early, 1, (1,), PART_ROWS // 2 + EXTRA))
    parts = [sums.done[name][:2] for name in ("qa", "qb") if name in sums.done]
    bias = sums.done["qb"][2][0, -EXTRA:]
    qkv_wg, query_bg, value_bg = qkv_place(pos, parts, bias, groups, n_heads)
    small = up_own[0, -EXTRA:]
    return (
        result,
        input_grad,
        qkv_wg.reshape(n_heads * PART_ROWS, width),
        query_bg,
        value_bg,
        proj_wg,
        small[0],
        small[1],
        small[2],
        up_wg,
        small[8 : 8 + hidden // width].reshape(hidden),
        dn_wg,
        small[3],
        small[4],
        small[5],
    )


SCHEDULE = (
    ("dn", "up"),
    ("dn", "up"),
    ("dn", "up"),
    ("qa", "dn", "up", "qa"),
    ("qb", "qa", "dn", "up", "qb"),
    ("qb", "qa", "dn", "up", "qb", "qa", "up", "dn", "qb", "qa", "up", "dn", "qb", "qa"),
)
UNROLLED = ()


def solution(mesh):
    n_dp, n_tensor = mesh.shape["dp"], mesh.shape["tensor"]

    def body(*arrays):
        rows = arrays[0].shape[0]
        if rows % SEQ_LEN == 0 and n_dp % 8 == 0 and n_dp & (n_dp - 1) == 0:
            return sequence_body(n_dp, n_tensor, *arrays)
        return token_body(*arrays)

    return jax.shard_map(
        body,
        mesh=mesh,
        in_specs=(
            P(("dp", "tensor"), None),
            P(("dp", "tensor"), None),
            P("tensor", None),
            P("tensor"),
            P("tensor"),
            P("tensor", None),
            P(),
            P(),
            P(),
            P(None, "tensor"),
            P("tensor"),
            P("tensor", None),
            P(),
            P(),
            P(),
        ),
        out_specs=(
            P(("dp", "tensor"), None),
            P(("dp", "tensor"), None),
            P("tensor", None),
            P("tensor"),
            P("tensor"),
            P("tensor", None),
            P(),
            P(),
            P(),
            P(None, "tensor"),
            P("tensor"),
            P("tensor", None),
            P(),
            P(),
            P(),
        ),
        check_vma=False,
    )
```

```python
from functools import partial

import jax
import jax.numpy as jnp
from jax import lax
from jax.experimental import pallas as pl
from jax.experimental.pallas import tpu as pltpu
from jax.sharding import PartitionSpec as P

HEAD_DIM = 64
SEQ_LEN = 1024
PART_ROWS = 3 * HEAD_DIM

norm_eps = 1e-05
f32 = jnp.float32
bf16 = jnp.bfloat16


def matmul_rows(left, right):
    return lax.dot_general(
        left, right, (((0,), (0,)), ((), ())), preferred_element_type=jnp.float32
    )


def matmul_back(left, right):
    return lax.dot_general(
        left, right, (((1,), (1,)), ((), ())), preferred_element_type=jnp.float32
    )


def attend_forward(queries, key_rows, value_rows):
    seq_heads = key_rows.shape[0] * key_rows.shape[1]
    head_dim = queries.shape[-1]
    score_scale = head_dim ** (-0.5)
    block_rows = min(512, SEQ_LEN)
    block_count = SEQ_LEN // block_rows
    item_count = seq_heads * block_count
    query_items = queries.reshape(item_count, block_rows, head_dim)
    key_all = key_rows.reshape(seq_heads, SEQ_LEN, head_dim)
    value_all = value_rows.reshape(seq_heads, SEQ_LEN, head_dim)

    def one_block(block_item):
        query_blk, position = block_item
        owner_index = position // block_count
        keys_here = key_all[owner_index]
        values_here = value_all[owner_index]
        scores = matmul_back(query_blk, keys_here) * score_scale
        row_top = jnp.max(scores, axis=-1, keepdims=True)
        exponent = jnp.exp(scores - row_top)
        row_total = jnp.sum(exponent, axis=-1, keepdims=True)
        weights_now = exponent / row_total
        mixed_rows = jnp.dot(
            weights_now.astype(jnp.bfloat16), values_here, preferred_element_type=jnp.float32
        )
        return (mixed_rows, row_top[:, 0] + jnp.log(row_total[:, 0]))

    mixed_rows, log_total = lax.map(
        one_block, (query_items, jnp.arange(item_count, dtype=jnp.int32))
    )
    return (mixed_rows.reshape(queries.shape), log_total.reshape(queries.shape[:-1]))


def attend_backward(queries, key_rows, value_rows, log_total, context_low):
    seq_heads = key_rows.shape[0] * key_rows.shape[1]
    head_dim = queries.shape[-1]
    score_scale = head_dim ** (-0.5)
    block_rows = min(512, SEQ_LEN)
    block_count = SEQ_LEN // block_rows
    item_count = seq_heads * block_count
    query_items = queries.reshape(item_count, block_rows, head_dim)
    total_items = log_total.reshape(item_count, block_rows)
    grad_items = context_low.reshape(item_count, block_rows, head_dim)
    key_all = key_rows.reshape(seq_heads, SEQ_LEN, head_dim)
    value_all = value_rows.reshape(seq_heads, SEQ_LEN, head_dim)

    def one_block(block_item):
        query_blk, total_blk, grad_blk, position = block_item
        owner_index = position // block_count
        keys_here = key_all[owner_index]
        values_here = value_all[owner_index]
        scores = matmul_back(query_blk, keys_here) * score_scale
        weights_now = jnp.exp(scores - total_blk[:, None])
        grad_weights = matmul_back(grad_blk, values_here)
        grad_scores = weights_now * (
            grad_weights - jnp.sum(weights_now * grad_weights, axis=-1, keepdims=True)
        )
        score_low = grad_scores.astype(jnp.bfloat16)
        grad_query = jnp.dot(score_low, keys_here, preferred_element_type=jnp.float32) * score_scale
        grad_key = matmul_rows(score_low, query_blk) * score_scale
        grad_value = matmul_rows(weights_now.astype(jnp.bfloat16), grad_blk)
        return (grad_query, grad_key, grad_value)

    grad_query, grad_key, grad_value = lax.map(
        one_block, (query_items, total_items, grad_items, jnp.arange(item_count, dtype=jnp.int32))
    )
    grad_key = jnp.sum(grad_key.reshape(seq_heads, block_count, SEQ_LEN, head_dim), axis=1)
    grad_value = jnp.sum(grad_value.reshape(seq_heads, block_count, SEQ_LEN, head_dim), axis=1)
    return (
        grad_query.reshape(queries.shape),
        grad_key.reshape(key_rows.shape),
        grad_value.reshape(value_rows.shape),
    )


def norm_forward(hidden, gain_vec, shift_vec):
    center = jnp.mean(hidden, axis=-1)
    second = jnp.mean(hidden * hidden, axis=-1) - center * center
    inv_std = lax.rsqrt(second + norm_eps)
    normal = (hidden - center[:, None]) * inv_std[:, None]
    return (normal * gain_vec + shift_vec, normal, inv_std)


def norm_backward(upstream, normal, inv_std, gain_vec):
    scaled = upstream * gain_vec
    first_mean = jnp.mean(scaled, axis=-1)
    second_mean = jnp.mean(scaled * normal, axis=-1)
    grad_in = inv_std[:, None] * (scaled - first_mean[:, None] - normal * second_mean[:, None])
    return (grad_in, jnp.sum(upstream * normal, axis=0), jnp.sum(upstream, axis=0))


def rows_in(value):
    return lax.all_gather(value, "tensor", axis=0, tiled=True)


def part_out(value):
    return lax.psum_scatter(value, "tensor", scatter_dimension=0, tiled=True)


def gather_grad(value):
    return lax.all_gather(value, "tensor", axis=0, tiled=True)


def part_back(value):
    return lax.psum_scatter(value, "tensor", scatter_dimension=0, tiled=True)


def token_body(
    layer_input,
    output_grad,
    qkv_weight,
    query_bias,
    value_bias,
    proj_weight,
    proj_bias,
    first_gain,
    first_shift,
    up_weight,
    up_bias,
    down_weight,
    down_bias,
    second_gain,
    second_shift,
):
    heads_here = query_bias.shape[0] // HEAD_DIM
    query_bf = query_bias.astype(jnp.float32).reshape(heads_here, HEAD_DIM)
    value_bf = value_bias.astype(jnp.float32).reshape(heads_here, HEAD_DIM)
    bias_rows = jnp.stack([query_bf, jnp.zeros_like(query_bf), value_bf], axis=1)
    gain_one = first_gain.astype(jnp.float32)
    shift_one = first_shift.astype(jnp.float32)
    gain_two = second_gain.astype(jnp.float32)
    shift_two = second_shift.astype(jnp.float32)
    input_full = rows_in(layer_input)
    row_count = input_full.shape[0]
    seq_count = row_count // SEQ_LEN
    projected = matmul_back(input_full, qkv_weight).reshape(row_count, heads_here, 3, HEAD_DIM)
    packed = (projected + bias_rows).astype(jnp.bfloat16)
    parts = packed.reshape(seq_count, SEQ_LEN, heads_here, 3, HEAD_DIM).transpose(3, 0, 2, 1, 4)
    queries, key_rows, value_rows = (parts[0], parts[1], parts[2])
    mixed_rows, log_total = attend_forward(queries, key_rows, value_rows)
    context = (
        mixed_rows.transpose(0, 2, 1, 3)
        .reshape(row_count, heads_here * HEAD_DIM)
        .astype(jnp.bfloat16)
    )
    partial_branch = jnp.dot(context, proj_weight, preferred_element_type=jnp.float32)
    branch = part_out(partial_branch) + proj_bias.astype(jnp.float32)
    normed_one, normal_one, inv_one = norm_forward(
        layer_input.astype(jnp.float32) + branch, gain_one, shift_one
    )
    normed_full = rows_in(normed_one.astype(jnp.bfloat16))
    inner_pre = jnp.dot(
        normed_full, up_weight, preferred_element_type=jnp.float32
    ) + up_bias.astype(jnp.float32)
    active, gelu_back = jax.vjp(partial(jax.nn.gelu, approximate=False), inner_pre)
    active_low = active.astype(jnp.bfloat16)
    second = part_out(
        jnp.dot(active_low, down_weight, preferred_element_type=jnp.float32)
    ) + down_bias.astype(jnp.float32)
    result_rows, normal_two, inv_two = norm_forward(normed_one + second, gain_two, shift_two)
    upstream = output_grad.astype(jnp.float32)
    grad_two, gain_two_grad, shift_two_grad = norm_backward(upstream, normal_two, inv_two, gain_two)
    second_low = grad_two.astype(jnp.bfloat16)
    down_b_grad = jnp.sum(second_low.astype(jnp.float32), axis=0)
    second_full = gather_grad(second_low)
    down_w_grad = matmul_rows(active_low, second_full)
    grad_active = matmul_back(second_full, down_weight)
    inner_low = gelu_back(grad_active)[0].astype(jnp.bfloat16)
    up_b_grad = jnp.sum(inner_low.astype(jnp.float32), axis=0)
    up_w_grad = matmul_rows(normed_full, inner_low)
    grad_mid = grad_two + part_back(matmul_back(inner_low, up_weight))
    grad_one, gain_one_grad, shift_one_grad = norm_backward(grad_mid, normal_one, inv_one, gain_one)
    branch_low = grad_one.astype(jnp.bfloat16)
    proj_b_grad = jnp.sum(branch_low.astype(jnp.float32), axis=0)
    branch_full = gather_grad(branch_low)
    proj_w_grad = matmul_rows(context, branch_full)
    context_low = matmul_back(branch_full, proj_weight).astype(jnp.bfloat16)
    context_low = context_low.reshape(seq_count, SEQ_LEN, heads_here, HEAD_DIM).transpose(
        0, 2, 1, 3
    )
    grad_query, grad_key, grad_value = attend_backward(
        queries, key_rows, value_rows, log_total, context_low
    )
    packed_low = jnp.stack([grad_query, grad_key, grad_value], axis=0).transpose(1, 3, 2, 0, 4)
    packed_low = packed_low.reshape(row_count, heads_here * 3 * HEAD_DIM).astype(jnp.bfloat16)
    packed_sums = jnp.sum(packed_low.astype(jnp.float32), axis=0).reshape(heads_here, 3, HEAD_DIM)
    query_b_grad = packed_sums[:, 0].reshape(heads_here * HEAD_DIM)
    value_b_grad = packed_sums[:, 2].reshape(heads_here * HEAD_DIM)
    qkv_w_grad = matmul_rows(packed_low, input_full)
    input_grad = (
        grad_one + part_back(jnp.dot(packed_low, qkv_weight, preferred_element_type=jnp.float32))
    ).astype(jnp.bfloat16)
    totals = (
        lax.psum(qkv_w_grad.astype(jnp.bfloat16), "dp").astype(jnp.float32),
        lax.psum(query_b_grad.astype(jnp.bfloat16), "dp").astype(jnp.float32),
        lax.psum(value_b_grad.astype(jnp.bfloat16), "dp").astype(jnp.float32),
        lax.psum(proj_w_grad.astype(jnp.bfloat16), "dp").astype(jnp.float32),
        lax.psum(up_w_grad.astype(jnp.bfloat16), "dp").astype(jnp.float32),
        lax.psum(up_b_grad.astype(jnp.bfloat16), "dp").astype(jnp.float32),
        lax.psum(down_w_grad.astype(jnp.bfloat16), "dp").astype(jnp.float32),
    )
    vectors = lax.psum(
        (proj_b_grad, gain_one_grad, shift_one_grad, down_b_grad, gain_two_grad, shift_two_grad),
        ("dp", "tensor"),
    )
    return (
        result_rows.astype(jnp.bfloat16),
        input_grad,
        totals[0],
        totals[1],
        totals[2],
        totals[3],
        vectors[0],
        vectors[1],
        vectors[2],
        totals[4],
        totals[5],
        totals[6],
        vectors[3],
        vectors[4],
        vectors[5],
    )


VMEM_LIMIT = 66_000_000
EXTRA = 16


def mm(left, right):
    return lax.dot_general(left, right, (((1,), (0,)), ((), ())), preferred_element_type=f32)


def mm_nt(left, right):
    return lax.dot_general(left, right, (((1,), (1,)), ((), ())), preferred_element_type=f32)


def mm_tn(left, right):
    return lax.dot_general(left, right, (((0,), (0,)), ((), ())), preferred_element_type=f32)


def kernel_params(limit=VMEM_LIMIT):
    return pltpu.CompilerParams(vmem_limit_bytes=limit)


def cost(flops, size):
    return pl.CostEstimate(flops=int(flops), bytes_accessed=int(size), transcendentals=0)


def in_vmem():
    return pl.BlockSpec(memory_space=pltpu.VMEM)


def aligned(start, size, by):
    return pl.ds(pl.multiple_of(start * size, by), size)


def pack_kernel(pos_ref, qkv_ref, query_b_ref, value_b_ref, proj_ref, down_ref, up_ref, up_b_ref, *refs):
    vec_refs, (qkv_out, own_b_ref, packed_ref, vecs_ref) = refs[:-4], refs[-4:]
    half = qkv_ref.shape[0]
    wide = query_b_ref.shape[0] // 2
    query_b, value_b = (ref[...].reshape(1, 2 * wide) for ref in (query_b_ref, value_b_ref))
    qkv_out[:half] = qkv_ref[...]
    qkv_out[half:] = jnp.zeros_like(qkv_out[half:])
    own_b_ref[...] = jnp.zeros_like(own_b_ref)
    parity = lax.rem(pos_ref[0], 2)
    for k in range(2):
        cols = slice(k * wide, (k + 1) * wide)
        own_b_ref[k * EXTRA : k * EXTRA + 1, :wide] = query_b[:, cols]
        own_b_ref[k * EXTRA : k * EXTRA + 1, wide : 2 * wide] = value_b[:, cols]

        @pl.when(parity == k)
        def _():
            qkv_out[half : half + 1, :wide] = query_b[:, cols]
            qkv_out[half : half + 1, wide : 2 * wide] = value_b[:, cols]

    width = proj_ref.shape[1]
    at = 0
    for value in (proj_ref[...], down_ref[...]):
        packed_ref[at : at + value.shape[0]] = value
        at += value.shape[0]
    blocks = up_ref.shape[1] // width
    for j in range(blocks):
        packed_ref[at : at + up_ref.shape[0]] = up_ref[:, j * width : (j + 1) * width]
        at += up_ref.shape[0]
    packed_ref[at:] = jnp.zeros_like(packed_ref[at:])
    vecs_ref[...] = jnp.zeros_like(vecs_ref)
    for j in range(blocks):
        row = up_b_ref[j * width : (j + 1) * width].reshape(1, width)
        packed_ref[at + j : at + j + 1] = row
        vecs_ref[8 + j : 9 + j] = row.astype(f32)
    for k, ref in enumerate(vec_refs):
        vecs_ref[k : k + 1] = ref[...].reshape(1, width).astype(f32)


def pack(pos, qkv, query_b, value_b, proj, down, up, up_b, vectors):
    width, hidden = up.shape
    qkv_rows = qkv.shape[0] // 2 + EXTRA
    mlp_rows = (proj.shape[0] + 2 * hidden) // 2 + EXTRA

    def half(array):
        return pl.BlockSpec((array.shape[0] // 2, array.shape[1]), lambda i, pos: (lax.rem(pos[0], 2), 0))

    def whole(array):
        return pl.BlockSpec(array.shape, lambda i, pos: (0,))

    outs = [(qkv_rows, bf16), (2 * EXTRA, bf16), (mlp_rows, bf16), (EXTRA, f32)]
    return pl.pallas_call(
        pack_kernel,
        grid_spec=pltpu.PrefetchScalarGridSpec(
            num_scalar_prefetch=1,
            grid=(1,),
            in_specs=[half(qkv), whole(query_b), whole(value_b), half(proj), half(down), half(up), whole(up_b)]
            + [whole(v) for v in vectors],
            out_specs=[pl.BlockSpec((rows, width), lambda i, pos: (0, 0)) for rows, _ in outs],
        ),
        out_shape=[jax.ShapeDtypeStruct((rows, width), dtype) for rows, dtype in outs],
        compiler_params=kernel_params(),
        cost_estimate=cost(0, 4 << 20),
        name="pack",
    )(pos, qkv, query_b, value_b, proj, down, up, up_b, *vectors)


def attn_fwd_kernel(pos_ref, x_ref, *refs, heads, q_block, fetched):
    packed_ref, probs_ref, ctx_ref, mixed_ref, key_ref, score_a, score_b = refs[-7:]
    seq = x_ref.shape[0]
    scale = HEAD_DIM**-0.5
    wide = heads * HEAD_DIM
    part = heads * PART_ROWS
    if fetched:
        near = pl.program_id(1) == 0
        weight = jnp.where(near, refs[0][:part], refs[1][:part])
        bias = jnp.where(near, refs[0][part:].astype(f32), refs[1][part:].astype(f32))
    else:
        weight, bias = refs[0][...], refs[1][...].astype(f32)
    column = bias[:8, : 2 * wide].T
    raw = mm_nt(weight, x_ref[...])
    for h in range(heads):
        base = h * PART_ROWS
        ends = (base + HEAD_DIM, base + 2 * HEAD_DIM, base + PART_ROWS)
        query = raw[base : ends[0]] + column[h * HEAD_DIM : (h + 1) * HEAD_DIM, :1]
        value = raw[ends[1] : ends[2]] + column[wide + h * HEAD_DIM : wide + (h + 1) * HEAD_DIM, :1]
        packed_ref[0, 0, base : ends[0]] = query.astype(bf16)
        packed_ref[0, 0, ends[0] : ends[1]] = raw[ends[0] : ends[1]].astype(bf16)
        packed_ref[0, 0, ends[1] : ends[2]] = value.astype(bf16)
        keys = packed_ref[0, 0, ends[0] : ends[1], :].astype(f32)
        key_ref[h] = (keys.T * scale).astype(bf16)
    tiles = [(h, c) for h in range(heads) for c in range(0, seq, q_block)]
    scores = (score_a, score_b)

    def score(tile, ref):
        h, c = tile
        base = h * PART_ROWS
        ref[...] = mm(key_ref[h], packed_ref[0, 0, base : base + HEAD_DIM, c : c + q_block])

    def finish(tile, ref):
        h, c = tile
        base = h * PART_ROWS
        top = jnp.max(ref[...], axis=0, keepdims=True)
        exponent = jnp.exp(ref[...] - top)
        total = jnp.sum(exponent, axis=0, keepdims=True)
        probs = (exponent * (1.0 / total)).astype(bf16)
        probs_ref[0, 0, h, :, c : c + q_block] = probs
        mixed = mm(packed_ref[0, 0, base + 2 * HEAD_DIM : base + 3 * HEAD_DIM, :], probs)
        ctx_ref[0, 0, h * HEAD_DIM : (h + 1) * HEAD_DIM, c : c + q_block] = mixed.astype(bf16)
        mixed_ref[0, 0, h * HEAD_DIM : (h + 1) * HEAD_DIM, c : c + q_block] = mixed

    score(tiles[0], scores[0])
    for j, tile in enumerate(tiles):
        if j + 1 < len(tiles):
            score(tiles[j + 1], scores[(j + 1) % 2])
        finish(tile, scores[j % 2])


def attn_fwd(pos, x, sources, shard, fetched, shapes, earlier):
    rows, width = x.shape
    n_seq = rows // SEQ_LEN
    heads = shapes[1].shape[2] // 2
    part = heads * PART_ROWS

    def at(k, pos):
        return lax.bitwise_xor(k, lax.rem(pos[0], 2)) if fetched else k

    if fetched:
        sizes = [pl.BlockSpec(v.shape, lambda s, k, pos: (0, 0), pipeline_mode=pl.Buffered(1)) for v in sources]
    else:
        sizes = [pl.BlockSpec((size, width), lambda s, k, pos: (k, 0)) for size in (part, EXTRA)]
    out_specs = [
        pl.BlockSpec((1, 1, part, SEQ_LEN), lambda s, k, pos: (shard, s, at(k, pos), 0)),
        pl.BlockSpec((1, 1, heads, SEQ_LEN, SEQ_LEN), lambda s, k, pos: (shard, s, at(k, pos), 0, 0)),
    ] + [pl.BlockSpec((1, 1, heads * HEAD_DIM, SEQ_LEN), lambda s, k, pos: (shard, s, at(k, pos), 0))] * 2
    q_block = 512
    share = 2 * n_seq * heads
    flops = share * (2 * SEQ_LEN * width * PART_ROWS + 4 * SEQ_LEN * SEQ_LEN * HEAD_DIM * 6)
    return pl.pallas_call(
        partial(attn_fwd_kernel, heads=heads, q_block=q_block, fetched=fetched),
        grid_spec=pltpu.PrefetchScalarGridSpec(
            num_scalar_prefetch=1,
            grid=(n_seq, 2),
            in_specs=[pl.BlockSpec((SEQ_LEN, width), lambda s, k, pos: (s, 0))]
            + sizes
            + [pl.BlockSpec(memory_space=pl.ANY)] * len(earlier),
            out_specs=out_specs,
            scratch_shapes=[
                pltpu.VMEM((heads, SEQ_LEN, HEAD_DIM), bf16),
                pltpu.VMEM((SEQ_LEN, q_block), f32),
                pltpu.VMEM((SEQ_LEN, q_block), f32),
            ],
        ),
        out_shape=shapes,
        input_output_aliases={4 + k: k for k in range(len(earlier))},
        compiler_params=kernel_params(),
        cost_estimate=cost(flops // 8 if fetched else flops, share * 3 << 20),
        name="attn_fwd",
    )(pos, x, *sources, *earlier)


def piece_bits(*order):
    bits = [0]
    for bit in reversed(order):
        bits = bits + [b | bit for b in bits]
    return bits


MLP_SLOTS = 8
DOWN_ORDER = ("tensor", 2, 4)
UP_ORDER = (4, "tensor", 2)
DOWN_BITS = piece_bits(1, 2, 4)
UP_BITS = piece_bits(1, 4, 2)


def middle_kernel(
    pos_ref,
    x_ref,
    og_ref,
    ctx_ref,
    vecs_ref,
    proj_own,
    up_own,
    down_own,
    *refs,
    n_others,
    chunk,
):
    fetched, refs = refs[: 2 * n_others], refs[2 * n_others :]
    out_ref, grad_one_ref, ctx_low_ref, dn_keep_ref, dn_send_ref, up_keep_ref, up_send_ref, *refs = refs
    proj_got, up_got, down_got, up_b_ref, act_ref, slope_ref, proj_acc, up_acc, dn_acc, vec_acc, up_b_acc = refs
    step = pl.program_id(0)
    n_shards = n_others + 1
    ctx_rows, width = proj_own.shape
    hidden = up_own.shape[1]
    blocks = hidden // width
    inv_width = 1.0 / width

    def mean(v):
        return jnp.sum(v, axis=1, keepdims=True) * inv_width

    @pl.when(step == 0)
    def _():
        for ref in (proj_acc, up_acc, dn_acc):
            size = min(64, ref.shape[1])

            def clear(i, carry, ref=ref, size=size):
                for t in range(n_shards):
                    ref[t, aligned(i, size, size), :] = jnp.zeros((size, ref.shape[2]), f32)
                return carry

            lax.fori_loop(0, ref.shape[1] // size, clear, 0)
        for ref in (vec_acc, up_b_acc):
            ref[...] = jnp.zeros_like(ref)
        parity = lax.rem(pos_ref[0], 2)
        for j in range(blocks):
            up_b_ref[:, j * width : (j + 1) * width] = vecs_ref[8 + j : 9 + j, :]
        for t in range(n_others):
            for k in range(2):
                ref = fetched[2 * t + k]
                side = parity if k == 0 else 1 - parity
                rows = ctx_rows // 2
                proj_got[t, aligned(side, rows, rows), :] = ref[:rows]
                at = rows
                rows = hidden // 2
                down_got[t, aligned(side, rows, rows), :] = ref[at : at + rows]
                at += rows
                rows = width // 2
                for j in range(blocks):
                    up_got[t, aligned(side, rows, rows), j * width : (j + 1) * width] = ref[at : at + rows]
                    at += rows
                if k == 0:
                    for j in range(blocks):
                        to = (t + 1) * hidden + j * width
                        up_b_ref[:, to : to + width] = ref[at : at + EXTRA].astype(f32)[j : j + 1]

    def proj(t):
        return proj_own[...] if t == 0 else proj_got[t - 1]

    def up(t, c):
        return up_own[:, c : c + chunk] if t == 0 else up_got[t - 1, :, c : c + chunk]

    def down(t, c):
        return down_own[c : c + chunk, :] if t == 0 else down_got[t - 1, c : c + chunk, :]

    proj_b, gain_one, shift_one, down_b, gain_two, shift_two = (vecs_ref[k : k + 1, :] for k in range(6))
    branch = proj_b
    for t in range(n_shards):
        branch = branch + mm_tn(ctx_ref[t, 0], proj(t))
    mid_sum = x_ref[...].astype(f32) + branch
    center = mean(mid_sum)
    inv_one = lax.rsqrt(mean(mid_sum * mid_sum) - center * center + norm_eps)
    normal_one = (mid_sum - center) * inv_one
    normed_one = normal_one * gain_one + shift_one
    normed_low = normed_one.astype(bf16)
    second = down_b
    chunks = [(t, c) for t in range(n_shards) for c in range(0, hidden, chunk)]
    for t, c in chunks:
        at = t * hidden + c
        inner = mm(normed_low, up(t, c)) + up_b_ref[:, at : at + chunk]
        phi = 0.5 * lax.erf(inner * 0.7071067811865476) + 0.5
        active = (inner * phi).astype(bf16)
        act_ref[:, at : at + chunk] = active
        slope_ref[:, at : at + chunk] = phi + inner * (0.3989422804014327 * jnp.exp(-0.5 * inner * inner))
        second = second + mm(active, down(t, c))
    last_sum = normed_one + second
    center_two = mean(last_sum)
    inv_two = lax.rsqrt(mean(last_sum * last_sum) - center_two * center_two + norm_eps)
    normal_two = (last_sum - center_two) * inv_two
    out_ref[...] = (normal_two * gain_two + shift_two).astype(bf16)
    upstream = og_ref[...].astype(f32)
    scaled = upstream * gain_two
    grad_two = inv_two * (scaled - mean(scaled) - normal_two * mean(scaled * normal_two))
    second_low = grad_two.astype(bf16)
    normed_t = normed_low.T
    back = None
    for t, c in chunks:
        at = t * hidden + c
        grad_active = mm_nt(second_low, down(t, c))
        inner_low = (grad_active * slope_ref[:, at : at + chunk]).astype(bf16)
        up_b_acc[:, at : at + chunk] += jnp.sum(inner_low.astype(f32), axis=0, keepdims=True)
        part = mm_nt(inner_low, up(t, c))
        back = part if back is None else back + part
        up_acc[t, :, c : c + chunk] += mm(normed_t, inner_low)
        dn_acc[t, c : c + chunk, :] += mm_tn(act_ref[:, at : at + chunk], second_low)
    grad_mid = grad_two + back
    scaled_one = grad_mid * gain_one
    grad_one = inv_one * (scaled_one - mean(scaled_one) - normal_one * mean(scaled_one * normal_one))
    grad_one_ref[...] = grad_one
    branch_low = grad_one.astype(bf16)
    sums = (
        branch_low.astype(f32),
        grad_mid * normal_one,
        grad_mid,
        second_low.astype(f32),
        upstream * normal_two,
        upstream,
    )
    for k, value in enumerate(sums):
        vec_acc[k : k + 1, :] += jnp.sum(value, axis=0, keepdims=True)
    for t in range(n_shards):
        ctx_low_ref[t, 0] = mm_nt(proj(t), branch_low).astype(bf16)
        proj_acc[t] += mm(ctx_ref[t, 0], branch_low)

    @pl.when(step == pl.num_programs(0) - 1)
    def _():
        low = lax.rem(pos_ref[0], MLP_SLOTS)
        dn_rows, up_rows, proj_rows = hidden // MLP_SLOTS, width // MLP_SLOTS, ctx_rows // MLP_SLOTS
        half = MLP_SLOTS // 2
        for slot in range(MLP_SLOTS):
            dn_ref = dn_keep_ref if slot < half else dn_send_ref
            upk_ref = up_keep_ref if slot < half else up_send_ref
            k = slot % half
            dn_at = lax.bitwise_xor(low, DOWN_BITS[slot])
            rows = aligned(lax.bitwise_xor(low, UP_BITS[slot]), up_rows, up_rows)
            for t in range(n_shards):
                dn_ref[t, k, :dn_rows] = dn_acc[t, aligned(dn_at, dn_rows, dn_rows), :].astype(bf16)
                dn_ref[t, k, dn_rows:] = proj_acc[t, aligned(dn_at, proj_rows, proj_rows), :].astype(bf16)
                for j in range(blocks):
                    to = j * up_rows
                    upk_ref[t, k, to : to + up_rows] = up_acc[t, rows, j * width : (j + 1) * width].astype(bf16)
                to = blocks * up_rows
                upk_ref[t, k, to : to + 8] = vec_acc[...].astype(bf16)
                tail = [
                    up_b_acc[:, t * hidden + j * width : t * hidden + (j + 1) * width] for j in range(blocks)
                ]
                tail.append(jnp.zeros((8 - blocks, width), f32))
                upk_ref[t, k, to + 8 : to + EXTRA] = jnp.concatenate(tail, axis=0).astype(bf16)


def middle(pos, x, out_grad, ctx, vecs, proj, up, down, fetched):
    rows, width = x.shape
    n_shards, n_seq, ctx_rows, _ = ctx.shape
    hidden = up.shape[1]
    n_others = n_shards - 1
    block = 512
    per_seq = SEQ_LEN // block
    half = MLP_SLOTS // 2
    dn_rows, up_rows = (hidden + ctx_rows) // MLP_SLOTS, hidden // MLP_SLOTS + EXTRA

    def whole(array):
        return pl.BlockSpec(array.shape, lambda i, pos: (0,) * array.ndim, pipeline_mode=pl.Buffered(1))

    def kept(*shape):
        return pl.BlockSpec(shape, lambda i, pos: (0,) * len(shape))

    row = pl.BlockSpec((block, width), lambda i, pos: (i, 0))
    cols = pl.BlockSpec((n_shards, 1, ctx_rows, block), lambda i, pos: (0, i // per_seq, 0, i % per_seq))
    dn_shape, up_shape = (n_shards, half, dn_rows, width), (n_shards, half, up_rows, width)
    consts = [vecs, proj, up, down] + fetched
    return pl.pallas_call(
        partial(middle_kernel, n_others=n_others, chunk=min(1024, hidden)),
        grid_spec=pltpu.PrefetchScalarGridSpec(
            num_scalar_prefetch=1,
            grid=(rows // block,),
            in_specs=[row, row, cols] + [whole(array) for array in consts],
            out_specs=[row, row, cols, kept(*dn_shape), kept(*dn_shape), kept(*up_shape), kept(*up_shape)],
            scratch_shapes=[
                pltpu.VMEM((n_others, ctx_rows, width), bf16),
                pltpu.VMEM((n_others, width, hidden), bf16),
                pltpu.VMEM((n_others, hidden, width), bf16),
                pltpu.VMEM((1, n_shards * hidden), f32),
                pltpu.VMEM((block, n_shards * hidden), bf16),
                pltpu.VMEM((block, n_shards * hidden), f32),
                pltpu.VMEM((n_shards, ctx_rows, width), f32),
                pltpu.VMEM((n_shards, width, hidden), f32),
                pltpu.VMEM((n_shards, hidden, width), f32),
                pltpu.VMEM((8, width), f32),
                pltpu.VMEM((1, n_shards * hidden), f32),
            ],
        ),
        out_shape=[
            jax.ShapeDtypeStruct((rows, width), bf16),
            jax.ShapeDtypeStruct((rows, width), f32),
            jax.ShapeDtypeStruct(ctx.shape, bf16),
            jax.ShapeDtypeStruct(dn_shape, bf16),
            jax.ShapeDtypeStruct(dn_shape, bf16),
            jax.ShapeDtypeStruct(up_shape, bf16),
            jax.ShapeDtypeStruct(up_shape, bf16),
        ],
        compiler_params=kernel_params(),
        cost_estimate=cost(30 << 30, 30 << 20),
        name="middle",
    )(pos, x, out_grad, ctx, *consts)


def piece_number(pos, slot, cut):
    number = 0
    for k, bit in enumerate(cut):
        own = lax.bitwise_and(lax.shift_right_logical(pos, bit.bit_length() - 1), 1)
        flip = (slot >> (len(cut) - 1 - k)) & 1
        number = number + (lax.bitwise_xor(own, flip) << k)
    return number


def attn_bwd_kernel(
    pos_ref,
    x_ref,
    packed_ref,
    probs_ref,
    ctx_low_ref,
    mixed_ref,
    sums_ref,
    *refs,
    head,
    cut,
    extra,
    unroll,
):
    grad_ref, keep_ref, send_ref, bias_ref, value_ref, weight_acc = refs[-6:]
    step = pl.program_id(0)
    seq = x_ref.shape[0]
    n_shards = packed_ref.shape[0]
    scale = HEAD_DIM**-0.5
    for t in range(n_shards):
        value_ref[t] = packed_ref[t, 0, 2 * HEAD_DIM : 3 * HEAD_DIM, :].T
    def one_shard(t, carry):
        ctx_low = ctx_low_ref[t, 0]
        total = jnp.sum(ctx_low.astype(f32) * mixed_ref[t, 0], axis=0, keepdims=True)
        probs = probs_ref[t, 0, 0]
        score_low = (probs.astype(f32) * (mm(value_ref[t], ctx_low) - total)).astype(bf16)
        grad_query = mm(packed_ref[t, 0, HEAD_DIM : 2 * HEAD_DIM, :], score_low) * scale
        grad_key = mm_nt(score_low, packed_ref[t, 0, :HEAD_DIM, :]) * scale
        grad_value = mm_nt(probs, ctx_low)
        grad_ref[t, 0, :HEAD_DIM, :] = grad_query.astype(bf16)
        grad_ref[t, 0, HEAD_DIM : 2 * HEAD_DIM, :] = grad_key.T.astype(bf16)
        grad_ref[t, 0, 2 * HEAD_DIM :, :] = grad_value.T.astype(bf16)
        return carry

    if unroll:
        for t in range(n_shards):
            one_shard(t, 0)
    else:
        lax.fori_loop(0, n_shards, one_shard, 0)

    @pl.when(step == 0)
    def _():
        weight_acc[...] = jnp.zeros_like(weight_acc)
        bias_ref[...] = sums_ref[...]

    ones = jnp.ones((8, seq), bf16)
    for t in range(n_shards):
        weight_acc[t] += mm(grad_ref[t, 0], x_ref[...])
        bias_ref[t, head : head + 1] += mm_nt(ones, grad_ref[t, 0])[:1]

    @pl.when(step == pl.num_programs(0) - 1)
    def _():
        slots = 1 << len(cut)
        half = slots // 2
        rows = PART_ROWS // slots
        for slot in range(slots):
            at = piece_number(pos_ref[0], slot, cut)
            ref = keep_ref if slot < half else send_ref
            for t in range(n_shards):
                ref[t, slot % half, :rows] = weight_acc[t, aligned(at, rows, 8), :].astype(bf16)
                if extra:
                    padded = jnp.concatenate(
                        [bias_ref[t], jnp.zeros((EXTRA, ref.shape[3] - PART_ROWS), f32)], axis=1
                    )
                    ref[t, slot % half, rows:] = padded.astype(bf16)


def attn_bwd(pos, x, packed, probs, ctx_low, mixed, sums, head, first, group, cut, extra, unroll, earlier):
    rows, width = x.shape
    n_shards, n_seq = packed.shape[:2]
    slots = 1 << len(cut)
    each = PART_ROWS // slots + (EXTRA if extra else 0)
    pieces = (n_shards, slots // 2, group * each, width)
    piece = pl.BlockSpec((n_shards, slots // 2, each, width), lambda s, pos: (0, 0, head - first, 0))
    sum_spec = pl.BlockSpec(sums.shape, lambda s, pos: (0, 0, 0))
    return pl.pallas_call(
        partial(attn_bwd_kernel, head=head, cut=cut, extra=extra, unroll=unroll),
        grid_spec=pltpu.PrefetchScalarGridSpec(
            num_scalar_prefetch=1,
            grid=(n_seq,),
            in_specs=[
                pl.BlockSpec((SEQ_LEN, width), lambda s, pos: (s, 0)),
                pl.BlockSpec((n_shards, 1, PART_ROWS, SEQ_LEN), lambda s, pos: (0, s, head, 0)),
                pl.BlockSpec((n_shards, 1, 1, SEQ_LEN, SEQ_LEN), lambda s, pos: (0, s, head, 0, 0)),
                pl.BlockSpec((n_shards, 1, HEAD_DIM, SEQ_LEN), lambda s, pos: (0, s, head, 0)),
                pl.BlockSpec((n_shards, 1, HEAD_DIM, SEQ_LEN), lambda s, pos: (0, s, head, 0)),
                sum_spec,
            ]
            + [pl.BlockSpec(memory_space=pl.ANY)] * len(earlier),
            out_specs=[
                pl.BlockSpec((n_shards, 1, PART_ROWS, SEQ_LEN), lambda s, pos: (0, s, 0, 0)),
                piece,
                piece,
                sum_spec,
            ],
            scratch_shapes=[
                pltpu.VMEM((n_shards, SEQ_LEN, HEAD_DIM), bf16),
                pltpu.VMEM((n_shards, PART_ROWS, width), f32),
            ],
        ),
        out_shape=[
            jax.ShapeDtypeStruct((n_shards, n_seq, PART_ROWS, SEQ_LEN), bf16),
            jax.ShapeDtypeStruct(pieces, bf16),
            jax.ShapeDtypeStruct(pieces, bf16),
            jax.ShapeDtypeStruct(sums.shape, f32),
        ],
        input_output_aliases={7: 1, 8: 2} if earlier else {},
        compiler_params=kernel_params(51_000_000),
        cost_estimate=cost(8 << 30, 10 << 20),
        name="attn_bwd",
    )(pos, x, packed, probs, ctx_low, mixed, sums, *earlier)


def input_grad_kernel(pos_ref, grad_one_ref, own_ref, *refs, n_others):
    fetched, grads, out_ref, got_ref = refs[: 2 * n_others], refs[2 * n_others : -2], refs[-2], refs[-1]
    half = own_ref.shape[0] // 2

    @pl.when(pl.program_id(0) == 0)
    def _():
        parity = lax.rem(pos_ref[0], 2)
        for t in range(n_others):
            for k in range(2):
                side = parity if k == 0 else 1 - parity
                got_ref[t, aligned(side, half, half), :] = fetched[2 * t + k][:half]

    total = grad_one_ref[...]
    for t in range(n_others + 1):
        weight = own_ref if t == 0 else got_ref.at[t - 1]
        for head, ref in enumerate(grads):
            total = total + mm_tn(ref[t, 0], weight[head * PART_ROWS : (head + 1) * PART_ROWS, :])
    out_ref[...] = total.astype(bf16)


def input_gradient(pos, grad_one, own, fetched, packed_grads):
    rows, width = grad_one.shape
    n_shards = packed_grads[0].shape[0]
    block = 512
    per_seq = SEQ_LEN // block
    row = pl.BlockSpec((block, width), lambda i, pos: (i, 0))
    cols = pl.BlockSpec((n_shards, 1, PART_ROWS, block), lambda i, pos: (0, i // per_seq, 0, i % per_seq))

    def whole(array):
        return pl.BlockSpec(array.shape, lambda i, pos: (0, 0), pipeline_mode=pl.Buffered(1))

    return pl.pallas_call(
        partial(input_grad_kernel, n_others=n_shards - 1),
        grid_spec=pltpu.PrefetchScalarGridSpec(
            num_scalar_prefetch=1,
            grid=(rows // block,),
            in_specs=[row, whole(own)] + [whole(v) for v in fetched] + [cols] * len(packed_grads),
            out_specs=row,
            scratch_shapes=[pltpu.VMEM((n_shards - 1,) + own.shape, bf16)],
        ),
        out_shape=jax.ShapeDtypeStruct((rows, width), bf16),
        compiler_params=kernel_params(51_000_000),
        cost_estimate=cost(4 << 30, 12 << 20),
        name="input_gradient",
    )(pos, grad_one, own, *fetched, *packed_grads)


def mlp_place_kernel(pos_ref, dn_near, dn_far, up_near, up_far, proj_out, up_out, dn_out):
    low = lax.rem(pos_ref[0], MLP_SLOTS)
    half = MLP_SLOTS // 2
    width = proj_out.shape[1]
    hidden = dn_out.shape[0]
    dn_rows, up_rows, proj_rows = hidden // MLP_SLOTS, width // MLP_SLOTS, proj_out.shape[0] // MLP_SLOTS
    for slot in range(MLP_SLOTS):
        dn_ref = dn_near if slot < half else dn_far
        up_ref = up_near if slot < half else up_far
        k = slot % half
        at = lax.bitwise_xor(low, DOWN_BITS[slot])
        dn_out[aligned(at, dn_rows, dn_rows), :] = dn_ref[k, :dn_rows].astype(f32)
        proj_out[aligned(at, proj_rows, proj_rows), :] = dn_ref[k, dn_rows:].astype(f32)
        rows = aligned(lax.bitwise_xor(low, UP_BITS[slot]), up_rows, up_rows)
        for j in range(hidden // width):
            up_out[rows, j * width : (j + 1) * width] = up_ref[k, j * up_rows : (j + 1) * up_rows].astype(f32)


def mlp_place(pos, dn_parts, up_parts, ctx_rows, width, hidden):
    return pl.pallas_call(
        mlp_place_kernel,
        in_specs=[pl.BlockSpec(memory_space=pltpu.SMEM)] + [in_vmem()] * 4,
        out_specs=[in_vmem()] * 3,
        out_shape=[
            jax.ShapeDtypeStruct((ctx_rows, width), f32),
            jax.ShapeDtypeStruct((width, hidden), f32),
            jax.ShapeDtypeStruct((hidden, width), f32),
        ],
        compiler_params=kernel_params(51_000_000),
        cost_estimate=cost(0, 14 << 20),
        name="mlp_place",
    )(pos, *dn_parts, *up_parts)


def qkv_place_kernel(pos_ref, *refs, groups):
    bias_ref, out_ref, query_ref, value_ref = refs[-4:]
    for g, (first, group, cut, each) in enumerate(groups):
        slots = 1 << len(cut)
        half = slots // 2
        rows = PART_ROWS // slots
        for slot in range(slots):
            at = aligned(piece_number(pos_ref[0], slot, cut), rows, 8)
            for k in range(group):
                value = refs[2 * g + slot // half][slot % half, k * each : k * each + rows]
                out_ref[first + k, at, :] = value.astype(f32)
    heads = out_ref.shape[0]
    for k, ref in ((0, query_ref), (2, value_ref)):
        parts = [bias_ref[h : h + 1, k * HEAD_DIM : (k + 1) * HEAD_DIM] for h in range(heads)]
        ref[...] = jnp.concatenate(parts, axis=1).reshape(heads * HEAD_DIM)


def qkv_place(pos, parts, bias, groups, heads):
    flat = [half for pair in parts for half in pair]
    vector = jax.ShapeDtypeStruct((heads * HEAD_DIM,), f32)
    return pl.pallas_call(
        partial(qkv_place_kernel, groups=groups),
        in_specs=[pl.BlockSpec(memory_space=pltpu.SMEM)] + [in_vmem()] * (len(flat) + 1),
        out_specs=[in_vmem()] * 3,
        out_shape=[jax.ShapeDtypeStruct((heads, PART_ROWS, flat[0].shape[2]), f32), vector, vector],
        compiler_params=kernel_params(51_000_000),
        cost_estimate=cost(0, 3 << 20),
        name="qkv_place",
    )(pos, *flat, bias)


def swap_dp(value, bits, n_dp):
    return lax.ppermute(value, "dp", [(i, i ^ bits) for i in range(n_dp)])


def shift_tensor(value, by, n_tensor):
    return lax.ppermute(value, "tensor", [((i + by) % n_tensor, i) for i in range(n_tensor)])


def reduce_pieces(keep, send, order, n_dp, n_tensor):
    halved = [axis for axis in order if axis != "tensor"]
    got = swap_dp(send, 1, n_dp)
    got = after(got, (yield send))
    parts = [keep[t].astype(f32) + got[t].astype(f32) for t in range(n_tensor)]
    for axis in order:
        if axis == "tensor":
            outs = [parts[by].astype(bf16) for by in range(1, n_tensor)]
            gots = [shift_tensor(out, -by, n_tensor) for by, out in enumerate(outs, 1)]
            gots = after(gots, (yield outs))
            parts = [sum((got.astype(f32) for got in gots), parts[0])]
        else:
            cut = parts[0].shape[0] // 2
            out = jnp.stack([part[cut:].astype(bf16) for part in parts])
            got = swap_dp(out, axis, n_dp)
            got = after(got, (yield out))
            parts = [part[:cut] + got[t].astype(f32) for t, part in enumerate(parts)]
    own = parts[0]
    bits = 2
    while bits < n_dp:
        if bits not in halved:
            out = own.astype(bf16)
            got = swap_dp(out, bits, n_dp)
            got = after(got, (yield out))
            own = own + got.astype(f32)
        bits *= 2
    near = own.astype(bf16)
    for axis in reversed(halved):
        got = swap_dp(near, axis, n_dp)
        got = after(got, (yield near))
        near = jnp.concatenate([near, got], axis=0)
    got = swap_dp(near, 1, n_dp)
    got = after(got, (yield near))
    return near, got, own


class Sums:
    def __init__(self):
        self.live, self.done, self.fresh = {}, {}, set()

    def add(self, name, generator):
        self.live[name] = generator
        self.fresh.add(name)

    def step(self, ready, *names):
        sent = []
        for name in names:
            if name in self.live:
                try:
                    sent.append(self.live[name].send(None if name in self.fresh else ready))
                    self.fresh.discard(name)
                except StopIteration as stop:
                    self.done[name] = stop.value
                    del self.live[name]
        return sent

    def finish(self):
        while self.live:
            self.step((), *list(self.live))


def after(value, *others):
    return lax.optimization_barrier((value, others))[0]


def sequence_body(n_dp, n_tensor, *arrays):
    (
        layer_input,
        output_grad,
        qkv_weight,
        query_bias,
        value_bias,
        proj_weight,
        proj_bias,
        first_gain,
        first_shift,
        up_weight,
        up_bias,
        down_weight,
        down_bias,
        second_gain,
        second_shift,
    ) = arrays
    rows, width = layer_input.shape
    n_seq = rows // SEQ_LEN
    ctx_rows, hidden = proj_weight.shape[0], up_weight.shape[1]
    n_heads = ctx_rows // HEAD_DIM
    pos = lax.axis_index("dp").astype(jnp.int32).reshape(1)
    shifts = range(1, n_tensor)

    vectors = [proj_bias, first_gain, first_shift, down_bias, second_gain, second_shift]
    qkv_half, own_bias, mlp_half, vecs = pack(
        pos, qkv_weight, query_bias, value_bias, proj_weight, down_weight, up_weight, up_bias, vectors
    )
    qkv_near = [shift_tensor(qkv_half, by, n_tensor) for by in shifts]
    shapes = [
        jax.ShapeDtypeStruct((n_tensor, n_seq, n_heads * PART_ROWS, SEQ_LEN), bf16),
        jax.ShapeDtypeStruct((n_tensor, n_seq, n_heads, SEQ_LEN, SEQ_LEN), bf16),
        jax.ShapeDtypeStruct((n_tensor, n_seq, n_heads * HEAD_DIM, SEQ_LEN), bf16),
        jax.ShapeDtypeStruct((n_tensor, n_seq, n_heads * HEAD_DIM, SEQ_LEN), f32),
    ]
    mlp_near = [shift_tensor(mlp_half, by, n_tensor) for by in shifts]
    x = after(layer_input, mlp_half)
    stacks = attn_fwd(pos, x, (qkv_weight, own_bias), 0, False, shapes, ())
    qkv_near = after(qkv_near, stacks[2])
    qkv_far = [swap_dp(near, 1, n_dp) for near in qkv_near]
    for t in shifts:
        stacks = attn_fwd(pos, layer_input, (qkv_near[t - 1], qkv_far[t - 1]), t, True, shapes, stacks)
    packed, probs, ctx, mixed = stacks
    mlp_near = after(mlp_near, ctx)
    mlp_far = [swap_dp(near, 1, n_dp) for near in mlp_near]
    fetched = [half for pair in zip(mlp_near, mlp_far) for half in pair]
    result, grad_one, ctx_low, dn_keep, dn_send, up_keep, up_send = middle(
        pos, layer_input, output_grad, ctx, vecs, proj_weight, up_weight, down_weight, fetched
    )
    sums = Sums()
    sums.add("dn", reduce_pieces(dn_keep, dn_send, DOWN_ORDER, n_dp, n_tensor))
    sums.add("up", reduce_pieces(up_keep, up_send, UP_ORDER, n_dp, n_tensor))
    bias_sums = jnp.zeros((n_tensor, EXTRA, PART_ROWS), f32)
    packed_grads = []
    ready = ()
    early = n_heads - 1
    stacked = ()
    early_cut, early_order = (1, 2), ("tensor", 2)
    for head in range(n_heads):
        last = head == early
        if last and early:
            sums.add("qa", reduce_pieces(*stacked, early_order, n_dp, n_tensor))
        sent = sums.step(ready, *SCHEDULE[min(head, len(SCHEDULE) - 3)])
        x = after(layer_input, sent)
        grads, keep, send, bias_sums = attn_bwd(
            pos,
            x,
            packed,
            probs,
            ctx_low,
            mixed,
            bias_sums,
            head,
            early if last else 0,
            1 if last else early,
            (1,) if last else early_cut,
            last,
            head in UNROLLED,
            () if last else stacked,
        )
        ready = bias_sums
        packed_grads.append(grads)
        if not last:
            stacked = (keep, send)
    sums.add("qb", reduce_pieces(keep, send, ("tensor",), n_dp, n_tensor))
    sent = sums.step(ready, *SCHEDULE[-2])
    qkv_fetched = [half for pair in zip(qkv_near, qkv_far) for half in pair]
    input_grad = input_gradient(pos, after(grad_one, sent), qkv_weight, qkv_fetched, packed_grads)
    ready = input_grad
    for name in SCHEDULE[-1]:
        sent = sums.step(ready, name)
        ready = sent or ready
    sums.finish()
    dn_near, dn_far, _ = sums.done["dn"]
    up_near, up_far, up_own = sums.done["up"]
    proj_wg, up_wg, dn_wg = mlp_place(pos, (dn_near, dn_far), (up_near, up_far), ctx_rows, width, hidden)
    groups = [(0, early, early_cut, PART_ROWS // 4)] if early else []
    groups.append((early, 1, (1,), PART_ROWS // 2 + EXTRA))
    parts = [sums.done[name][:2] for name in ("qa", "qb") if name in sums.done]
    bias = sums.done["qb"][2][0, -EXTRA:]
    qkv_wg, query_bg, value_bg = qkv_place(pos, parts, bias, groups, n_heads)
    small = up_own[0, -EXTRA:]
    return (
        result,
        input_grad,
        qkv_wg.reshape(n_heads * PART_ROWS, width),
        query_bg,
        value_bg,
        proj_wg,
        small[0],
        small[1],
        small[2],
        up_wg,
        small[8 : 8 + hidden // width].reshape(hidden),
        dn_wg,
        small[3],
        small[4],
        small[5],
    )


SCHEDULE = (
    ("dn", "up"),
    ("dn", "up"),
    ("dn", "up"),
    ("qa", "dn", "up", "qa"),
    ("qb", "qa", "dn", "up", "qb"),
    ("qb", "qa", "dn", "up", "qb", "qa", "up", "dn", "qb", "qa", "up", "dn", "qb", "qa"),
)
UNROLLED = (0,)


def solution(mesh):
    n_dp, n_tensor = mesh.shape["dp"], mesh.shape["tensor"]

    def body(*arrays):
        rows = arrays[0].shape[0]
        if rows % SEQ_LEN == 0 and n_dp % 8 == 0 and n_dp & (n_dp - 1) == 0:
            return sequence_body(n_dp, n_tensor, *arrays)
        return token_body(*arrays)

    return jax.shard_map(
        body,
        mesh=mesh,
        in_specs=(
            P(("dp", "tensor"), None),
            P(("dp", "tensor"), None),
            P("tensor", None),
            P("tensor"),
            P("tensor"),
            P("tensor", None),
            P(),
            P(),
            P(),
            P(None, "tensor"),
            P("tensor"),
            P("tensor", None),
            P(),
            P(),
            P(),
        ),
        out_specs=(
            P(("dp", "tensor"), None),
            P(("dp", "tensor"), None),
            P("tensor", None),
            P("tensor"),
            P("tensor"),
            P("tensor", None),
            P(),
            P(),
            P(),
            P(None, "tensor"),
            P("tensor"),
            P("tensor", None),
            P(),
            P(),
            P(),
        ),
        check_vma=False,
    )
```

```python
from functools import partial

import jax
import jax.numpy as jnp
from jax import lax
from jax.experimental import pallas as pl
from jax.experimental.pallas import tpu as pltpu
from jax.sharding import PartitionSpec as P

HEAD_DIM = 64
SEQ_LEN = 1024
PART_ROWS = 3 * HEAD_DIM

norm_eps = 1e-05
f32 = jnp.float32
bf16 = jnp.bfloat16


def matmul_rows(left, right):
    return lax.dot_general(
        left, right, (((0,), (0,)), ((), ())), preferred_element_type=jnp.float32
    )


def matmul_back(left, right):
    return lax.dot_general(
        left, right, (((1,), (1,)), ((), ())), preferred_element_type=jnp.float32
    )


def attend_forward(queries, key_rows, value_rows):
    seq_heads = key_rows.shape[0] * key_rows.shape[1]
    head_dim = queries.shape[-1]
    score_scale = head_dim ** (-0.5)
    block_rows = min(512, SEQ_LEN)
    block_count = SEQ_LEN // block_rows
    item_count = seq_heads * block_count
    query_items = queries.reshape(item_count, block_rows, head_dim)
    key_all = key_rows.reshape(seq_heads, SEQ_LEN, head_dim)
    value_all = value_rows.reshape(seq_heads, SEQ_LEN, head_dim)

    def one_block(block_item):
        query_blk, position = block_item
        owner_index = position // block_count
        keys_here = key_all[owner_index]
        values_here = value_all[owner_index]
        scores = matmul_back(query_blk, keys_here) * score_scale
        row_top = jnp.max(scores, axis=-1, keepdims=True)
        exponent = jnp.exp(scores - row_top)
        row_total = jnp.sum(exponent, axis=-1, keepdims=True)
        weights_now = exponent / row_total
        mixed_rows = jnp.dot(
            weights_now.astype(jnp.bfloat16), values_here, preferred_element_type=jnp.float32
        )
        return (mixed_rows, row_top[:, 0] + jnp.log(row_total[:, 0]))

    mixed_rows, log_total = lax.map(
        one_block, (query_items, jnp.arange(item_count, dtype=jnp.int32))
    )
    return (mixed_rows.reshape(queries.shape), log_total.reshape(queries.shape[:-1]))


def attend_backward(queries, key_rows, value_rows, log_total, context_low):
    seq_heads = key_rows.shape[0] * key_rows.shape[1]
    head_dim = queries.shape[-1]
    score_scale = head_dim ** (-0.5)
    block_rows = min(512, SEQ_LEN)
    block_count = SEQ_LEN // block_rows
    item_count = seq_heads * block_count
    query_items = queries.reshape(item_count, block_rows, head_dim)
    total_items = log_total.reshape(item_count, block_rows)
    grad_items = context_low.reshape(item_count, block_rows, head_dim)
    key_all = key_rows.reshape(seq_heads, SEQ_LEN, head_dim)
    value_all = value_rows.reshape(seq_heads, SEQ_LEN, head_dim)

    def one_block(block_item):
        query_blk, total_blk, grad_blk, position = block_item
        owner_index = position // block_count
        keys_here = key_all[owner_index]
        values_here = value_all[owner_index]
        scores = matmul_back(query_blk, keys_here) * score_scale
        weights_now = jnp.exp(scores - total_blk[:, None])
        grad_weights = matmul_back(grad_blk, values_here)
        grad_scores = weights_now * (
            grad_weights - jnp.sum(weights_now * grad_weights, axis=-1, keepdims=True)
        )
        score_low = grad_scores.astype(jnp.bfloat16)
        grad_query = jnp.dot(score_low, keys_here, preferred_element_type=jnp.float32) * score_scale
        grad_key = matmul_rows(score_low, query_blk) * score_scale
        grad_value = matmul_rows(weights_now.astype(jnp.bfloat16), grad_blk)
        return (grad_query, grad_key, grad_value)

    grad_query, grad_key, grad_value = lax.map(
        one_block, (query_items, total_items, grad_items, jnp.arange(item_count, dtype=jnp.int32))
    )
    grad_key = jnp.sum(grad_key.reshape(seq_heads, block_count, SEQ_LEN, head_dim), axis=1)
    grad_value = jnp.sum(grad_value.reshape(seq_heads, block_count, SEQ_LEN, head_dim), axis=1)
    return (
        grad_query.reshape(queries.shape),
        grad_key.reshape(key_rows.shape),
        grad_value.reshape(value_rows.shape),
    )


def norm_forward(hidden, gain_vec, shift_vec):
    center = jnp.mean(hidden, axis=-1)
    second = jnp.mean(hidden * hidden, axis=-1) - center * center
    inv_std = lax.rsqrt(second + norm_eps)
    normal = (hidden - center[:, None]) * inv_std[:, None]
    return (normal * gain_vec + shift_vec, normal, inv_std)


def norm_backward(upstream, normal, inv_std, gain_vec):
    scaled = upstream * gain_vec
    first_mean = jnp.mean(scaled, axis=-1)
    second_mean = jnp.mean(scaled * normal, axis=-1)
    grad_in = inv_std[:, None] * (scaled - first_mean[:, None] - normal * second_mean[:, None])
    return (grad_in, jnp.sum(upstream * normal, axis=0), jnp.sum(upstream, axis=0))


def rows_in(value):
    return lax.all_gather(value, "tensor", axis=0, tiled=True)


def part_out(value):
    return lax.psum_scatter(value, "tensor", scatter_dimension=0, tiled=True)


def gather_grad(value):
    return lax.all_gather(value, "tensor", axis=0, tiled=True)


def part_back(value):
    return lax.psum_scatter(value, "tensor", scatter_dimension=0, tiled=True)


def token_body(
    layer_input,
    output_grad,
    qkv_weight,
    query_bias,
    value_bias,
    proj_weight,
    proj_bias,
    first_gain,
    first_shift,
    up_weight,
    up_bias,
    down_weight,
    down_bias,
    second_gain,
    second_shift,
):
    heads_here = query_bias.shape[0] // HEAD_DIM
    query_bf = query_bias.astype(jnp.float32).reshape(heads_here, HEAD_DIM)
    value_bf = value_bias.astype(jnp.float32).reshape(heads_here, HEAD_DIM)
    bias_rows = jnp.stack([query_bf, jnp.zeros_like(query_bf), value_bf], axis=1)
    gain_one = first_gain.astype(jnp.float32)
    shift_one = first_shift.astype(jnp.float32)
    gain_two = second_gain.astype(jnp.float32)
    shift_two = second_shift.astype(jnp.float32)
    input_full = rows_in(layer_input)
    row_count = input_full.shape[0]
    seq_count = row_count // SEQ_LEN
    projected = matmul_back(input_full, qkv_weight).reshape(row_count, heads_here, 3, HEAD_DIM)
    packed = (projected + bias_rows).astype(jnp.bfloat16)
    parts = packed.reshape(seq_count, SEQ_LEN, heads_here, 3, HEAD_DIM).transpose(3, 0, 2, 1, 4)
    queries, key_rows, value_rows = (parts[0], parts[1], parts[2])
    mixed_rows, log_total = attend_forward(queries, key_rows, value_rows)
    context = (
        mixed_rows.transpose(0, 2, 1, 3)
        .reshape(row_count, heads_here * HEAD_DIM)
        .astype(jnp.bfloat16)
    )
    partial_branch = jnp.dot(context, proj_weight, preferred_element_type=jnp.float32)
    branch = part_out(partial_branch) + proj_bias.astype(jnp.float32)
    normed_one, normal_one, inv_one = norm_forward(
        layer_input.astype(jnp.float32) + branch, gain_one, shift_one
    )
    normed_full = rows_in(normed_one.astype(jnp.bfloat16))
    inner_pre = jnp.dot(
        normed_full, up_weight, preferred_element_type=jnp.float32
    ) + up_bias.astype(jnp.float32)
    active, gelu_back = jax.vjp(partial(jax.nn.gelu, approximate=False), inner_pre)
    active_low = active.astype(jnp.bfloat16)
    second = part_out(
        jnp.dot(active_low, down_weight, preferred_element_type=jnp.float32)
    ) + down_bias.astype(jnp.float32)
    result_rows, normal_two, inv_two = norm_forward(normed_one + second, gain_two, shift_two)
    upstream = output_grad.astype(jnp.float32)
    grad_two, gain_two_grad, shift_two_grad = norm_backward(upstream, normal_two, inv_two, gain_two)
    second_low = grad_two.astype(jnp.bfloat16)
    down_b_grad = jnp.sum(second_low.astype(jnp.float32), axis=0)
    second_full = gather_grad(second_low)
    down_w_grad = matmul_rows(active_low, second_full)
    grad_active = matmul_back(second_full, down_weight)
    inner_low = gelu_back(grad_active)[0].astype(jnp.bfloat16)
    up_b_grad = jnp.sum(inner_low.astype(jnp.float32), axis=0)
    up_w_grad = matmul_rows(normed_full, inner_low)
    grad_mid = grad_two + part_back(matmul_back(inner_low, up_weight))
    grad_one, gain_one_grad, shift_one_grad = norm_backward(grad_mid, normal_one, inv_one, gain_one)
    branch_low = grad_one.astype(jnp.bfloat16)
    proj_b_grad = jnp.sum(branch_low.astype(jnp.float32), axis=0)
    branch_full = gather_grad(branch_low)
    proj_w_grad = matmul_rows(context, branch_full)
    context_low = matmul_back(branch_full, proj_weight).astype(jnp.bfloat16)
    context_low = context_low.reshape(seq_count, SEQ_LEN, heads_here, HEAD_DIM).transpose(
        0, 2, 1, 3
    )
    grad_query, grad_key, grad_value = attend_backward(
        queries, key_rows, value_rows, log_total, context_low
    )
    packed_low = jnp.stack([grad_query, grad_key, grad_value], axis=0).transpose(1, 3, 2, 0, 4)
    packed_low = packed_low.reshape(row_count, heads_here * 3 * HEAD_DIM).astype(jnp.bfloat16)
    packed_sums = jnp.sum(packed_low.astype(jnp.float32), axis=0).reshape(heads_here, 3, HEAD_DIM)
    query_b_grad = packed_sums[:, 0].reshape(heads_here * HEAD_DIM)
    value_b_grad = packed_sums[:, 2].reshape(heads_here * HEAD_DIM)
    qkv_w_grad = matmul_rows(packed_low, input_full)
    input_grad = (
        grad_one + part_back(jnp.dot(packed_low, qkv_weight, preferred_element_type=jnp.float32))
    ).astype(jnp.bfloat16)
    totals = (
        lax.psum(qkv_w_grad.astype(jnp.bfloat16), "dp").astype(jnp.float32),
        lax.psum(query_b_grad.astype(jnp.bfloat16), "dp").astype(jnp.float32),
        lax.psum(value_b_grad.astype(jnp.bfloat16), "dp").astype(jnp.float32),
        lax.psum(proj_w_grad.astype(jnp.bfloat16), "dp").astype(jnp.float32),
        lax.psum(up_w_grad.astype(jnp.bfloat16), "dp").astype(jnp.float32),
        lax.psum(up_b_grad.astype(jnp.bfloat16), "dp").astype(jnp.float32),
        lax.psum(down_w_grad.astype(jnp.bfloat16), "dp").astype(jnp.float32),
    )
    vectors = lax.psum(
        (proj_b_grad, gain_one_grad, shift_one_grad, down_b_grad, gain_two_grad, shift_two_grad),
        ("dp", "tensor"),
    )
    return (
        result_rows.astype(jnp.bfloat16),
        input_grad,
        totals[0],
        totals[1],
        totals[2],
        totals[3],
        vectors[0],
        vectors[1],
        vectors[2],
        totals[4],
        totals[5],
        totals[6],
        vectors[3],
        vectors[4],
        vectors[5],
    )


VMEM_LIMIT = 66_000_000
EXTRA = 16


def mm(left, right):
    return lax.dot_general(left, right, (((1,), (0,)), ((), ())), preferred_element_type=f32)


def mm_nt(left, right):
    return lax.dot_general(left, right, (((1,), (1,)), ((), ())), preferred_element_type=f32)


def mm_tn(left, right):
    return lax.dot_general(left, right, (((0,), (0,)), ((), ())), preferred_element_type=f32)


def kernel_params(limit=VMEM_LIMIT):
    return pltpu.CompilerParams(vmem_limit_bytes=limit)


def cost(flops, size):
    return pl.CostEstimate(flops=int(flops), bytes_accessed=int(size), transcendentals=0)


def in_vmem():
    return pl.BlockSpec(memory_space=pltpu.VMEM)


def aligned(start, size, by):
    return pl.ds(pl.multiple_of(start * size, by), size)


def pack_kernel(pos_ref, qkv_ref, query_b_ref, value_b_ref, proj_ref, down_ref, up_ref, up_b_ref, *refs):
    vec_refs, (qkv_out, own_b_ref, packed_ref, vecs_ref) = refs[:-4], refs[-4:]
    half = qkv_ref.shape[0]
    wide = query_b_ref.shape[0] // 2
    query_b, value_b = (ref[...].reshape(1, 2 * wide) for ref in (query_b_ref, value_b_ref))
    qkv_out[:half] = qkv_ref[...]
    qkv_out[half:] = jnp.zeros_like(qkv_out[half:])
    own_b_ref[...] = jnp.zeros_like(own_b_ref)
    parity = lax.rem(pos_ref[0], 2)
    for k in range(2):
        cols = slice(k * wide, (k + 1) * wide)
        own_b_ref[k * EXTRA : k * EXTRA + 1, :wide] = query_b[:, cols]
        own_b_ref[k * EXTRA : k * EXTRA + 1, wide : 2 * wide] = value_b[:, cols]

        @pl.when(parity == k)
        def _():
            qkv_out[half : half + 1, :wide] = query_b[:, cols]
            qkv_out[half : half + 1, wide : 2 * wide] = value_b[:, cols]

    width = proj_ref.shape[1]
    at = 0
    for value in (proj_ref[...], down_ref[...]):
        packed_ref[at : at + value.shape[0]] = value
        at += value.shape[0]
    blocks = up_ref.shape[1] // width
    for j in range(blocks):
        packed_ref[at : at + up_ref.shape[0]] = up_ref[:, j * width : (j + 1) * width]
        at += up_ref.shape[0]
    packed_ref[at:] = jnp.zeros_like(packed_ref[at:])
    vecs_ref[...] = jnp.zeros_like(vecs_ref)
    for j in range(blocks):
        row = up_b_ref[j * width : (j + 1) * width].reshape(1, width)
        packed_ref[at + j : at + j + 1] = row
        vecs_ref[8 + j : 9 + j] = row.astype(f32)
    for k, ref in enumerate(vec_refs):
        vecs_ref[k : k + 1] = ref[...].reshape(1, width).astype(f32)


def pack(pos, qkv, query_b, value_b, proj, down, up, up_b, vectors):
    width, hidden = up.shape
    qkv_rows = qkv.shape[0] // 2 + EXTRA
    mlp_rows = (proj.shape[0] + 2 * hidden) // 2 + EXTRA

    def half(array):
        return pl.BlockSpec((array.shape[0] // 2, array.shape[1]), lambda i, pos: (lax.rem(pos[0], 2), 0))

    def whole(array):
        return pl.BlockSpec(array.shape, lambda i, pos: (0,))

    outs = [(qkv_rows, bf16), (2 * EXTRA, bf16), (mlp_rows, bf16), (EXTRA, f32)]
    return pl.pallas_call(
        pack_kernel,
        grid_spec=pltpu.PrefetchScalarGridSpec(
            num_scalar_prefetch=1,
            grid=(1,),
            in_specs=[half(qkv), whole(query_b), whole(value_b), half(proj), half(down), half(up), whole(up_b)]
            + [whole(v) for v in vectors],
            out_specs=[pl.BlockSpec((rows, width), lambda i, pos: (0, 0)) for rows, _ in outs],
        ),
        out_shape=[jax.ShapeDtypeStruct((rows, width), dtype) for rows, dtype in outs],
        compiler_params=kernel_params(),
        cost_estimate=cost(0, 4 << 20),
        name="pack",
    )(pos, qkv, query_b, value_b, proj, down, up, up_b, *vectors)


def attn_fwd_kernel(pos_ref, x_ref, *refs, heads, q_block, fetched):
    packed_ref, probs_ref, ctx_ref, mixed_ref, key_ref, score_a, score_b = refs[-7:]
    seq = x_ref.shape[0]
    scale = HEAD_DIM**-0.5
    wide = heads * HEAD_DIM
    part = heads * PART_ROWS
    if fetched:
        near = pl.program_id(1) == 0
        weight = jnp.where(near, refs[0][:part], refs[1][:part])
        bias = jnp.where(near, refs[0][part:].astype(f32), refs[1][part:].astype(f32))
    else:
        weight, bias = refs[0][...], refs[1][...].astype(f32)
    column = bias[:8, : 2 * wide].T
    raw = mm_nt(weight, x_ref[...])
    for h in range(heads):
        base = h * PART_ROWS
        ends = (base + HEAD_DIM, base + 2 * HEAD_DIM, base + PART_ROWS)
        query = raw[base : ends[0]] + column[h * HEAD_DIM : (h + 1) * HEAD_DIM, :1]
        value = raw[ends[1] : ends[2]] + column[wide + h * HEAD_DIM : wide + (h + 1) * HEAD_DIM, :1]
        packed_ref[0, 0, base : ends[0]] = query.astype(bf16)
        packed_ref[0, 0, ends[0] : ends[1]] = raw[ends[0] : ends[1]].astype(bf16)
        packed_ref[0, 0, ends[1] : ends[2]] = value.astype(bf16)
        keys = packed_ref[0, 0, ends[0] : ends[1], :].astype(f32)
        key_ref[h] = (keys.T * scale).astype(bf16)
    tiles = [(h, c) for h in range(heads) for c in range(0, seq, q_block)]
    scores = (score_a, score_b)

    def score(tile, ref):
        h, c = tile
        base = h * PART_ROWS
        ref[...] = mm(key_ref[h], packed_ref[0, 0, base : base + HEAD_DIM, c : c + q_block])

    def finish(tile, ref):
        h, c = tile
        base = h * PART_ROWS
        top = jnp.max(ref[...], axis=0, keepdims=True)
        exponent = jnp.exp(ref[...] - top)
        total = jnp.sum(exponent, axis=0, keepdims=True)
        probs = (exponent * (1.0 / total)).astype(bf16)
        probs_ref[0, 0, h, :, c : c + q_block] = probs
        mixed = mm(packed_ref[0, 0, base + 2 * HEAD_DIM : base + 3 * HEAD_DIM, :], probs)
        ctx_ref[0, 0, h * HEAD_DIM : (h + 1) * HEAD_DIM, c : c + q_block] = mixed.astype(bf16)
        mixed_ref[0, 0, h * HEAD_DIM : (h + 1) * HEAD_DIM, c : c + q_block] = mixed

    score(tiles[0], scores[0])
    for j, tile in enumerate(tiles):
        if j + 1 < len(tiles):
            score(tiles[j + 1], scores[(j + 1) % 2])
        finish(tile, scores[j % 2])


def attn_fwd(pos, x, sources, shard, fetched, shapes, earlier):
    rows, width = x.shape
    n_seq = rows // SEQ_LEN
    heads = shapes[1].shape[2] // 2
    part = heads * PART_ROWS

    def at(k, pos):
        return lax.bitwise_xor(k, lax.rem(pos[0], 2)) if fetched else k

    if fetched:
        sizes = [pl.BlockSpec(v.shape, lambda s, k, pos: (0, 0), pipeline_mode=pl.Buffered(1)) for v in sources]
    else:
        sizes = [pl.BlockSpec((size, width), lambda s, k, pos: (k, 0)) for size in (part, EXTRA)]
    out_specs = [
        pl.BlockSpec((1, 1, part, SEQ_LEN), lambda s, k, pos: (shard, s, at(k, pos), 0)),
        pl.BlockSpec((1, 1, heads, SEQ_LEN, SEQ_LEN), lambda s, k, pos: (shard, s, at(k, pos), 0, 0)),
    ] + [pl.BlockSpec((1, 1, heads * HEAD_DIM, SEQ_LEN), lambda s, k, pos: (shard, s, at(k, pos), 0))] * 2
    q_block = 1024
    share = 2 * n_seq * heads
    flops = share * (2 * SEQ_LEN * width * PART_ROWS + 4 * SEQ_LEN * SEQ_LEN * HEAD_DIM * 6)
    return pl.pallas_call(
        partial(attn_fwd_kernel, heads=heads, q_block=q_block, fetched=fetched),
        grid_spec=pltpu.PrefetchScalarGridSpec(
            num_scalar_prefetch=1,
            grid=(n_seq, 2),
            in_specs=[pl.BlockSpec((SEQ_LEN, width), lambda s, k, pos: (s, 0))]
            + sizes
            + [pl.BlockSpec(memory_space=pl.ANY)] * len(earlier),
            out_specs=out_specs,
            scratch_shapes=[
                pltpu.VMEM((heads, SEQ_LEN, HEAD_DIM), bf16),
                pltpu.VMEM((SEQ_LEN, q_block), f32),
                pltpu.VMEM((SEQ_LEN, q_block), f32),
            ],
        ),
        out_shape=shapes,
        input_output_aliases={4 + k: k for k in range(len(earlier))},
        compiler_params=kernel_params(),
        cost_estimate=cost(flops // 8 if fetched else flops, share * 3 << 20),
        name="attn_fwd",
    )(pos, x, *sources, *earlier)


def piece_bits(*order):
    bits = [0]
    for bit in reversed(order):
        bits = bits + [b | bit for b in bits]
    return bits


MLP_SLOTS = 8
DOWN_ORDER = ("tensor", 2, 4)
UP_ORDER = (4, "tensor", 2)
DOWN_BITS = piece_bits(1, 2, 4)
UP_BITS = piece_bits(1, 4, 2)


def middle_kernel(
    pos_ref,
    x_ref,
    og_ref,
    ctx_ref,
    vecs_ref,
    proj_own,
    up_own,
    down_own,
    *refs,
    n_others,
    chunk,
):
    fetched, refs = refs[: 2 * n_others], refs[2 * n_others :]
    out_ref, grad_one_ref, ctx_low_ref, dn_keep_ref, dn_send_ref, up_keep_ref, up_send_ref, *refs = refs
    proj_got, up_got, down_got, up_b_ref, act_ref, slope_ref, proj_acc, up_acc, dn_acc, vec_acc, up_b_acc = refs
    step = pl.program_id(0)
    n_shards = n_others + 1
    ctx_rows, width = proj_own.shape
    hidden = up_own.shape[1]
    blocks = hidden // width
    inv_width = 1.0 / width

    def mean(v):
        return jnp.sum(v, axis=1, keepdims=True) * inv_width

    @pl.when(step == 0)
    def _():
        for ref in (proj_acc, up_acc, dn_acc):
            size = min(64, ref.shape[1])

            def clear(i, carry, ref=ref, size=size):
                for t in range(n_shards):
                    ref[t, aligned(i, size, size), :] = jnp.zeros((size, ref.shape[2]), f32)
                return carry

            lax.fori_loop(0, ref.shape[1] // size, clear, 0)
        for ref in (vec_acc, up_b_acc):
            ref[...] = jnp.zeros_like(ref)
        parity = lax.rem(pos_ref[0], 2)
        for j in range(blocks):
            up_b_ref[:, j * width : (j + 1) * width] = vecs_ref[8 + j : 9 + j, :]
        for t in range(n_others):
            for k in range(2):
                ref = fetched[2 * t + k]
                side = parity if k == 0 else 1 - parity
                rows = ctx_rows // 2
                proj_got[t, aligned(side, rows, rows), :] = ref[:rows]
                at = rows
                rows = hidden // 2
                down_got[t, aligned(side, rows, rows), :] = ref[at : at + rows]
                at += rows
                rows = width // 2
                for j in range(blocks):
                    up_got[t, aligned(side, rows, rows), j * width : (j + 1) * width] = ref[at : at + rows]
                    at += rows
                if k == 0:
                    for j in range(blocks):
                        to = (t + 1) * hidden + j * width
                        up_b_ref[:, to : to + width] = ref[at : at + EXTRA].astype(f32)[j : j + 1]

    def proj(t):
        return proj_own[...] if t == 0 else proj_got[t - 1]

    def up(t, c):
        return up_own[:, c : c + chunk] if t == 0 else up_got[t - 1, :, c : c + chunk]

    def down(t, c):
        return down_own[c : c + chunk, :] if t == 0 else down_got[t - 1, c : c + chunk, :]

    proj_b, gain_one, shift_one, down_b, gain_two, shift_two = (vecs_ref[k : k + 1, :] for k in range(6))
    branch = proj_b
    for t in range(n_shards):
        branch = branch + mm_tn(ctx_ref[t, 0], proj(t))
    mid_sum = x_ref[...].astype(f32) + branch
    center = mean(mid_sum)
    inv_one = lax.rsqrt(mean(mid_sum * mid_sum) - center * center + norm_eps)
    normal_one = (mid_sum - center) * inv_one
    normed_one = normal_one * gain_one + shift_one
    normed_low = normed_one.astype(bf16)
    second = down_b
    chunks = [(t, c) for t in range(n_shards) for c in range(0, hidden, chunk)]
    for t, c in chunks:
        at = t * hidden + c
        inner = mm(normed_low, up(t, c)) + up_b_ref[:, at : at + chunk]
        phi = 0.5 * lax.erf(inner * 0.7071067811865476) + 0.5
        active = (inner * phi).astype(bf16)
        act_ref[:, at : at + chunk] = active
        slope_ref[:, at : at + chunk] = phi + inner * (0.3989422804014327 * jnp.exp(-0.5 * inner * inner))
        second = second + mm(active, down(t, c))
    last_sum = normed_one + second
    center_two = mean(last_sum)
    inv_two = lax.rsqrt(mean(last_sum * last_sum) - center_two * center_two + norm_eps)
    normal_two = (last_sum - center_two) * inv_two
    out_ref[...] = (normal_two * gain_two + shift_two).astype(bf16)
    upstream = og_ref[...].astype(f32)
    scaled = upstream * gain_two
    grad_two = inv_two * (scaled - mean(scaled) - normal_two * mean(scaled * normal_two))
    second_low = grad_two.astype(bf16)
    normed_t = normed_low.T
    back = None
    for t, c in chunks:
        at = t * hidden + c
        grad_active = mm_nt(second_low, down(t, c))
        inner_low = (grad_active * slope_ref[:, at : at + chunk]).astype(bf16)
        up_b_acc[:, at : at + chunk] += jnp.sum(inner_low.astype(f32), axis=0, keepdims=True)
        part = mm_nt(inner_low, up(t, c))
        back = part if back is None else back + part
        up_acc[t, :, c : c + chunk] += mm(normed_t, inner_low)
        dn_acc[t, c : c + chunk, :] += mm_tn(act_ref[:, at : at + chunk], second_low)
    grad_mid = grad_two + back
    scaled_one = grad_mid * gain_one
    grad_one = inv_one * (scaled_one - mean(scaled_one) - normal_one * mean(scaled_one * normal_one))
    grad_one_ref[...] = grad_one
    branch_low = grad_one.astype(bf16)
    sums = (
        branch_low.astype(f32),
        grad_mid * normal_one,
        grad_mid,
        second_low.astype(f32),
        upstream * normal_two,
        upstream,
    )
    for k, value in enumerate(sums):
        vec_acc[k : k + 1, :] += jnp.sum(value, axis=0, keepdims=True)
    for t in range(n_shards):
        ctx_low_ref[t, 0] = mm_nt(proj(t), branch_low).astype(bf16)
        proj_acc[t] += mm(ctx_ref[t, 0], branch_low)

    @pl.when(step == pl.num_programs(0) - 1)
    def _():
        low = lax.rem(pos_ref[0], MLP_SLOTS)
        dn_rows, up_rows, proj_rows = hidden // MLP_SLOTS, width // MLP_SLOTS, ctx_rows // MLP_SLOTS
        half = MLP_SLOTS // 2
        for slot in range(MLP_SLOTS):
            dn_ref = dn_keep_ref if slot < half else dn_send_ref
            upk_ref = up_keep_ref if slot < half else up_send_ref
            k = slot % half
            dn_at = lax.bitwise_xor(low, DOWN_BITS[slot])
            rows = aligned(lax.bitwise_xor(low, UP_BITS[slot]), up_rows, up_rows)
            for t in range(n_shards):
                dn_ref[t, k, :dn_rows] = dn_acc[t, aligned(dn_at, dn_rows, dn_rows), :].astype(bf16)
                dn_ref[t, k, dn_rows:] = proj_acc[t, aligned(dn_at, proj_rows, proj_rows), :].astype(bf16)
                for j in range(blocks):
                    to = j * up_rows
                    upk_ref[t, k, to : to + up_rows] = up_acc[t, rows, j * width : (j + 1) * width].astype(bf16)
                to = blocks * up_rows
                upk_ref[t, k, to : to + 8] = vec_acc[...].astype(bf16)
                tail = [
                    up_b_acc[:, t * hidden + j * width : t * hidden + (j + 1) * width] for j in range(blocks)
                ]
                tail.append(jnp.zeros((8 - blocks, width), f32))
                upk_ref[t, k, to + 8 : to + EXTRA] = jnp.concatenate(tail, axis=0).astype(bf16)


def middle(pos, x, out_grad, ctx, vecs, proj, up, down, fetched):
    rows, width = x.shape
    n_shards, n_seq, ctx_rows, _ = ctx.shape
    hidden = up.shape[1]
    n_others = n_shards - 1
    block = 512
    per_seq = SEQ_LEN // block
    half = MLP_SLOTS // 2
    dn_rows, up_rows = (hidden + ctx_rows) // MLP_SLOTS, hidden // MLP_SLOTS + EXTRA

    def whole(array):
        return pl.BlockSpec(array.shape, lambda i, pos: (0,) * array.ndim, pipeline_mode=pl.Buffered(1))

    def kept(*shape):
        return pl.BlockSpec(shape, lambda i, pos: (0,) * len(shape))

    row = pl.BlockSpec((block, width), lambda i, pos: (i, 0))
    cols = pl.BlockSpec((n_shards, 1, ctx_rows, block), lambda i, pos: (0, i // per_seq, 0, i % per_seq))
    dn_shape, up_shape = (n_shards, half, dn_rows, width), (n_shards, half, up_rows, width)
    consts = [vecs, proj, up, down] + fetched
    return pl.pallas_call(
        partial(middle_kernel, n_others=n_others, chunk=min(1024, hidden)),
        grid_spec=pltpu.PrefetchScalarGridSpec(
            num_scalar_prefetch=1,
            grid=(rows // block,),
            in_specs=[row, row, cols] + [whole(array) for array in consts],
            out_specs=[row, row, cols, kept(*dn_shape), kept(*dn_shape), kept(*up_shape), kept(*up_shape)],
            scratch_shapes=[
                pltpu.VMEM((n_others, ctx_rows, width), bf16),
                pltpu.VMEM((n_others, width, hidden), bf16),
                pltpu.VMEM((n_others, hidden, width), bf16),
                pltpu.VMEM((1, n_shards * hidden), f32),
                pltpu.VMEM((block, n_shards * hidden), bf16),
                pltpu.VMEM((block, n_shards * hidden), f32),
                pltpu.VMEM((n_shards, ctx_rows, width), f32),
                pltpu.VMEM((n_shards, width, hidden), f32),
                pltpu.VMEM((n_shards, hidden, width), f32),
                pltpu.VMEM((8, width), f32),
                pltpu.VMEM((1, n_shards * hidden), f32),
            ],
        ),
        out_shape=[
            jax.ShapeDtypeStruct((rows, width), bf16),
            jax.ShapeDtypeStruct((rows, width), f32),
            jax.ShapeDtypeStruct(ctx.shape, bf16),
            jax.ShapeDtypeStruct(dn_shape, bf16),
            jax.ShapeDtypeStruct(dn_shape, bf16),
            jax.ShapeDtypeStruct(up_shape, bf16),
            jax.ShapeDtypeStruct(up_shape, bf16),
        ],
        compiler_params=kernel_params(),
        cost_estimate=cost(30 << 30, 30 << 20),
        name="middle",
    )(pos, x, out_grad, ctx, *consts)


def piece_number(pos, slot, cut):
    number = 0
    for k, bit in enumerate(cut):
        own = lax.bitwise_and(lax.shift_right_logical(pos, bit.bit_length() - 1), 1)
        flip = (slot >> (len(cut) - 1 - k)) & 1
        number = number + (lax.bitwise_xor(own, flip) << k)
    return number


def attn_bwd_kernel(
    pos_ref,
    x_ref,
    packed_ref,
    probs_ref,
    ctx_low_ref,
    mixed_ref,
    sums_ref,
    *refs,
    head,
    cut,
    extra,
    unroll,
):
    grad_ref, keep_ref, send_ref, bias_ref, value_ref, weight_acc = refs[-6:]
    step = pl.program_id(0)
    seq = x_ref.shape[0]
    n_shards = packed_ref.shape[0]
    scale = HEAD_DIM**-0.5
    for t in range(n_shards):
        value_ref[t] = packed_ref[t, 0, 2 * HEAD_DIM : 3 * HEAD_DIM, :].T
    def one_shard(t, carry):
        ctx_low = ctx_low_ref[t, 0]
        total = jnp.sum(ctx_low.astype(f32) * mixed_ref[t, 0], axis=0, keepdims=True)
        probs = probs_ref[t, 0, 0]
        score_low = (probs.astype(f32) * (mm(value_ref[t], ctx_low) - total)).astype(bf16)
        grad_query = mm(packed_ref[t, 0, HEAD_DIM : 2 * HEAD_DIM, :], score_low) * scale
        grad_key = mm_nt(score_low, packed_ref[t, 0, :HEAD_DIM, :]) * scale
        grad_value = mm_nt(probs, ctx_low)
        grad_ref[t, 0, :HEAD_DIM, :] = grad_query.astype(bf16)
        grad_ref[t, 0, HEAD_DIM : 2 * HEAD_DIM, :] = grad_key.T.astype(bf16)
        grad_ref[t, 0, 2 * HEAD_DIM :, :] = grad_value.T.astype(bf16)
        return carry

    if unroll:
        for t in range(n_shards):
            one_shard(t, 0)
    else:
        lax.fori_loop(0, n_shards, one_shard, 0)

    @pl.when(step == 0)
    def _():
        weight_acc[...] = jnp.zeros_like(weight_acc)
        bias_ref[...] = sums_ref[...]

    ones = jnp.ones((8, seq), bf16)
    for t in range(n_shards):
        weight_acc[t] += mm(grad_ref[t, 0], x_ref[...])
        bias_ref[t, head : head + 1] += mm_nt(ones, grad_ref[t, 0])[:1]

    @pl.when(step == pl.num_programs(0) - 1)
    def _():
        slots = 1 << len(cut)
        half = slots // 2
        rows = PART_ROWS // slots
        for slot in range(slots):
            at = piece_number(pos_ref[0], slot, cut)
            ref = keep_ref if slot < half else send_ref
            for t in range(n_shards):
                ref[t, slot % half, :rows] = weight_acc[t, aligned(at, rows, 8), :].astype(bf16)
                if extra:
                    padded = jnp.concatenate(
                        [bias_ref[t], jnp.zeros((EXTRA, ref.shape[3] - PART_ROWS), f32)], axis=1
                    )
                    ref[t, slot % half, rows:] = padded.astype(bf16)


def attn_bwd(pos, x, packed, probs, ctx_low, mixed, sums, head, first, group, cut, extra, unroll, earlier):
    rows, width = x.shape
    n_shards, n_seq = packed.shape[:2]
    slots = 1 << len(cut)
    each = PART_ROWS // slots + (EXTRA if extra else 0)
    pieces = (n_shards, slots // 2, group * each, width)
    piece = pl.BlockSpec((n_shards, slots // 2, each, width), lambda s, pos: (0, 0, head - first, 0))
    sum_spec = pl.BlockSpec(sums.shape, lambda s, pos: (0, 0, 0))
    return pl.pallas_call(
        partial(attn_bwd_kernel, head=head, cut=cut, extra=extra, unroll=unroll),
        grid_spec=pltpu.PrefetchScalarGridSpec(
            num_scalar_prefetch=1,
            grid=(n_seq,),
            in_specs=[
                pl.BlockSpec((SEQ_LEN, width), lambda s, pos: (s, 0)),
                pl.BlockSpec((n_shards, 1, PART_ROWS, SEQ_LEN), lambda s, pos: (0, s, head, 0)),
                pl.BlockSpec((n_shards, 1, 1, SEQ_LEN, SEQ_LEN), lambda s, pos: (0, s, head, 0, 0)),
                pl.BlockSpec((n_shards, 1, HEAD_DIM, SEQ_LEN), lambda s, pos: (0, s, head, 0)),
                pl.BlockSpec((n_shards, 1, HEAD_DIM, SEQ_LEN), lambda s, pos: (0, s, head, 0)),
                sum_spec,
            ]
            + [pl.BlockSpec(memory_space=pl.ANY)] * len(earlier),
            out_specs=[
                pl.BlockSpec((n_shards, 1, PART_ROWS, SEQ_LEN), lambda s, pos: (0, s, 0, 0)),
                piece,
                piece,
                sum_spec,
            ],
            scratch_shapes=[
                pltpu.VMEM((n_shards, SEQ_LEN, HEAD_DIM), bf16),
                pltpu.VMEM((n_shards, PART_ROWS, width), f32),
            ],
        ),
        out_shape=[
            jax.ShapeDtypeStruct((n_shards, n_seq, PART_ROWS, SEQ_LEN), bf16),
            jax.ShapeDtypeStruct(pieces, bf16),
            jax.ShapeDtypeStruct(pieces, bf16),
            jax.ShapeDtypeStruct(sums.shape, f32),
        ],
        input_output_aliases={7: 1, 8: 2} if earlier else {},
        compiler_params=kernel_params(51_000_000),
        cost_estimate=cost(8 << 30, 10 << 20),
        name="attn_bwd",
    )(pos, x, packed, probs, ctx_low, mixed, sums, *earlier)


def input_grad_kernel(pos_ref, grad_one_ref, own_ref, *refs, n_others):
    fetched, grads, out_ref, got_ref = refs[: 2 * n_others], refs[2 * n_others : -2], refs[-2], refs[-1]
    half = own_ref.shape[0] // 2

    @pl.when(pl.program_id(0) == 0)
    def _():
        parity = lax.rem(pos_ref[0], 2)
        for t in range(n_others):
            for k in range(2):
                side = parity if k == 0 else 1 - parity
                got_ref[t, aligned(side, half, half), :] = fetched[2 * t + k][:half]

    total = grad_one_ref[...]
    for t in range(n_others + 1):
        weight = own_ref if t == 0 else got_ref.at[t - 1]
        total = total + mm_tn(jnp.concatenate([ref[t, 0] for ref in grads], axis=0), weight[...])
    out_ref[...] = total.astype(bf16)


def input_gradient(pos, grad_one, own, fetched, packed_grads):
    rows, width = grad_one.shape
    n_shards = packed_grads[0].shape[0]
    block = 512
    per_seq = SEQ_LEN // block
    row = pl.BlockSpec((block, width), lambda i, pos: (i, 0))
    cols = pl.BlockSpec((n_shards, 1, PART_ROWS, block), lambda i, pos: (0, i // per_seq, 0, i % per_seq))

    def whole(array):
        return pl.BlockSpec(array.shape, lambda i, pos: (0, 0), pipeline_mode=pl.Buffered(1))

    return pl.pallas_call(
        partial(input_grad_kernel, n_others=n_shards - 1),
        grid_spec=pltpu.PrefetchScalarGridSpec(
            num_scalar_prefetch=1,
            grid=(rows // block,),
            in_specs=[row, whole(own)] + [whole(v) for v in fetched] + [cols] * len(packed_grads),
            out_specs=row,
            scratch_shapes=[pltpu.VMEM((n_shards - 1,) + own.shape, bf16)],
        ),
        out_shape=jax.ShapeDtypeStruct((rows, width), bf16),
        compiler_params=kernel_params(51_000_000),
        cost_estimate=cost(4 << 30, 12 << 20),
        name="input_gradient",
    )(pos, grad_one, own, *fetched, *packed_grads)


def mlp_place_kernel(pos_ref, dn_near, dn_far, up_near, up_far, proj_out, up_out, dn_out):
    low = lax.rem(pos_ref[0], MLP_SLOTS)
    half = MLP_SLOTS // 2
    width = proj_out.shape[1]
    hidden = dn_out.shape[0]
    dn_rows, up_rows, proj_rows = hidden // MLP_SLOTS, width // MLP_SLOTS, proj_out.shape[0] // MLP_SLOTS
    for slot in range(MLP_SLOTS):
        dn_ref = dn_near if slot < half else dn_far
        up_ref = up_near if slot < half else up_far
        k = slot % half
        at = lax.bitwise_xor(low, DOWN_BITS[slot])
        dn_out[aligned(at, dn_rows, dn_rows), :] = dn_ref[k, :dn_rows].astype(f32)
        proj_out[aligned(at, proj_rows, proj_rows), :] = dn_ref[k, dn_rows:].astype(f32)
        rows = aligned(lax.bitwise_xor(low, UP_BITS[slot]), up_rows, up_rows)
        for j in range(hidden // width):
            up_out[rows, j * width : (j + 1) * width] = up_ref[k, j * up_rows : (j + 1) * up_rows].astype(f32)


def mlp_place(pos, dn_parts, up_parts, ctx_rows, width, hidden):
    return pl.pallas_call(
        mlp_place_kernel,
        in_specs=[pl.BlockSpec(memory_space=pltpu.SMEM)] + [in_vmem()] * 4,
        out_specs=[in_vmem()] * 3,
        out_shape=[
            jax.ShapeDtypeStruct((ctx_rows, width), f32),
            jax.ShapeDtypeStruct((width, hidden), f32),
            jax.ShapeDtypeStruct((hidden, width), f32),
        ],
        compiler_params=kernel_params(51_000_000),
        cost_estimate=cost(0, 14 << 20),
        name="mlp_place",
    )(pos, *dn_parts, *up_parts)


def qkv_place_kernel(pos_ref, *refs, groups):
    bias_ref, out_ref, query_ref, value_ref = refs[-4:]
    for g, (first, group, cut, each) in enumerate(groups):
        slots = 1 << len(cut)
        half = slots // 2
        rows = PART_ROWS // slots
        for slot in range(slots):
            at = aligned(piece_number(pos_ref[0], slot, cut), rows, 8)
            for k in range(group):
                value = refs[2 * g + slot // half][slot % half, k * each : k * each + rows]
                out_ref[first + k, at, :] = value.astype(f32)
    heads = out_ref.shape[0]
    for k, ref in ((0, query_ref), (2, value_ref)):
        parts = [bias_ref[h : h + 1, k * HEAD_DIM : (k + 1) * HEAD_DIM] for h in range(heads)]
        ref[...] = jnp.concatenate(parts, axis=1).reshape(heads * HEAD_DIM)


def qkv_place(pos, parts, bias, groups, heads):
    flat = [half for pair in parts for half in pair]
    vector = jax.ShapeDtypeStruct((heads * HEAD_DIM,), f32)
    return pl.pallas_call(
        partial(qkv_place_kernel, groups=groups),
        in_specs=[pl.BlockSpec(memory_space=pltpu.SMEM)] + [in_vmem()] * (len(flat) + 1),
        out_specs=[in_vmem()] * 3,
        out_shape=[jax.ShapeDtypeStruct((heads, PART_ROWS, flat[0].shape[2]), f32), vector, vector],
        compiler_params=kernel_params(51_000_000),
        cost_estimate=cost(0, 3 << 20),
        name="qkv_place",
    )(pos, *flat, bias)


def swap_dp(value, bits, n_dp):
    return lax.ppermute(value, "dp", [(i, i ^ bits) for i in range(n_dp)])


def shift_tensor(value, by, n_tensor):
    return lax.ppermute(value, "tensor", [((i + by) % n_tensor, i) for i in range(n_tensor)])


def reduce_pieces(keep, send, order, n_dp, n_tensor):
    halved = [axis for axis in order if axis != "tensor"]
    got = swap_dp(send, 1, n_dp)
    got = after(got, (yield send))
    parts = [keep[t].astype(f32) + got[t].astype(f32) for t in range(n_tensor)]
    for axis in order:
        if axis == "tensor":
            outs = [parts[by].astype(bf16) for by in range(1, n_tensor)]
            gots = [shift_tensor(out, -by, n_tensor) for by, out in enumerate(outs, 1)]
            gots = after(gots, (yield outs))
            parts = [sum((got.astype(f32) for got in gots), parts[0])]
        else:
            cut = parts[0].shape[0] // 2
            out = jnp.stack([part[cut:].astype(bf16) for part in parts])
            got = swap_dp(out, axis, n_dp)
            got = after(got, (yield out))
            parts = [part[:cut] + got[t].astype(f32) for t, part in enumerate(parts)]
    own = parts[0]
    bits = 2
    while bits < n_dp:
        if bits not in halved:
            out = own.astype(bf16)
            got = swap_dp(out, bits, n_dp)
            got = after(got, (yield out))
            own = own + got.astype(f32)
        bits *= 2
    near = own.astype(bf16)
    for axis in reversed(halved):
        got = swap_dp(near, axis, n_dp)
        got = after(got, (yield near))
        near = jnp.concatenate([near, got], axis=0)
    got = swap_dp(near, 1, n_dp)
    got = after(got, (yield near))
    return near, got, own


class Sums:
    def __init__(self):
        self.live, self.done, self.fresh = {}, {}, set()

    def add(self, name, generator):
        self.live[name] = generator
        self.fresh.add(name)

    def step(self, ready, *names):
        sent = []
        for name in names:
            if name in self.live:
                try:
                    sent.append(self.live[name].send(None if name in self.fresh else ready))
                    self.fresh.discard(name)
                except StopIteration as stop:
                    self.done[name] = stop.value
                    del self.live[name]
        return sent

    def finish(self):
        while self.live:
            self.step((), *list(self.live))


def after(value, *others):
    return lax.optimization_barrier((value, others))[0]


def sequence_body(n_dp, n_tensor, *arrays):
    (
        layer_input,
        output_grad,
        qkv_weight,
        query_bias,
        value_bias,
        proj_weight,
        proj_bias,
        first_gain,
        first_shift,
        up_weight,
        up_bias,
        down_weight,
        down_bias,
        second_gain,
        second_shift,
    ) = arrays
    rows, width = layer_input.shape
    n_seq = rows // SEQ_LEN
    ctx_rows, hidden = proj_weight.shape[0], up_weight.shape[1]
    n_heads = ctx_rows // HEAD_DIM
    pos = lax.axis_index("dp").astype(jnp.int32).reshape(1)
    shifts = range(1, n_tensor)

    vectors = [proj_bias, first_gain, first_shift, down_bias, second_gain, second_shift]
    qkv_half, own_bias, mlp_half, vecs = pack(
        pos, qkv_weight, query_bias, value_bias, proj_weight, down_weight, up_weight, up_bias, vectors
    )
    qkv_near = [shift_tensor(qkv_half, by, n_tensor) for by in shifts]
    shapes = [
        jax.ShapeDtypeStruct((n_tensor, n_seq, n_heads * PART_ROWS, SEQ_LEN), bf16),
        jax.ShapeDtypeStruct((n_tensor, n_seq, n_heads, SEQ_LEN, SEQ_LEN), bf16),
        jax.ShapeDtypeStruct((n_tensor, n_seq, n_heads * HEAD_DIM, SEQ_LEN), bf16),
        jax.ShapeDtypeStruct((n_tensor, n_seq, n_heads * HEAD_DIM, SEQ_LEN), f32),
    ]
    mlp_near = [shift_tensor(mlp_half, by, n_tensor) for by in shifts]
    x = after(layer_input, mlp_half)
    stacks = attn_fwd(pos, x, (qkv_weight, own_bias), 0, False, shapes, ())
    qkv_near = after(qkv_near, stacks[2])
    qkv_far = [swap_dp(near, 1, n_dp) for near in qkv_near]
    for t in shifts:
        stacks = attn_fwd(pos, layer_input, (qkv_near[t - 1], qkv_far[t - 1]), t, True, shapes, stacks)
    packed, probs, ctx, mixed = stacks
    mlp_near = after(mlp_near, ctx)
    mlp_far = [swap_dp(near, 1, n_dp) for near in mlp_near]
    fetched = [half for pair in zip(mlp_near, mlp_far) for half in pair]
    result, grad_one, ctx_low, dn_keep, dn_send, up_keep, up_send = middle(
        pos, layer_input, output_grad, ctx, vecs, proj_weight, up_weight, down_weight, fetched
    )
    sums = Sums()
    sums.add("dn", reduce_pieces(dn_keep, dn_send, DOWN_ORDER, n_dp, n_tensor))
    sums.add("up", reduce_pieces(up_keep, up_send, UP_ORDER, n_dp, n_tensor))
    bias_sums = jnp.zeros((n_tensor, EXTRA, PART_ROWS), f32)
    packed_grads = []
    ready = ()
    early = n_heads - 1
    stacked = ()
    early_cut, early_order = (1, 2), ("tensor", 2)
    for head in range(n_heads):
        last = head == early
        if last and early:
            sums.add("qa", reduce_pieces(*stacked, early_order, n_dp, n_tensor))
        sent = sums.step(ready, *SCHEDULE[min(head, len(SCHEDULE) - 3)])
        x = after(layer_input, sent)
        grads, keep, send, bias_sums = attn_bwd(
            pos,
            x,
            packed,
            probs,
            ctx_low,
            mixed,
            bias_sums,
            head,
            early if last else 0,
            1 if last else early,
            (1,) if last else early_cut,
            last,
            head in UNROLLED,
            () if last else stacked,
        )
        ready = bias_sums
        packed_grads.append(grads)
        if not last:
            stacked = (keep, send)
    sums.add("qb", reduce_pieces(keep, send, ("tensor",), n_dp, n_tensor))
    sent = sums.step(ready, *SCHEDULE[-2])
    qkv_fetched = [half for pair in zip(qkv_near, qkv_far) for half in pair]
    input_grad = input_gradient(pos, after(grad_one, sent), qkv_weight, qkv_fetched, packed_grads)
    ready = input_grad
    for name in SCHEDULE[-1]:
        sent = sums.step(ready, name)
        ready = sent or ready
    sums.finish()
    dn_near, dn_far, _ = sums.done["dn"]
    up_near, up_far, up_own = sums.done["up"]
    proj_wg, up_wg, dn_wg = mlp_place(pos, (dn_near, dn_far), (up_near, up_far), ctx_rows, width, hidden)
    groups = [(0, early, early_cut, PART_ROWS // 4)] if early else []
    groups.append((early, 1, (1,), PART_ROWS // 2 + EXTRA))
    parts = [sums.done[name][:2] for name in ("qa", "qb") if name in sums.done]
    bias = sums.done["qb"][2][0, -EXTRA:]
    qkv_wg, query_bg, value_bg = qkv_place(pos, parts, bias, groups, n_heads)
    small = up_own[0, -EXTRA:]
    return (
        result,
        input_grad,
        qkv_wg.reshape(n_heads * PART_ROWS, width),
        query_bg,
        value_bg,
        proj_wg,
        small[0],
        small[1],
        small[2],
        up_wg,
        small[8 : 8 + hidden // width].reshape(hidden),
        dn_wg,
        small[3],
        small[4],
        small[5],
    )


SCHEDULE = (
    ("dn", "up"),
    ("dn", "up"),
    ("dn", "up"),
    ("qa", "dn", "up", "qa"),
    ("qb", "qa", "dn", "up", "qb"),
    ("qb", "qa", "dn", "up", "qb", "qa", "up", "dn", "qb", "qa", "up", "dn", "qb", "qa"),
)
UNROLLED = (0,)


def solution(mesh):
    n_dp, n_tensor = mesh.shape["dp"], mesh.shape["tensor"]

    def body(*arrays):
        rows = arrays[0].shape[0]
        if rows % SEQ_LEN == 0 and n_dp % 8 == 0 and n_dp & (n_dp - 1) == 0:
            return sequence_body(n_dp, n_tensor, *arrays)
        return token_body(*arrays)

    return jax.shard_map(
        body,
        mesh=mesh,
        in_specs=(
            P(("dp", "tensor"), None),
            P(("dp", "tensor"), None),
            P("tensor", None),
            P("tensor"),
            P("tensor"),
            P("tensor", None),
            P(),
            P(),
            P(),
            P(None, "tensor"),
            P("tensor"),
            P("tensor", None),
            P(),
            P(),
            P(),
        ),
        out_specs=(
            P(("dp", "tensor"), None),
            P(("dp", "tensor"), None),
            P("tensor", None),
            P("tensor"),
            P("tensor"),
            P("tensor", None),
            P(),
            P(),
            P(),
            P(None, "tensor"),
            P("tensor"),
            P("tensor", None),
            P(),
            P(),
            P(),
        ),
        check_vma=False,
    )
```

```python
from functools import partial

import jax
import jax.numpy as jnp
from jax import lax
from jax.experimental import pallas as pl
from jax.experimental.pallas import tpu as pltpu
from jax.sharding import PartitionSpec as P

HEAD_DIM = 64
SEQ_LEN = 1024
PART_ROWS = 3 * HEAD_DIM

norm_eps = 1e-05
f32 = jnp.float32
bf16 = jnp.bfloat16


def matmul_rows(left, right):
    return lax.dot_general(
        left, right, (((0,), (0,)), ((), ())), preferred_element_type=jnp.float32
    )


def matmul_back(left, right):
    return lax.dot_general(
        left, right, (((1,), (1,)), ((), ())), preferred_element_type=jnp.float32
    )


def attend_forward(queries, key_rows, value_rows):
    seq_heads = key_rows.shape[0] * key_rows.shape[1]
    head_dim = queries.shape[-1]
    score_scale = head_dim ** (-0.5)
    block_rows = min(512, SEQ_LEN)
    block_count = SEQ_LEN // block_rows
    item_count = seq_heads * block_count
    query_items = queries.reshape(item_count, block_rows, head_dim)
    key_all = key_rows.reshape(seq_heads, SEQ_LEN, head_dim)
    value_all = value_rows.reshape(seq_heads, SEQ_LEN, head_dim)

    def one_block(block_item):
        query_blk, position = block_item
        owner_index = position // block_count
        keys_here = key_all[owner_index]
        values_here = value_all[owner_index]
        scores = matmul_back(query_blk, keys_here) * score_scale
        row_top = jnp.max(scores, axis=-1, keepdims=True)
        exponent = jnp.exp(scores - row_top)
        row_total = jnp.sum(exponent, axis=-1, keepdims=True)
        weights_now = exponent / row_total
        mixed_rows = jnp.dot(
            weights_now.astype(jnp.bfloat16), values_here, preferred_element_type=jnp.float32
        )
        return (mixed_rows, row_top[:, 0] + jnp.log(row_total[:, 0]))

    mixed_rows, log_total = lax.map(
        one_block, (query_items, jnp.arange(item_count, dtype=jnp.int32))
    )
    return (mixed_rows.reshape(queries.shape), log_total.reshape(queries.shape[:-1]))


def attend_backward(queries, key_rows, value_rows, log_total, context_low):
    seq_heads = key_rows.shape[0] * key_rows.shape[1]
    head_dim = queries.shape[-1]
    score_scale = head_dim ** (-0.5)
    block_rows = min(512, SEQ_LEN)
    block_count = SEQ_LEN // block_rows
    item_count = seq_heads * block_count
    query_items = queries.reshape(item_count, block_rows, head_dim)
    total_items = log_total.reshape(item_count, block_rows)
    grad_items = context_low.reshape(item_count, block_rows, head_dim)
    key_all = key_rows.reshape(seq_heads, SEQ_LEN, head_dim)
    value_all = value_rows.reshape(seq_heads, SEQ_LEN, head_dim)

    def one_block(block_item):
        query_blk, total_blk, grad_blk, position = block_item
        owner_index = position // block_count
        keys_here = key_all[owner_index]
        values_here = value_all[owner_index]
        scores = matmul_back(query_blk, keys_here) * score_scale
        weights_now = jnp.exp(scores - total_blk[:, None])
        grad_weights = matmul_back(grad_blk, values_here)
        grad_scores = weights_now * (
            grad_weights - jnp.sum(weights_now * grad_weights, axis=-1, keepdims=True)
        )
        score_low = grad_scores.astype(jnp.bfloat16)
        grad_query = jnp.dot(score_low, keys_here, preferred_element_type=jnp.float32) * score_scale
        grad_key = matmul_rows(score_low, query_blk) * score_scale
        grad_value = matmul_rows(weights_now.astype(jnp.bfloat16), grad_blk)
        return (grad_query, grad_key, grad_value)

    grad_query, grad_key, grad_value = lax.map(
        one_block, (query_items, total_items, grad_items, jnp.arange(item_count, dtype=jnp.int32))
    )
    grad_key = jnp.sum(grad_key.reshape(seq_heads, block_count, SEQ_LEN, head_dim), axis=1)
    grad_value = jnp.sum(grad_value.reshape(seq_heads, block_count, SEQ_LEN, head_dim), axis=1)
    return (
        grad_query.reshape(queries.shape),
        grad_key.reshape(key_rows.shape),
        grad_value.reshape(value_rows.shape),
    )


def norm_forward(hidden, gain_vec, shift_vec):
    center = jnp.mean(hidden, axis=-1)
    second = jnp.mean(hidden * hidden, axis=-1) - center * center
    inv_std = lax.rsqrt(second + norm_eps)
    normal = (hidden - center[:, None]) * inv_std[:, None]
    return (normal * gain_vec + shift_vec, normal, inv_std)


def norm_backward(upstream, normal, inv_std, gain_vec):
    scaled = upstream * gain_vec
    first_mean = jnp.mean(scaled, axis=-1)
    second_mean = jnp.mean(scaled * normal, axis=-1)
    grad_in = inv_std[:, None] * (scaled - first_mean[:, None] - normal * second_mean[:, None])
    return (grad_in, jnp.sum(upstream * normal, axis=0), jnp.sum(upstream, axis=0))


def rows_in(value):
    return lax.all_gather(value, "tensor", axis=0, tiled=True)


def part_out(value):
    return lax.psum_scatter(value, "tensor", scatter_dimension=0, tiled=True)


def gather_grad(value):
    return lax.all_gather(value, "tensor", axis=0, tiled=True)


def part_back(value):
    return lax.psum_scatter(value, "tensor", scatter_dimension=0, tiled=True)


def token_body(
    layer_input,
    output_grad,
    qkv_weight,
    query_bias,
    value_bias,
    proj_weight,
    proj_bias,
    first_gain,
    first_shift,
    up_weight,
    up_bias,
    down_weight,
    down_bias,
    second_gain,
    second_shift,
):
    heads_here = query_bias.shape[0] // HEAD_DIM
    query_bf = query_bias.astype(jnp.float32).reshape(heads_here, HEAD_DIM)
    value_bf = value_bias.astype(jnp.float32).reshape(heads_here, HEAD_DIM)
    bias_rows = jnp.stack([query_bf, jnp.zeros_like(query_bf), value_bf], axis=1)
    gain_one = first_gain.astype(jnp.float32)
    shift_one = first_shift.astype(jnp.float32)
    gain_two = second_gain.astype(jnp.float32)
    shift_two = second_shift.astype(jnp.float32)
    input_full = rows_in(layer_input)
    row_count = input_full.shape[0]
    seq_count = row_count // SEQ_LEN
    projected = matmul_back(input_full, qkv_weight).reshape(row_count, heads_here, 3, HEAD_DIM)
    packed = (projected + bias_rows).astype(jnp.bfloat16)
    parts = packed.reshape(seq_count, SEQ_LEN, heads_here, 3, HEAD_DIM).transpose(3, 0, 2, 1, 4)
    queries, key_rows, value_rows = (parts[0], parts[1], parts[2])
    mixed_rows, log_total = attend_forward(queries, key_rows, value_rows)
    context = (
        mixed_rows.transpose(0, 2, 1, 3)
        .reshape(row_count, heads_here * HEAD_DIM)
        .astype(jnp.bfloat16)
    )
    partial_branch = jnp.dot(context, proj_weight, preferred_element_type=jnp.float32)
    branch = part_out(partial_branch) + proj_bias.astype(jnp.float32)
    normed_one, normal_one, inv_one = norm_forward(
        layer_input.astype(jnp.float32) + branch, gain_one, shift_one
    )
    normed_full = rows_in(normed_one.astype(jnp.bfloat16))
    inner_pre = jnp.dot(
        normed_full, up_weight, preferred_element_type=jnp.float32
    ) + up_bias.astype(jnp.float32)
    active, gelu_back = jax.vjp(partial(jax.nn.gelu, approximate=False), inner_pre)
    active_low = active.astype(jnp.bfloat16)
    second = part_out(
        jnp.dot(active_low, down_weight, preferred_element_type=jnp.float32)
    ) + down_bias.astype(jnp.float32)
    result_rows, normal_two, inv_two = norm_forward(normed_one + second, gain_two, shift_two)
    upstream = output_grad.astype(jnp.float32)
    grad_two, gain_two_grad, shift_two_grad = norm_backward(upstream, normal_two, inv_two, gain_two)
    second_low = grad_two.astype(jnp.bfloat16)
    down_b_grad = jnp.sum(second_low.astype(jnp.float32), axis=0)
    second_full = gather_grad(second_low)
    down_w_grad = matmul_rows(active_low, second_full)
    grad_active = matmul_back(second_full, down_weight)
    inner_low = gelu_back(grad_active)[0].astype(jnp.bfloat16)
    up_b_grad = jnp.sum(inner_low.astype(jnp.float32), axis=0)
    up_w_grad = matmul_rows(normed_full, inner_low)
    grad_mid = grad_two + part_back(matmul_back(inner_low, up_weight))
    grad_one, gain_one_grad, shift_one_grad = norm_backward(grad_mid, normal_one, inv_one, gain_one)
    branch_low = grad_one.astype(jnp.bfloat16)
    proj_b_grad = jnp.sum(branch_low.astype(jnp.float32), axis=0)
    branch_full = gather_grad(branch_low)
    proj_w_grad = matmul_rows(context, branch_full)
    context_low = matmul_back(branch_full, proj_weight).astype(jnp.bfloat16)
    context_low = context_low.reshape(seq_count, SEQ_LEN, heads_here, HEAD_DIM).transpose(
        0, 2, 1, 3
    )
    grad_query, grad_key, grad_value = attend_backward(
        queries, key_rows, value_rows, log_total, context_low
    )
    packed_low = jnp.stack([grad_query, grad_key, grad_value], axis=0).transpose(1, 3, 2, 0, 4)
    packed_low = packed_low.reshape(row_count, heads_here * 3 * HEAD_DIM).astype(jnp.bfloat16)
    packed_sums = jnp.sum(packed_low.astype(jnp.float32), axis=0).reshape(heads_here, 3, HEAD_DIM)
    query_b_grad = packed_sums[:, 0].reshape(heads_here * HEAD_DIM)
    value_b_grad = packed_sums[:, 2].reshape(heads_here * HEAD_DIM)
    qkv_w_grad = matmul_rows(packed_low, input_full)
    input_grad = (
        grad_one + part_back(jnp.dot(packed_low, qkv_weight, preferred_element_type=jnp.float32))
    ).astype(jnp.bfloat16)
    totals = (
        lax.psum(qkv_w_grad.astype(jnp.bfloat16), "dp").astype(jnp.float32),
        lax.psum(query_b_grad.astype(jnp.bfloat16), "dp").astype(jnp.float32),
        lax.psum(value_b_grad.astype(jnp.bfloat16), "dp").astype(jnp.float32),
        lax.psum(proj_w_grad.astype(jnp.bfloat16), "dp").astype(jnp.float32),
        lax.psum(up_w_grad.astype(jnp.bfloat16), "dp").astype(jnp.float32),
        lax.psum(up_b_grad.astype(jnp.bfloat16), "dp").astype(jnp.float32),
        lax.psum(down_w_grad.astype(jnp.bfloat16), "dp").astype(jnp.float32),
    )
    vectors = lax.psum(
        (proj_b_grad, gain_one_grad, shift_one_grad, down_b_grad, gain_two_grad, shift_two_grad),
        ("dp", "tensor"),
    )
    return (
        result_rows.astype(jnp.bfloat16),
        input_grad,
        totals[0],
        totals[1],
        totals[2],
        totals[3],
        vectors[0],
        vectors[1],
        vectors[2],
        totals[4],
        totals[5],
        totals[6],
        vectors[3],
        vectors[4],
        vectors[5],
    )


VMEM_LIMIT = 66_000_000
EXTRA = 16


def mm(left, right):
    return lax.dot_general(left, right, (((1,), (0,)), ((), ())), preferred_element_type=f32)


def mm_nt(left, right):
    return lax.dot_general(left, right, (((1,), (1,)), ((), ())), preferred_element_type=f32)


def mm_tn(left, right):
    return lax.dot_general(left, right, (((0,), (0,)), ((), ())), preferred_element_type=f32)


def kernel_params(limit=VMEM_LIMIT):
    return pltpu.CompilerParams(vmem_limit_bytes=limit)


def cost(flops, size):
    return pl.CostEstimate(flops=int(flops), bytes_accessed=int(size), transcendentals=0)


def in_vmem():
    return pl.BlockSpec(memory_space=pltpu.VMEM)


def aligned(start, size, by):
    return pl.ds(pl.multiple_of(start * size, by), size)


def pack_kernel(pos_ref, qkv_ref, query_b_ref, value_b_ref, proj_ref, down_ref, up_ref, up_b_ref, *refs):
    vec_refs, (qkv_out, own_b_ref, packed_ref, vecs_ref) = refs[:-4], refs[-4:]
    half = qkv_ref.shape[0]
    wide = query_b_ref.shape[0] // 2
    query_b, value_b = (ref[...].reshape(1, 2 * wide) for ref in (query_b_ref, value_b_ref))
    qkv_out[:half] = qkv_ref[...]
    qkv_out[half:] = jnp.zeros_like(qkv_out[half:])
    own_b_ref[...] = jnp.zeros_like(own_b_ref)
    parity = lax.rem(pos_ref[0], 2)
    for k in range(2):
        cols = slice(k * wide, (k + 1) * wide)
        own_b_ref[k * EXTRA : k * EXTRA + 1, :wide] = query_b[:, cols]
        own_b_ref[k * EXTRA : k * EXTRA + 1, wide : 2 * wide] = value_b[:, cols]

        @pl.when(parity == k)
        def _():
            qkv_out[half : half + 1, :wide] = query_b[:, cols]
            qkv_out[half : half + 1, wide : 2 * wide] = value_b[:, cols]

    width = proj_ref.shape[1]
    at = 0
    for value in (proj_ref[...], down_ref[...]):
        packed_ref[at : at + value.shape[0]] = value
        at += value.shape[0]
    blocks = up_ref.shape[1] // width
    for j in range(blocks):
        packed_ref[at : at + up_ref.shape[0]] = up_ref[:, j * width : (j + 1) * width]
        at += up_ref.shape[0]
    packed_ref[at:] = jnp.zeros_like(packed_ref[at:])
    vecs_ref[...] = jnp.zeros_like(vecs_ref)
    for j in range(blocks):
        row = up_b_ref[j * width : (j + 1) * width].reshape(1, width)
        packed_ref[at + j : at + j + 1] = row
        vecs_ref[8 + j : 9 + j] = row.astype(f32)
    for k, ref in enumerate(vec_refs):
        vecs_ref[k : k + 1] = ref[...].reshape(1, width).astype(f32)


def pack(pos, qkv, query_b, value_b, proj, down, up, up_b, vectors):
    width, hidden = up.shape
    qkv_rows = qkv.shape[0] // 2 + EXTRA
    mlp_rows = (proj.shape[0] + 2 * hidden) // 2 + EXTRA

    def half(array):
        return pl.BlockSpec((array.shape[0] // 2, array.shape[1]), lambda i, pos: (lax.rem(pos[0], 2), 0))

    def whole(array):
        return pl.BlockSpec(array.shape, lambda i, pos: (0,))

    outs = [(qkv_rows, bf16), (2 * EXTRA, bf16), (mlp_rows, bf16), (EXTRA, f32)]
    return pl.pallas_call(
        pack_kernel,
        grid_spec=pltpu.PrefetchScalarGridSpec(
            num_scalar_prefetch=1,
            grid=(1,),
            in_specs=[half(qkv), whole(query_b), whole(value_b), half(proj), half(down), half(up), whole(up_b)]
            + [whole(v) for v in vectors],
            out_specs=[pl.BlockSpec((rows, width), lambda i, pos: (0, 0)) for rows, _ in outs],
        ),
        out_shape=[jax.ShapeDtypeStruct((rows, width), dtype) for rows, dtype in outs],
        compiler_params=kernel_params(),
        cost_estimate=cost(0, 4 << 20),
        name="pack",
    )(pos, qkv, query_b, value_b, proj, down, up, up_b, *vectors)


def attn_fwd_kernel(pos_ref, x_ref, *refs, heads, q_block, fetched):
    packed_ref, probs_ref, ctx_ref, mixed_ref, key_ref, score_a, score_b = refs[-7:]
    seq = x_ref.shape[0]
    scale = HEAD_DIM**-0.5
    wide = heads * HEAD_DIM
    part = heads * PART_ROWS
    if fetched:
        near = pl.program_id(1) == 0
        weight = jnp.where(near, refs[0][:part], refs[1][:part])
        bias = jnp.where(near, refs[0][part:].astype(f32), refs[1][part:].astype(f32))
    else:
        weight, bias = refs[0][...], refs[1][...].astype(f32)
    column = bias[:8, : 2 * wide].T
    raw = mm_nt(weight, x_ref[...])
    for h in range(heads):
        base = h * PART_ROWS
        ends = (base + HEAD_DIM, base + 2 * HEAD_DIM, base + PART_ROWS)
        query = raw[base : ends[0]] + column[h * HEAD_DIM : (h + 1) * HEAD_DIM, :1]
        value = raw[ends[1] : ends[2]] + column[wide + h * HEAD_DIM : wide + (h + 1) * HEAD_DIM, :1]
        packed_ref[0, 0, base : ends[0]] = query.astype(bf16)
        packed_ref[0, 0, ends[0] : ends[1]] = raw[ends[0] : ends[1]].astype(bf16)
        packed_ref[0, 0, ends[1] : ends[2]] = value.astype(bf16)
        keys = packed_ref[0, 0, ends[0] : ends[1], :].astype(f32)
        key_ref[h] = (keys.T * scale).astype(bf16)
    tiles = [(h, c) for h in range(heads) for c in range(0, seq, q_block)]
    scores = (score_a, score_b)

    def score(tile, ref):
        h, c = tile
        base = h * PART_ROWS
        ref[...] = mm(key_ref[h], packed_ref[0, 0, base : base + HEAD_DIM, c : c + q_block])

    def finish(tile, ref):
        h, c = tile
        base = h * PART_ROWS
        top = jnp.max(ref[...], axis=0, keepdims=True)
        exponent = jnp.exp(ref[...] - top)
        total = jnp.sum(exponent, axis=0, keepdims=True)
        probs = (exponent * (1.0 / total)).astype(bf16)
        probs_ref[0, 0, h, :, c : c + q_block] = probs
        mixed = mm(packed_ref[0, 0, base + 2 * HEAD_DIM : base + 3 * HEAD_DIM, :], probs)
        ctx_ref[0, 0, h * HEAD_DIM : (h + 1) * HEAD_DIM, c : c + q_block] = mixed.astype(bf16)
        mixed_ref[0, 0, h * HEAD_DIM : (h + 1) * HEAD_DIM, c : c + q_block] = mixed

    score(tiles[0], scores[0])
    for j, tile in enumerate(tiles):
        if j + 1 < len(tiles):
            score(tiles[j + 1], scores[(j + 1) % 2])
        finish(tile, scores[j % 2])


def attn_fwd(pos, x, sources, shard, fetched, shapes, earlier):
    rows, width = x.shape
    n_seq = rows // SEQ_LEN
    heads = shapes[1].shape[2] // 2
    part = heads * PART_ROWS

    def at(k, pos):
        return lax.bitwise_xor(k, lax.rem(pos[0], 2)) if fetched else k

    if fetched:
        sizes = [pl.BlockSpec(v.shape, lambda s, k, pos: (0, 0), pipeline_mode=pl.Buffered(1)) for v in sources]
    else:
        sizes = [pl.BlockSpec((size, width), lambda s, k, pos: (k, 0)) for size in (part, EXTRA)]
    out_specs = [
        pl.BlockSpec((1, 1, part, SEQ_LEN), lambda s, k, pos: (shard, s, at(k, pos), 0)),
        pl.BlockSpec((1, 1, heads, SEQ_LEN, SEQ_LEN), lambda s, k, pos: (shard, s, at(k, pos), 0, 0)),
    ] + [pl.BlockSpec((1, 1, heads * HEAD_DIM, SEQ_LEN), lambda s, k, pos: (shard, s, at(k, pos), 0))] * 2
    q_block = 1024
    share = 2 * n_seq * heads
    flops = share * (2 * SEQ_LEN * width * PART_ROWS + 4 * SEQ_LEN * SEQ_LEN * HEAD_DIM * 6)
    return pl.pallas_call(
        partial(attn_fwd_kernel, heads=heads, q_block=q_block, fetched=fetched),
        grid_spec=pltpu.PrefetchScalarGridSpec(
            num_scalar_prefetch=1,
            grid=(n_seq, 2),
            in_specs=[pl.BlockSpec((SEQ_LEN, width), lambda s, k, pos: (s, 0))]
            + sizes
            + [pl.BlockSpec(memory_space=pl.ANY)] * len(earlier),
            out_specs=out_specs,
            scratch_shapes=[
                pltpu.VMEM((heads, SEQ_LEN, HEAD_DIM), bf16),
                pltpu.VMEM((SEQ_LEN, q_block), f32),
                pltpu.VMEM((SEQ_LEN, q_block), f32),
            ],
        ),
        out_shape=shapes,
        input_output_aliases={4 + k: k for k in range(len(earlier))},
        compiler_params=kernel_params(),
        cost_estimate=cost(flops // 8 if fetched else flops, share * 3 << 20),
        name="attn_fwd",
    )(pos, x, *sources, *earlier)


def piece_bits(*order):
    bits = [0]
    for bit in reversed(order):
        bits = bits + [b | bit for b in bits]
    return bits


MLP_SLOTS = 8
DOWN_ORDER = ("tensor", 2, 4)
UP_ORDER = (4, "tensor", 2)
DOWN_BITS = piece_bits(1, 2, 4)
UP_BITS = piece_bits(1, 4, 2)


def middle_kernel(
    pos_ref,
    x_ref,
    og_ref,
    ctx_ref,
    vecs_ref,
    proj_own,
    up_own,
    down_own,
    *refs,
    n_others,
    chunk,
):
    fetched, refs = refs[: 2 * n_others], refs[2 * n_others :]
    out_ref, grad_one_ref, ctx_low_ref, dn_keep_ref, dn_send_ref, up_keep_ref, up_send_ref, *refs = refs
    proj_got, up_got, down_got, up_b_ref, act_ref, slope_ref, proj_acc, up_acc, dn_acc, vec_acc, up_b_acc = refs
    step = pl.program_id(0)
    n_shards = n_others + 1
    ctx_rows, width = proj_own.shape
    hidden = up_own.shape[1]
    blocks = hidden // width
    inv_width = 1.0 / width

    def mean(v):
        return jnp.sum(v, axis=1, keepdims=True) * inv_width

    @pl.when(step == 0)
    def _():
        for ref in (proj_acc, up_acc, dn_acc):
            size = min(64, ref.shape[1])

            def clear(i, carry, ref=ref, size=size):
                for t in range(n_shards):
                    ref[t, aligned(i, size, size), :] = jnp.zeros((size, ref.shape[2]), f32)
                return carry

            lax.fori_loop(0, ref.shape[1] // size, clear, 0)
        for ref in (vec_acc, up_b_acc):
            ref[...] = jnp.zeros_like(ref)
        parity = lax.rem(pos_ref[0], 2)
        for j in range(blocks):
            up_b_ref[:, j * width : (j + 1) * width] = vecs_ref[8 + j : 9 + j, :]
        for t in range(n_others):
            for k in range(2):
                ref = fetched[2 * t + k]
                side = parity if k == 0 else 1 - parity
                rows = ctx_rows // 2
                proj_got[t, aligned(side, rows, rows), :] = ref[:rows]
                at = rows
                rows = hidden // 2
                down_got[t, aligned(side, rows, rows), :] = ref[at : at + rows]
                at += rows
                rows = width // 2
                for j in range(blocks):
                    up_got[t, aligned(side, rows, rows), j * width : (j + 1) * width] = ref[at : at + rows]
                    at += rows
                if k == 0:
                    for j in range(blocks):
                        to = (t + 1) * hidden + j * width
                        up_b_ref[:, to : to + width] = ref[at : at + EXTRA].astype(f32)[j : j + 1]

    def proj(t):
        return proj_own[...] if t == 0 else proj_got[t - 1]

    def up(t, c):
        return up_own[:, c : c + chunk] if t == 0 else up_got[t - 1, :, c : c + chunk]

    def down(t, c):
        return down_own[c : c + chunk, :] if t == 0 else down_got[t - 1, c : c + chunk, :]

    proj_b, gain_one, shift_one, down_b, gain_two, shift_two = (vecs_ref[k : k + 1, :] for k in range(6))
    branch = proj_b
    for t in range(n_shards):
        branch = branch + mm_tn(ctx_ref[t, 0], proj(t))
    mid_sum = x_ref[...].astype(f32) + branch
    center = mean(mid_sum)
    inv_one = lax.rsqrt(mean(mid_sum * mid_sum) - center * center + norm_eps)
    normal_one = (mid_sum - center) * inv_one
    normed_one = normal_one * gain_one + shift_one
    normed_low = normed_one.astype(bf16)
    second = down_b
    chunks = [(t, c) for t in range(n_shards) for c in range(0, hidden, chunk)]
    for t, c in chunks:
        at = t * hidden + c
        inner = mm(normed_low, up(t, c)) + up_b_ref[:, at : at + chunk]
        phi = 0.5 * lax.erf(inner * 0.7071067811865476) + 0.5
        active = (inner * phi).astype(bf16)
        act_ref[:, at : at + chunk] = active
        slope_ref[:, at : at + chunk] = phi + inner * (0.3989422804014327 * jnp.exp(-0.5 * inner * inner))
        second = second + mm(active, down(t, c))
    last_sum = normed_one + second
    center_two = mean(last_sum)
    inv_two = lax.rsqrt(mean(last_sum * last_sum) - center_two * center_two + norm_eps)
    normal_two = (last_sum - center_two) * inv_two
    out_ref[...] = (normal_two * gain_two + shift_two).astype(bf16)
    upstream = og_ref[...].astype(f32)
    scaled = upstream * gain_two
    grad_two = inv_two * (scaled - mean(scaled) - normal_two * mean(scaled * normal_two))
    second_low = grad_two.astype(bf16)
    normed_t = normed_low.T
    back = None
    for t, c in chunks:
        at = t * hidden + c
        grad_active = mm_nt(second_low, down(t, c))
        inner_low = (grad_active * slope_ref[:, at : at + chunk]).astype(bf16)
        up_b_acc[:, at : at + chunk] += jnp.sum(inner_low.astype(f32), axis=0, keepdims=True)
        part = mm_nt(inner_low, up(t, c))
        back = part if back is None else back + part
        up_acc[t, :, c : c + chunk] += mm(normed_t, inner_low)
        dn_acc[t, c : c + chunk, :] += mm_tn(act_ref[:, at : at + chunk], second_low)
    grad_mid = grad_two + back
    scaled_one = grad_mid * gain_one
    grad_one = inv_one * (scaled_one - mean(scaled_one) - normal_one * mean(scaled_one * normal_one))
    grad_one_ref[...] = grad_one
    branch_low = grad_one.astype(bf16)
    sums = (
        branch_low.astype(f32),
        grad_mid * normal_one,
        grad_mid,
        second_low.astype(f32),
        upstream * normal_two,
        upstream,
    )
    for k, value in enumerate(sums):
        vec_acc[k : k + 1, :] += jnp.sum(value, axis=0, keepdims=True)
    for t in range(n_shards):
        ctx_low_ref[t, 0] = mm_nt(proj(t), branch_low).astype(bf16)
        proj_acc[t] += mm(ctx_ref[t, 0], branch_low)

    @pl.when(step == pl.num_programs(0) - 1)
    def _():
        low = lax.rem(pos_ref[0], MLP_SLOTS)
        dn_rows, up_rows, proj_rows = hidden // MLP_SLOTS, width // MLP_SLOTS, ctx_rows // MLP_SLOTS
        half = MLP_SLOTS // 2
        tails = []
        for t in range(n_shards):
            rest = [up_b_acc[:, t * hidden + j * width : t * hidden + (j + 1) * width] for j in range(blocks)]
            tails.append(jnp.concatenate([vec_acc[...], *rest, jnp.zeros((8 - blocks, width), f32)], axis=0).astype(bf16))

        for side, (dn_ref, upk_ref) in enumerate(((dn_keep_ref, up_keep_ref), (dn_send_ref, up_send_ref))):

            def emit(k, carry, side=side, dn_ref=dn_ref, upk_ref=upk_ref):
                first, second = lax.shift_right_logical(k, 1), lax.bitwise_and(k, 1)
                dn_at = lax.bitwise_xor(low, side + 2 * first + 4 * second)
                up_at = lax.bitwise_xor(low, side + 4 * first + 2 * second)
                rows = aligned(up_at, up_rows, up_rows)
                for t in range(n_shards):
                    dn_ref[t, k, :dn_rows] = dn_acc[t, aligned(dn_at, dn_rows, dn_rows), :].astype(bf16)
                    dn_ref[t, k, dn_rows:] = proj_acc[t, aligned(dn_at, proj_rows, proj_rows), :].astype(bf16)
                    for j in range(blocks):
                        to = j * up_rows
                        upk_ref[t, k, to : to + up_rows] = up_acc[t, rows, j * width : (j + 1) * width].astype(bf16)
                    upk_ref[t, k, blocks * up_rows :] = tails[t]
                return carry

            lax.fori_loop(0, half, emit, 0)


def middle(pos, x, out_grad, ctx, vecs, proj, up, down, fetched):
    rows, width = x.shape
    n_shards, n_seq, ctx_rows, _ = ctx.shape
    hidden = up.shape[1]
    n_others = n_shards - 1
    block = 512
    per_seq = SEQ_LEN // block
    half = MLP_SLOTS // 2
    dn_rows, up_rows = (hidden + ctx_rows) // MLP_SLOTS, hidden // MLP_SLOTS + EXTRA

    def whole(array):
        return pl.BlockSpec(array.shape, lambda i, pos: (0,) * array.ndim, pipeline_mode=pl.Buffered(1))

    def kept(*shape):
        return pl.BlockSpec(shape, lambda i, pos: (0,) * len(shape))

    row = pl.BlockSpec((block, width), lambda i, pos: (i, 0))
    cols = pl.BlockSpec((n_shards, 1, ctx_rows, block), lambda i, pos: (0, i // per_seq, 0, i % per_seq))
    dn_shape, up_shape = (n_shards, half, dn_rows, width), (n_shards, half, up_rows, width)
    consts = [vecs, proj, up, down] + fetched
    return pl.pallas_call(
        partial(middle_kernel, n_others=n_others, chunk=min(1024, hidden)),
        grid_spec=pltpu.PrefetchScalarGridSpec(
            num_scalar_prefetch=1,
            grid=(rows // block,),
            in_specs=[row, row, cols] + [whole(array) for array in consts],
            out_specs=[row, row, cols, kept(*dn_shape), kept(*dn_shape), kept(*up_shape), kept(*up_shape)],
            scratch_shapes=[
                pltpu.VMEM((n_others, ctx_rows, width), bf16),
                pltpu.VMEM((n_others, width, hidden), bf16),
                pltpu.VMEM((n_others, hidden, width), bf16),
                pltpu.VMEM((1, n_shards * hidden), f32),
                pltpu.VMEM((block, n_shards * hidden), bf16),
                pltpu.VMEM((block, n_shards * hidden), f32),
                pltpu.VMEM((n_shards, ctx_rows, width), f32),
                pltpu.VMEM((n_shards, width, hidden), f32),
                pltpu.VMEM((n_shards, hidden, width), f32),
                pltpu.VMEM((8, width), f32),
                pltpu.VMEM((1, n_shards * hidden), f32),
            ],
        ),
        out_shape=[
            jax.ShapeDtypeStruct((rows, width), bf16),
            jax.ShapeDtypeStruct((rows, width), f32),
            jax.ShapeDtypeStruct(ctx.shape, bf16),
            jax.ShapeDtypeStruct(dn_shape, bf16),
            jax.ShapeDtypeStruct(dn_shape, bf16),
            jax.ShapeDtypeStruct(up_shape, bf16),
            jax.ShapeDtypeStruct(up_shape, bf16),
        ],
        compiler_params=kernel_params(),
        cost_estimate=cost(30 << 30, 30 << 20),
        name="middle",
    )(pos, x, out_grad, ctx, *consts)


def piece_number(pos, slot, cut):
    number = 0
    for k, bit in enumerate(cut):
        own = lax.bitwise_and(lax.shift_right_logical(pos, bit.bit_length() - 1), 1)
        flip = (slot >> (len(cut) - 1 - k)) & 1
        number = number + (lax.bitwise_xor(own, flip) << k)
    return number


def attn_bwd_kernel(
    pos_ref,
    x_ref,
    packed_ref,
    probs_ref,
    ctx_low_ref,
    mixed_ref,
    sums_ref,
    *refs,
    head,
    cut,
    extra,
    unroll,
):
    grad_ref, keep_ref, send_ref, bias_ref, value_ref, weight_acc = refs[-6:]
    step = pl.program_id(0)
    seq = x_ref.shape[0]
    n_shards = packed_ref.shape[0]
    scale = HEAD_DIM**-0.5
    for t in range(n_shards):
        value_ref[t] = packed_ref[t, 0, 2 * HEAD_DIM : 3 * HEAD_DIM, :].T
    def one_shard(t, carry):
        ctx_low = ctx_low_ref[t, 0]
        total = jnp.sum(ctx_low.astype(f32) * mixed_ref[t, 0], axis=0, keepdims=True)
        probs = probs_ref[t, 0, 0]
        score_low = (probs.astype(f32) * (mm(value_ref[t], ctx_low) - total)).astype(bf16)
        grad_query = mm(packed_ref[t, 0, HEAD_DIM : 2 * HEAD_DIM, :], score_low) * scale
        grad_key = mm_nt(score_low, packed_ref[t, 0, :HEAD_DIM, :]) * scale
        grad_value = mm_nt(probs, ctx_low)
        grad_ref[t, 0, :HEAD_DIM, :] = grad_query.astype(bf16)
        grad_ref[t, 0, HEAD_DIM : 2 * HEAD_DIM, :] = grad_key.T.astype(bf16)
        grad_ref[t, 0, 2 * HEAD_DIM :, :] = grad_value.T.astype(bf16)
        return carry

    if unroll:
        for t in range(n_shards):
            one_shard(t, 0)
    else:
        lax.fori_loop(0, n_shards, one_shard, 0)

    @pl.when(step == 0)
    def _():
        weight_acc[...] = jnp.zeros_like(weight_acc)
        bias_ref[...] = sums_ref[...]

    ones = jnp.ones((8, seq), bf16)
    for t in range(n_shards):
        weight_acc[t] += mm(grad_ref[t, 0], x_ref[...])
        bias_ref[t, head : head + 1] += mm_nt(ones, grad_ref[t, 0])[:1]

    @pl.when(step == pl.num_programs(0) - 1)
    def _():
        slots = 1 << len(cut)
        half = slots // 2
        rows = PART_ROWS // slots
        for slot in range(slots):
            at = piece_number(pos_ref[0], slot, cut)
            ref = keep_ref if slot < half else send_ref
            for t in range(n_shards):
                ref[t, slot % half, :rows] = weight_acc[t, aligned(at, rows, 8), :].astype(bf16)
                if extra:
                    padded = jnp.concatenate(
                        [bias_ref[t], jnp.zeros((EXTRA, ref.shape[3] - PART_ROWS), f32)], axis=1
                    )
                    ref[t, slot % half, rows:] = padded.astype(bf16)


def attn_bwd(pos, x, packed, probs, ctx_low, mixed, sums, head, first, group, cut, extra, unroll, earlier):
    rows, width = x.shape
    n_shards, n_seq = packed.shape[:2]
    slots = 1 << len(cut)
    each = PART_ROWS // slots + (EXTRA if extra else 0)
    pieces = (n_shards, slots // 2, group * each, width)
    piece = pl.BlockSpec((n_shards, slots // 2, each, width), lambda s, pos: (0, 0, head - first, 0))
    sum_spec = pl.BlockSpec(sums.shape, lambda s, pos: (0, 0, 0))
    return pl.pallas_call(
        partial(attn_bwd_kernel, head=head, cut=cut, extra=extra, unroll=unroll),
        grid_spec=pltpu.PrefetchScalarGridSpec(
            num_scalar_prefetch=1,
            grid=(n_seq,),
            in_specs=[
                pl.BlockSpec((SEQ_LEN, width), lambda s, pos: (s, 0)),
                pl.BlockSpec((n_shards, 1, PART_ROWS, SEQ_LEN), lambda s, pos: (0, s, head, 0)),
                pl.BlockSpec((n_shards, 1, 1, SEQ_LEN, SEQ_LEN), lambda s, pos: (0, s, head, 0, 0)),
                pl.BlockSpec((n_shards, 1, HEAD_DIM, SEQ_LEN), lambda s, pos: (0, s, head, 0)),
                pl.BlockSpec((n_shards, 1, HEAD_DIM, SEQ_LEN), lambda s, pos: (0, s, head, 0)),
                sum_spec,
            ]
            + [pl.BlockSpec(memory_space=pl.ANY)] * len(earlier),
            out_specs=[
                pl.BlockSpec((n_shards, 1, PART_ROWS, SEQ_LEN), lambda s, pos: (0, s, 0, 0)),
                piece,
                piece,
                sum_spec,
            ],
            scratch_shapes=[
                pltpu.VMEM((n_shards, SEQ_LEN, HEAD_DIM), bf16),
                pltpu.VMEM((n_shards, PART_ROWS, width), f32),
            ],
        ),
        out_shape=[
            jax.ShapeDtypeStruct((n_shards, n_seq, PART_ROWS, SEQ_LEN), bf16),
            jax.ShapeDtypeStruct(pieces, bf16),
            jax.ShapeDtypeStruct(pieces, bf16),
            jax.ShapeDtypeStruct(sums.shape, f32),
        ],
        input_output_aliases={7: 1, 8: 2} if earlier else {},
        compiler_params=kernel_params(51_000_000),
        cost_estimate=cost(8 << 30, 10 << 20),
        name="attn_bwd",
    )(pos, x, packed, probs, ctx_low, mixed, sums, *earlier)


def input_grad_kernel(pos_ref, grad_one_ref, own_ref, *refs, n_others):
    fetched, grads, out_ref, got_ref = refs[: 2 * n_others], refs[2 * n_others : -2], refs[-2], refs[-1]
    half = own_ref.shape[0] // 2

    @pl.when(pl.program_id(0) == 0)
    def _():
        parity = lax.rem(pos_ref[0], 2)
        for t in range(n_others):
            for k in range(2):
                side = parity if k == 0 else 1 - parity
                got_ref[t, aligned(side, half, half), :] = fetched[2 * t + k][:half]

    total = grad_one_ref[...]
    for t in range(n_others + 1):
        weight = own_ref if t == 0 else got_ref.at[t - 1]
        total = total + mm_tn(jnp.concatenate([ref[t, 0] for ref in grads], axis=0), weight[...])
    out_ref[...] = total.astype(bf16)


def input_gradient(pos, grad_one, own, fetched, packed_grads):
    rows, width = grad_one.shape
    n_shards = packed_grads[0].shape[0]
    block = 512
    per_seq = SEQ_LEN // block
    row = pl.BlockSpec((block, width), lambda i, pos: (i, 0))
    cols = pl.BlockSpec((n_shards, 1, PART_ROWS, block), lambda i, pos: (0, i // per_seq, 0, i % per_seq))

    def whole(array):
        return pl.BlockSpec(array.shape, lambda i, pos: (0, 0), pipeline_mode=pl.Buffered(1))

    return pl.pallas_call(
        partial(input_grad_kernel, n_others=n_shards - 1),
        grid_spec=pltpu.PrefetchScalarGridSpec(
            num_scalar_prefetch=1,
            grid=(rows // block,),
            in_specs=[row, whole(own)] + [whole(v) for v in fetched] + [cols] * len(packed_grads),
            out_specs=row,
            scratch_shapes=[pltpu.VMEM((n_shards - 1,) + own.shape, bf16)],
        ),
        out_shape=jax.ShapeDtypeStruct((rows, width), bf16),
        compiler_params=kernel_params(51_000_000),
        cost_estimate=cost(4 << 30, 12 << 20),
        name="input_gradient",
    )(pos, grad_one, own, *fetched, *packed_grads)


def mlp_place_kernel(pos_ref, dn_near, dn_far, up_near, up_far, proj_out, up_out, dn_out):
    low = lax.rem(pos_ref[0], MLP_SLOTS)
    half = MLP_SLOTS // 2
    width = proj_out.shape[1]
    hidden = dn_out.shape[0]
    dn_rows, up_rows, proj_rows = hidden // MLP_SLOTS, width // MLP_SLOTS, proj_out.shape[0] // MLP_SLOTS
    for slot in range(MLP_SLOTS):
        dn_ref = dn_near if slot < half else dn_far
        up_ref = up_near if slot < half else up_far
        k = slot % half
        at = lax.bitwise_xor(low, DOWN_BITS[slot])
        dn_out[aligned(at, dn_rows, dn_rows), :] = dn_ref[k, :dn_rows].astype(f32)
        proj_out[aligned(at, proj_rows, proj_rows), :] = dn_ref[k, dn_rows:].astype(f32)
        rows = aligned(lax.bitwise_xor(low, UP_BITS[slot]), up_rows, up_rows)
        for j in range(hidden // width):
            up_out[rows, j * width : (j + 1) * width] = up_ref[k, j * up_rows : (j + 1) * up_rows].astype(f32)


def mlp_place(pos, dn_parts, up_parts, ctx_rows, width, hidden):
    return pl.pallas_call(
        mlp_place_kernel,
        in_specs=[pl.BlockSpec(memory_space=pltpu.SMEM)] + [in_vmem()] * 4,
        out_specs=[in_vmem()] * 3,
        out_shape=[
            jax.ShapeDtypeStruct((ctx_rows, width), f32),
            jax.ShapeDtypeStruct((width, hidden), f32),
            jax.ShapeDtypeStruct((hidden, width), f32),
        ],
        compiler_params=kernel_params(51_000_000),
        cost_estimate=cost(0, 14 << 20),
        name="mlp_place",
    )(pos, *dn_parts, *up_parts)


def qkv_place_kernel(pos_ref, *refs, groups):
    bias_ref, out_ref, query_ref, value_ref = refs[-4:]
    for g, (first, group, cut, each) in enumerate(groups):
        slots = 1 << len(cut)
        half = slots // 2
        rows = PART_ROWS // slots
        for slot in range(slots):
            at = aligned(piece_number(pos_ref[0], slot, cut), rows, 8)
            for k in range(group):
                value = refs[2 * g + slot // half][slot % half, k * each : k * each + rows]
                out_ref[first + k, at, :] = value.astype(f32)
    heads = out_ref.shape[0]
    for k, ref in ((0, query_ref), (2, value_ref)):
        parts = [bias_ref[h : h + 1, k * HEAD_DIM : (k + 1) * HEAD_DIM] for h in range(heads)]
        ref[...] = jnp.concatenate(parts, axis=1).reshape(heads * HEAD_DIM)


def qkv_place(pos, parts, bias, groups, heads):
    flat = [half for pair in parts for half in pair]
    vector = jax.ShapeDtypeStruct((heads * HEAD_DIM,), f32)
    return pl.pallas_call(
        partial(qkv_place_kernel, groups=groups),
        in_specs=[pl.BlockSpec(memory_space=pltpu.SMEM)] + [in_vmem()] * (len(flat) + 1),
        out_specs=[in_vmem()] * 3,
        out_shape=[jax.ShapeDtypeStruct((heads, PART_ROWS, flat[0].shape[2]), f32), vector, vector],
        compiler_params=kernel_params(51_000_000),
        cost_estimate=cost(0, 3 << 20),
        name="qkv_place",
    )(pos, *flat, bias)


def swap_dp(value, bits, n_dp):
    return lax.ppermute(value, "dp", [(i, i ^ bits) for i in range(n_dp)])


def shift_tensor(value, by, n_tensor):
    return lax.ppermute(value, "tensor", [((i + by) % n_tensor, i) for i in range(n_tensor)])


def reduce_pieces(keep, send, order, n_dp, n_tensor):
    halved = [axis for axis in order if axis != "tensor"]
    got = swap_dp(send, 1, n_dp)
    got = after(got, (yield send))
    parts = [keep[t].astype(f32) + got[t].astype(f32) for t in range(n_tensor)]
    for axis in order:
        if axis == "tensor":
            outs = [parts[by].astype(bf16) for by in range(1, n_tensor)]
            gots = [shift_tensor(out, -by, n_tensor) for by, out in enumerate(outs, 1)]
            gots = after(gots, (yield outs))
            parts = [sum((got.astype(f32) for got in gots), parts[0])]
        else:
            cut = parts[0].shape[0] // 2
            out = jnp.stack([part[cut:].astype(bf16) for part in parts])
            got = swap_dp(out, axis, n_dp)
            got = after(got, (yield out))
            parts = [part[:cut] + got[t].astype(f32) for t, part in enumerate(parts)]
    own = parts[0]
    bits = 2
    while bits < n_dp:
        if bits not in halved:
            out = own.astype(bf16)
            got = swap_dp(out, bits, n_dp)
            got = after(got, (yield out))
            own = own + got.astype(f32)
        bits *= 2
    near = own.astype(bf16)
    for axis in reversed(halved):
        got = swap_dp(near, axis, n_dp)
        got = after(got, (yield near))
        near = jnp.concatenate([near, got], axis=0)
    got = swap_dp(near, 1, n_dp)
    got = after(got, (yield near))
    return near, got, own


class Sums:
    def __init__(self):
        self.live, self.done, self.fresh = {}, {}, set()

    def add(self, name, generator):
        self.live[name] = generator
        self.fresh.add(name)

    def step(self, ready, *names):
        sent = []
        for name in names:
            if name in self.live:
                try:
                    sent.append(self.live[name].send(None if name in self.fresh else ready))
                    self.fresh.discard(name)
                except StopIteration as stop:
                    self.done[name] = stop.value
                    del self.live[name]
        return sent

    def finish(self):
        while self.live:
            self.step((), *list(self.live))


def after(value, *others):
    return lax.optimization_barrier((value, others))[0]


def sequence_body(n_dp, n_tensor, *arrays):
    (
        layer_input,
        output_grad,
        qkv_weight,
        query_bias,
        value_bias,
        proj_weight,
        proj_bias,
        first_gain,
        first_shift,
        up_weight,
        up_bias,
        down_weight,
        down_bias,
        second_gain,
        second_shift,
    ) = arrays
    rows, width = layer_input.shape
    n_seq = rows // SEQ_LEN
    ctx_rows, hidden = proj_weight.shape[0], up_weight.shape[1]
    n_heads = ctx_rows // HEAD_DIM
    pos = lax.axis_index("dp").astype(jnp.int32).reshape(1)
    shifts = range(1, n_tensor)

    vectors = [proj_bias, first_gain, first_shift, down_bias, second_gain, second_shift]
    qkv_half, own_bias, mlp_half, vecs = pack(
        pos, qkv_weight, query_bias, value_bias, proj_weight, down_weight, up_weight, up_bias, vectors
    )
    qkv_near = [shift_tensor(qkv_half, by, n_tensor) for by in shifts]
    shapes = [
        jax.ShapeDtypeStruct((n_tensor, n_seq, n_heads * PART_ROWS, SEQ_LEN), bf16),
        jax.ShapeDtypeStruct((n_tensor, n_seq, n_heads, SEQ_LEN, SEQ_LEN), bf16),
        jax.ShapeDtypeStruct((n_tensor, n_seq, n_heads * HEAD_DIM, SEQ_LEN), bf16),
        jax.ShapeDtypeStruct((n_tensor, n_seq, n_heads * HEAD_DIM, SEQ_LEN), f32),
    ]
    mlp_near = [shift_tensor(mlp_half, by, n_tensor) for by in shifts]
    x = after(layer_input, mlp_half)
    stacks = attn_fwd(pos, x, (qkv_weight, own_bias), 0, False, shapes, ())
    qkv_near = after(qkv_near, stacks[2])
    qkv_far = [swap_dp(near, 1, n_dp) for near in qkv_near]
    for t in shifts:
        stacks = attn_fwd(pos, layer_input, (qkv_near[t - 1], qkv_far[t - 1]), t, True, shapes, stacks)
    packed, probs, ctx, mixed = stacks
    mlp_near = after(mlp_near, ctx)
    mlp_far = [swap_dp(near, 1, n_dp) for near in mlp_near]
    fetched = [half for pair in zip(mlp_near, mlp_far) for half in pair]
    result, grad_one, ctx_low, dn_keep, dn_send, up_keep, up_send = middle(
        pos, layer_input, output_grad, ctx, vecs, proj_weight, up_weight, down_weight, fetched
    )
    sums = Sums()
    sums.add("dn", reduce_pieces(dn_keep, dn_send, DOWN_ORDER, n_dp, n_tensor))
    sums.add("up", reduce_pieces(up_keep, up_send, UP_ORDER, n_dp, n_tensor))
    bias_sums = jnp.zeros((n_tensor, EXTRA, PART_ROWS), f32)
    packed_grads = []
    ready = ()
    early = n_heads - 1
    stacked = ()
    early_cut, early_order = (1, 2), ("tensor", 2)
    for head in range(n_heads):
        last = head == early
        if last and early:
            sums.add("qa", reduce_pieces(*stacked, early_order, n_dp, n_tensor))
        sent = sums.step(ready, *SCHEDULE[min(head, len(SCHEDULE) - 3)])
        x = after(layer_input, sent)
        grads, keep, send, bias_sums = attn_bwd(
            pos,
            x,
            packed,
            probs,
            ctx_low,
            mixed,
            bias_sums,
            head,
            early if last else 0,
            1 if last else early,
            (1,) if last else early_cut,
            last,
            head in UNROLLED,
            () if last else stacked,
        )
        ready = bias_sums
        packed_grads.append(grads)
        if not last:
            stacked = (keep, send)
    sums.add("qb", reduce_pieces(keep, send, ("tensor",), n_dp, n_tensor))
    sent = sums.step(ready, *SCHEDULE[-2])
    qkv_fetched = [half for pair in zip(qkv_near, qkv_far) for half in pair]
    input_grad = input_gradient(pos, after(grad_one, sent), qkv_weight, qkv_fetched, packed_grads)
    ready = input_grad
    for name in SCHEDULE[-1]:
        sent = sums.step(ready, name)
        ready = sent or ready
    sums.finish()
    dn_near, dn_far, _ = sums.done["dn"]
    up_near, up_far, up_own = sums.done["up"]
    proj_wg, up_wg, dn_wg = mlp_place(pos, (dn_near, dn_far), (up_near, up_far), ctx_rows, width, hidden)
    groups = [(0, early, early_cut, PART_ROWS // 4)] if early else []
    groups.append((early, 1, (1,), PART_ROWS // 2 + EXTRA))
    parts = [sums.done[name][:2] for name in ("qa", "qb") if name in sums.done]
    bias = sums.done["qb"][2][0, -EXTRA:]
    qkv_wg, query_bg, value_bg = qkv_place(pos, parts, bias, groups, n_heads)
    small = up_own[0, -EXTRA:]
    return (
        result,
        input_grad,
        qkv_wg.reshape(n_heads * PART_ROWS, width),
        query_bg,
        value_bg,
        proj_wg,
        small[0],
        small[1],
        small[2],
        up_wg,
        small[8 : 8 + hidden // width].reshape(hidden),
        dn_wg,
        small[3],
        small[4],
        small[5],
    )


SCHEDULE = (
    ("dn", "up"),
    ("dn", "up"),
    ("dn", "up"),
    ("qa", "dn", "up", "qa"),
    ("qb", "qa", "dn", "up", "qb"),
    ("qb", "qa", "dn", "up", "qb", "qa", "up", "dn", "qb", "qa", "up", "dn", "qb", "qa"),
)
UNROLLED = (0, 1)


def solution(mesh):
    n_dp, n_tensor = mesh.shape["dp"], mesh.shape["tensor"]

    def body(*arrays):
        rows = arrays[0].shape[0]
        if rows % SEQ_LEN == 0 and n_dp % 8 == 0 and n_dp & (n_dp - 1) == 0:
            return sequence_body(n_dp, n_tensor, *arrays)
        return token_body(*arrays)

    return jax.shard_map(
        body,
        mesh=mesh,
        in_specs=(
            P(("dp", "tensor"), None),
            P(("dp", "tensor"), None),
            P("tensor", None),
            P("tensor"),
            P("tensor"),
            P("tensor", None),
            P(),
            P(),
            P(),
            P(None, "tensor"),
            P("tensor"),
            P("tensor", None),
            P(),
            P(),
            P(),
        ),
        out_specs=(
            P(("dp", "tensor"), None),
            P(("dp", "tensor"), None),
            P("tensor", None),
            P("tensor"),
            P("tensor"),
            P("tensor", None),
            P(),
            P(),
            P(),
            P(None, "tensor"),
            P("tensor"),
            P("tensor", None),
            P(),
            P(),
            P(),
        ),
        check_vma=False,
    )
```
